256 devices in a mesh: row: 16 (over y, z_hi, core), col: 16 (over x, z_lo).
Axes of the slice: x: 4, y: 4, z: 8 (z_hi: 2, z_lo: 4; z = z_hi * 4 + z_lo), core: 2. Of those that a mesh axis runs over, the one named last changes fastest.
Arguments:
- values: bfloat16 [65536, 128], P('row'), may hold values from -30 to 30
- points0: bfloat16 [2, 65536], P(None, 'row'), may hold values from 0 to 1
- points1: bfloat16 [2, 16384], P(None, 'row'), may hold values from 0 to 1
- points2: bfloat16 [2, 2048], P(None, 'row'), may hold values from 0 to 1
- tiles_a0: int32 [16, 16, 2, 384], P('row', 'col'), may hold values from 0 to 31, as said below
- tiles_e1: int32 [16, 16, 2, 160], P('row', 'col'), may hold values from 0 to 31, as said below
- tiles_a1: int32 [16, 16, 2, 32], P('row', 'col'), may hold values from 0 to 7, as said below
- factor: bfloat16 [2048, 2048], P('row', 'col'), as said below
Outputs:
- fine_coef: float32 [65536, 128], P(('row', 'col'))
- mid_coef: float32 [16384, 128], P('col')
- coarse_coef: float32 [2048, 128], P('row')
- norms: float32 [1], replicated
The draws below stay inside these ranges and needn't reach their ends.
Inputs may be any that keep to these rules, and one draw needn't show every extreme that they name: `tiles_a0`: within each block the 384 listed tile pairs are distinct; tile rows are below 32 and tile columns below 32. `tiles_e1`: within each block the 160 listed tile pairs are distinct; tile rows are below 32 and tile columns below 8. `tiles_a1`: within each block the 32 listed tile pairs are distinct; tile rows are below 8 and tile columns below 8. `factor`: upper triangular; diagonal entries from 1 to 2.
All inputs are finite; a program needn't handle non-finite values.
Results may differ from the reference program's by a relative error of at most 0.0042.
Values may be sent and summed in bfloat16 or wider, within the bound.
No kernel may reach another device: no remote copies, remote signals or barrier semaphores. Data moves between devices by JAX's collectives and lax.ppermute only.
A program may use at most 64 MiB of HBM per device.

```python
import jax
import jax.numpy as jnp
from jax import lax

TILE = 128
FIELDS = 128
N0 = 65536
N1 = 16384
N2 = 2048
ROWS0 = 4096
COLS0 = 4096
ROWS1 = 1024
COLS1 = 1024
ROWS2 = 128
MAXT_A0 = 384
MAXT_E1 = 160
MAXT_A1 = 32
N_ROW = 16
N_COL = 16


def pick_tiles(key, stream, row_range, col_range, listed):
    subkeys = jax.random.split(jax.random.fold_in(key, stream), N_ROW * N_COL)

    def choose_one(subkey):
        return jax.random.permutation(subkey, row_range * col_range)[:listed]
    chosen = jax.vmap(choose_one)(subkeys).astype(jnp.int32)
    chosen = chosen.reshape(N_ROW, N_COL, 1, listed)
    return jnp.concatenate([chosen // col_range, chosen % col_range], axis=2)


def draw_values(key, part):
    base = jax.random.fold_in(key, 505)
    entry_key, row_key = jax.random.split(base)
    position = jnp.arange(N0, dtype=jnp.float32) / N0
    jitter = jnp.exp(jax.random.uniform(row_key, (N0,), jnp.float32, -0.22, 0.22))
    entries = jnp.clip(jax.random.normal(entry_key, (N0, FIELDS), jnp.float32), -6.0, 6.0)
    scale = jnp.exp(position * jnp.log(3.5)) * jitter
    return (entries * scale[:, None]).astype(jnp.bfloat16)


def draw_tiles_a0(key, part):
    return pick_tiles(key, 101, ROWS0 // TILE, COLS0 // TILE, MAXT_A0)


def draw_tiles_e1(key, part):
    return pick_tiles(key, 202, ROWS0 // TILE, COLS1 // TILE, MAXT_E1)


def draw_tiles_a1(key, part):
    return pick_tiles(key, 303, ROWS1 // TILE, COLS1 // TILE, MAXT_A1)


def draw_factor(key, part):
    base = jax.random.fold_in(key, 404)
    diag_key, upper_key = jax.random.split(base)
    index = jnp.arange(N2)
    upper = index[None, :] > index[:, None]
    spread = jax.random.normal(upper_key, (N2, N2), jnp.float32)
    diagonal = jax.random.uniform(diag_key, (N2,), jnp.float32, 1.0, 2.0)
    matrix = jnp.where(upper, spread * (0.6 / N2 ** 0.5), 0.0) + jnp.diag(diagonal)
    return matrix.astype(jnp.bfloat16)


def shard_levels(stream_key, extent, pieces, smallest, top_value):
    factor_of, own = 1.0, jax.random.fold_in(stream_key, 6)
    for dim, shards_of in pieces:
        steps = jnp.exp(jax.random.uniform(jax.random.fold_in(own, dim), (shards_of,), jnp.float32, smallest / len(pieces), top_value / len(pieces)))
        factor_of = factor_of * jnp.repeat(steps, extent[dim] // shards_of).reshape([-1 if axis == dim else 1 for axis in range(len(extent))])
    return factor_of


def setup_inputs(seed: int = 0) -> dict:
    key_of = jax.random.split(jax.random.key(seed), 9)
    return {
        "values": draw_values(jax.random.fold_in(key_of[8], 71), 0),
        "points0": jnp.clip(1.0 * jax.random.uniform(key_of[1], (2, N0), jnp.float32) ** shard_levels(key_of[1], (2, N0), ((1, 16),), -0.2, 0.2), 0.0, 1.0).astype(jnp.bfloat16),
        "points1": jnp.clip(1.0 * jax.random.uniform(key_of[2], (2, N1), jnp.float32) ** shard_levels(key_of[2], (2, N1), ((1, 16),), -0.2, 0.2), 0.0, 1.0).astype(jnp.bfloat16),
        "points2": jnp.clip(1.0 * jax.random.uniform(key_of[3], (2, N2), jnp.float32) ** shard_levels(key_of[3], (2, N2), ((1, 16),), -0.2, 0.2), 0.0, 1.0).astype(jnp.bfloat16),
        "tiles_a0": draw_tiles_a0(jax.random.fold_in(key_of[8], 71), 0),
        "tiles_e1": draw_tiles_e1(jax.random.fold_in(key_of[8], 71), 0),
        "tiles_a1": draw_tiles_a1(jax.random.fold_in(key_of[8], 71), 0),
        "factor": draw_factor(jax.random.fold_in(key_of[8], 71), 0),
    }


support_fine = 0.35
support_mid = 0.55
support_coarse = 0.8

def wendland(left_pts, right_pts, support):
    left = left_pts.astype(jnp.float32)
    right = right_pts.astype(jnp.float32)
    across = left[0][..., :, None] - right[0][..., None, :]
    upward = left[1][..., :, None] - right[1][..., None, :]
    ratio_t = jnp.sqrt(across * across + upward * upward) / support
    margin = jnp.maximum(1.0 - ratio_t, 0.0)
    squared = margin * margin
    return (squared * squared * (4.0 * ratio_t + 1.0)).astype(jnp.bfloat16)

def listed_all(row_pts, col_pts, listing, vector, support, flipped):
    row_tiles = row_pts.reshape(2, -1, TILE)
    col_tiles = col_pts.reshape(2, -1, TILE)
    rows_block = row_tiles.shape[1] // N_ROW
    cols_block = col_tiles.shape[1] // N_COL
    row_start = (jnp.arange(N_ROW, dtype=jnp.int32) * rows_block)[:, None, None]
    col_start = (jnp.arange(N_COL, dtype=jnp.int32) * cols_block)[None, :, None]
    global_rows = (listing[:, :, 0, :].astype(jnp.int32) + row_start).reshape(N_ROW * N_COL, -1)
    global_cols = (listing[:, :, 1, :].astype(jnp.int32) + col_start).reshape(N_ROW * N_COL, -1)
    fields = vector.shape[-1]
    inputs = vector.astype(jnp.float32).reshape(-1, TILE, fields)
    target = col_tiles.shape[1] if flipped else row_tiles.shape[1]
    total = jnp.zeros((target, TILE, fields), jnp.float32)

    def add_block(total, pair):
        tile_rows, tile_cols = pair
        kernel = wendland(row_tiles[:, tile_rows], col_tiles[:, tile_cols], support).astype(jnp.float32)
        if flipped:
            contrib = jnp.einsum('gij,gir->gjr', kernel, inputs[tile_rows])
            return (total.at[tile_cols].add(contrib), None)
        contrib = jnp.einsum('gij,gjr->gir', kernel, inputs[tile_cols])
        return (total.at[tile_rows].add(contrib), None)
    total, unused = lax.scan(add_block, total, (global_rows, global_cols))
    return total.reshape(-1, fields)

def reference(values, points0, points1, points2, tiles_a0, tiles_e1, tiles_a1, factor):
    scale_a0 = (ROWS0 / (N_COL * MAXT_A0 * TILE * TILE)) ** 0.5
    scale_e1 = (ROWS0 / (N_COL * MAXT_E1 * TILE * TILE)) ** 0.5
    scale_a1 = (ROWS1 / (N_COL * MAXT_A1 * TILE * TILE)) ** 0.5
    scale_e2 = (1.0 / N1) ** 0.5
    fine_data = values.astype(jnp.float32)
    fine_res = fine_data - 0.5 * (scale_a0 * listed_all(points0, points0, tiles_a0, values, support_fine, False))
    mid_data = scale_e1 * listed_all(points0, points1, tiles_e1, fine_res.astype(jnp.bfloat16), support_mid, True)
    mid_prod = (scale_a1 * listed_all(points1, points1, tiles_a1, mid_data.astype(jnp.bfloat16), support_mid, False)).astype(jnp.bfloat16)
    mid_res = mid_data - 0.5 * mid_prod.astype(jnp.float32)
    mid_low = mid_res.astype(jnp.bfloat16)
    coarse_blocks = points2.reshape(2, N_ROW, ROWS2).transpose(1, 0, 2)

    def restrict_block(block_pts):
        kernel = wendland(block_pts, points1, support_coarse)
        return jnp.dot(kernel, mid_low, preferred_element_type=jnp.float32)
    coarse_raw = lax.map(restrict_block, coarse_blocks).reshape(N2, -1)
    coarse_data = (scale_e2 * coarse_raw).astype(jnp.bfloat16)
    halfway = jnp.dot(factor.T, coarse_data, preferred_element_type=jnp.float32).astype(jnp.bfloat16)
    coarse_coef = jnp.dot(factor, halfway, preferred_element_type=jnp.float32)
    coarse_low = coarse_coef.astype(jnp.bfloat16).reshape(N_ROW, ROWS2, -1)

    def prolong_block(total, pair):
        block_pts, block_coef = pair
        kernel = wendland(block_pts, points1, support_coarse)
        return (total + jnp.dot(kernel.T, block_coef, preferred_element_type=jnp.float32), None)
    mid_corr, unused = lax.scan(prolong_block, jnp.zeros((N1, FIELDS), jnp.float32), (coarse_blocks, coarse_low))
    mid_coef = 0.5 * mid_data + scale_e2 * mid_corr
    fine_coef = 0.5 * fine_data + scale_e1 * listed_all(points0, points1, tiles_e1, mid_coef.astype(jnp.bfloat16), support_mid, False)
    norms = jnp.stack([jnp.mean(fine_res * fine_res)])
    return (fine_coef, mid_coef, coarse_coef, norms)
```

```python
import jax
import jax.numpy as jnp
from jax import lax
from jax.experimental import pallas as pl
from jax.experimental.pallas import tpu as pltpu
from jax.sharding import Mesh
from jax.sharding import PartitionSpec as P

TILE = 128
SIDE = 16
BLOCK = 8
FEATURES = 16

support_fine = 0.35
support_mid = 0.55
support_coarse = 0.8

ROW = ("y", "zh", "k")
YZ = ("y", "zh")
COL = ("x", "zl")
ALL = ROW + COL

bf16 = jnp.bfloat16
f32 = jnp.float32

VMEM = pl.BlockSpec(memory_space=pltpu.VMEM)
SMEM = pl.BlockSpec(memory_space=pltpu.SMEM)
PARAMS = pltpu.CompilerParams(vmem_limit_bytes=56 * 1024 * 1024)


def turned(x):
    pairs = [(c * SIDE + r, r * SIDE + c) for r in range(SIDE) for c in range(SIDE)]
    return lax.ppermute(x, ALL, pairs)


def place_of_block(block, core):
    return ((block % 2) ^ core) * (SIDE // 2) + block // 2


def turned_blocks(x):
    pairs = [
        (c * SIDE + place_of_block(r, c % 2), r * SIDE + c) for r in range(SIDE) for c in range(SIDE)
    ]
    return lax.ppermute(x, ALL, pairs)


def from_partner(x):
    return lax.ppermute(x, "k", [(0, 1), (1, 0)])


def exchanged(x, axes):
    return lax.all_to_all(x, axes, split_axis=0, concat_axis=0, tiled=True)


def gathered(x, axes):
    return exchanged(jnp.broadcast_to(x, (lax.axis_size(axes), *x.shape)), axes)


def gathered_row(x):
    own = gathered(x, YZ)
    return own, from_partner(own)


def summed_row(own, other):
    pair = (own.astype(f32) + from_partner(other).astype(f32)).astype(bf16)
    return exchanged(pair, YZ).astype(f32).sum(axis=0)


def norm_parts(points):
    x = points.astype(f32)
    norm = x[0] * x[0] + x[1] * x[1]
    high = lax.reduce_precision(norm, 8, 7)
    rest = norm - high
    middle = lax.reduce_precision(rest, 8, 7)
    return [high, middle, rest - middle]


def row_features(points):
    one = jnp.ones(points.shape[1], f32)
    x = points.astype(f32)
    lines = [x[0], x[1], *norm_parts(points), one, one, one]
    lines += [jnp.zeros_like(one)] * (FEATURES - len(lines))
    return jnp.stack(lines).astype(bf16).T


def col_features(points):
    one = jnp.ones(points.shape[1], f32)
    x = points.astype(f32)
    lines = [-2.0 * x[0], -2.0 * x[1], one, one, one, *norm_parts(points)]
    lines += [jnp.zeros_like(one)] * (FEATURES - len(lines))
    return jnp.stack(lines).astype(bf16)


def wendland(left, right, support):
    square = jnp.maximum(jnp.dot(left, right, preferred_element_type=f32), 1e-30)
    margin = jnp.maximum(support - square * lax.rsqrt(square), 0.0)
    margin2 = margin * margin
    line = 5.0 / support**4 - (4.0 / support**5) * margin
    return (margin2 * margin2 * line).astype(bf16)


def at_tile(i):
    return pl.ds(pl.multiple_of(i * TILE, TILE), TILE)


def dot_turned(a, b):
    return lax.dot_general(a, b, (((1,), (1,)), ((), ())), preferred_element_type=f32)


def product_a0(listing, core, left, right, vector):
    listed = listing.shape[1]
    group = 8
    rows = left.shape[0] // TILE

    def kernel(list_ref, core_ref, left_ref, right_ref, vector_ref, own_ref, other_ref, total):
        total[...] = jnp.zeros_like(total)

        def step(g, carry):
            products = []
            for u in range(group):
                i, j = list_ref[0, g * group + u], list_ref[1, g * group + u]
                tile = wendland(left_ref[at_tile(i), :], right_ref[:, at_tile(j)], support_fine)
                products.append((i, dot_turned(vector_ref[:, at_tile(j)], tile)))
            for i, product in products:
                total[i] += product.reshape(SIDE, BLOCK, TILE)
            return carry

        lax.fori_loop(0, listed // group, step, 0)
        me = core_ref[0]
        for half in range(SIDE // 2):
            for i in range(rows):
                at = pl.ds(i * TILE, TILE)
                own_ref[half, :, at] = total[i, 2 * half + me].astype(bf16)
                other_ref[half, :, at] = total[i, 2 * half + 1 - me].astype(bf16)

    half = jax.ShapeDtypeStruct((SIDE // 2, BLOCK, left.shape[0]), bf16)
    return pl.pallas_call(
        kernel,
        out_shape=(half, half),
        in_specs=[SMEM, SMEM, VMEM, VMEM, VMEM],
        out_specs=(VMEM, VMEM),
        scratch_shapes=[pltpu.VMEM((rows, SIDE, BLOCK, TILE), f32)],
        compiler_params=PARAMS,
        name="product_a0",
    )(listing, core, left, right, vector)


def listed_tiles(listing, left, right, support):
    listed = listing.shape[1]
    group = 16

    def kernel(list_ref, left_ref, right_ref, out_ref):
        g = pl.program_id(0)
        for u in range(group):
            i, j = list_ref[0, g * group + u], list_ref[1, g * group + u]
            out_ref[u] = wendland(left_ref[at_tile(i), :], right_ref[:, at_tile(j)], support)

    return pl.pallas_call(
        kernel,
        out_shape=jax.ShapeDtypeStruct((listed, TILE, TILE), bf16),
        grid=(listed // group,),
        in_specs=[SMEM, VMEM, VMEM],
        out_specs=pl.BlockSpec((group, TILE, TILE), lambda g: (g, 0, 0)),
        compiler_params=PARAMS,
        name="listed_tiles",
    )(listing, left, right)


def all_pairs(left, right, support):
    def kernel(left_ref, right_ref, out_ref):
        for j in range(right.shape[1] // TILE):
            at = pl.ds(j * TILE, TILE)
            out_ref[:, at] = wendland(left_ref[...], right_ref[:, at], support)

    return pl.pallas_call(
        kernel,
        out_shape=jax.ShapeDtypeStruct((left.shape[0], right.shape[1]), bf16),
        grid=(left.shape[0] // TILE,),
        in_specs=[pl.BlockSpec((TILE, FEATURES), lambda i: (i, 0)), VMEM],
        out_specs=pl.BlockSpec((TILE, right.shape[1]), lambda i: (i, 0)),
        compiler_params=PARAMS,
        name="all_pairs",
    )(left, right)


def product_of_tiles(listing, tiles, halves, outs, flipped, shares):
    listed = listing.shape[1]
    group = 16
    steps = listed // group

    def kernel(list_ref, tile_ref, own_ref, other_ref, out_ref, vector, total):
        g = pl.program_id(0)

        @pl.when(g == 0)
        def _():
            total[...] = jnp.zeros_like(total)
            fields = SIDE * BLOCK // 2
            for ref, first in ((own_ref, 0), (other_ref, fields)):
                vector[pl.ds(first, fields), :] = ref[...].reshape(fields, ref.shape[2])

        products = []
        for u in range(group):
            i, j = list_ref[0, g * group + u], list_ref[1, g * group + u]
            if flipped:
                part = jnp.dot(vector[:, at_tile(i)], tile_ref[u], preferred_element_type=f32)
                products.append((j, part))
            else:
                products.append((i, dot_turned(vector[:, at_tile(j)], tile_ref[u])))
        for at, product in products:
            total[at] += product

        @pl.when(g == steps - 1)
        def _():
            for i in range(outs // TILE):
                if shares:
                    each = outs // SIDE // TILE
                    at = pl.ds(i % each * TILE, TILE)
                    out_ref[i // each, :, at] = total[i].astype(bf16)
                else:
                    out_ref[:, :, pl.ds(i * TILE, TILE)] = (
                        total[i].astype(bf16).reshape(SIDE, BLOCK, TILE)
                    )

    fields = SIDE * BLOCK
    shape = (SIDE, fields, outs // SIDE) if shares else (SIDE, BLOCK, outs)
    return pl.pallas_call(
        kernel,
        out_shape=jax.ShapeDtypeStruct(shape, bf16),
        grid=(steps,),
        in_specs=[SMEM, pl.BlockSpec((group, TILE, TILE), lambda g: (g, 0, 0)), VMEM, VMEM],
        out_specs=VMEM,
        scratch_shapes=[
            pltpu.VMEM((fields, halves[0].shape[2]), bf16),
            pltpu.VMEM((outs // TILE, fields, TILE), f32),
        ],
        compiler_params=PARAMS,
        name="product_of_tiles",
    )(listing, tiles, *halves)


def in_field_order(x, core):
    n = x.shape[-1]
    x = jnp.where(core == 0, x, x[::-1])
    return x.transpose(3, 1, 0, 2).reshape(n, SIDE * BLOCK)


def per_device(values, points0, points1, points2, tiles_a0, tiles_e1, tiles_a1, factor):
    core = lax.axis_index("k")
    col_id = lax.axis_index(COL)
    rows_fine, fields = values.shape
    rows_mid = points1.shape[1]
    coarse = points2.shape[1] * SIDE
    share = rows_fine // SIDE
    half = SIDE // 2
    list_a0, list_e1, list_a1 = tiles_a0[0, 0], tiles_e1[0, 0], tiles_a1[0, 0]
    ends = (list_a0.shape[1], list_a0.shape[1] + list_e1.shape[1])
    scale_a0 = (rows_fine / (SIDE * list_a0.shape[1] * TILE * TILE)) ** 0.5
    scale_e1 = (rows_fine / (SIDE * list_e1.shape[1] * TILE * TILE)) ** 0.5
    scale_a1 = (rows_mid / (SIDE * list_a1.shape[1] * TILE * TILE)) ** 0.5
    scale_e2 = (1.0 / (rows_mid * SIDE)) ** 0.5

    lists = turned(jnp.concatenate([list_a0, list_e1, list_a1], axis=1))
    turned_a0, turned_e1, turned_a1 = jnp.split(lists, ends, axis=1)
    points = turned(jnp.concatenate([points0, points1], axis=1))
    fine_there, mid_there = points[:, :rows_fine], points[:, rows_fine:]
    vector = values.T
    data_share = turned(
        lax.dynamic_index_in_dim(vector.reshape(SIDE, BLOCK, rows_fine), col_id, 0, keepdims=False)
    )
    left_fine = row_features(fine_there)

    own, other = product_a0(
        turned_a0, core.astype(jnp.int32).reshape(1), left_fine, col_features(points0), vector
    )

    right_there = col_features(mid_there)
    right_here = col_features(points1)
    tiles_back = listed_tiles(turned_e1, left_fine, right_here, support_mid)
    tiles_mid = listed_tiles(turned_a1, row_features(mid_there), right_here, support_mid)
    tiles_out = listed_tiles(list_e1, row_features(points0), right_there, support_mid)
    points2_all = exchanged(jnp.broadcast_to(points2, (SIDE, *points2.shape)), ROW)
    points2_all = points2_all.transpose(1, 0, 2).reshape(2, coarse)
    coarse_kernel = all_pairs(row_features(points2_all), right_there, support_coarse)
    factors = exchanged(
        jnp.broadcast_to(jnp.stack([factor, turned(factor)]), (SIDE, 2, *factor.shape)), ROW
    )
    factor_down = factors[:, 0].reshape(coarse, -1)
    factor_across = factors[:, 1]

    residual = data_share.astype(f32) - (0.5 * scale_a0) * summed_row(own, other)
    squares = jnp.sum(residual * residual, axis=0).reshape(-1, TILE).sum(axis=0)
    residual_halves = gathered_row(residual.astype(bf16))

    restricted = product_of_tiles(turned_e1, tiles_back, residual_halves, rows_mid, True, False)
    mid_share = scale_e1 * exchanged(restricted, COL).astype(f32).sum(axis=0)
    mid_all = gathered(mid_share.astype(bf16), COL)
    mid_data = turned_blocks(mid_share)

    mid_part = product_of_tiles(
        turned_a1, tiles_mid, (mid_all[:half], mid_all[half:]), rows_mid, False, False
    )
    mid_prod = scale_a1 * summed_row(mid_part[:half], mid_part[half:])
    mid_residual = mid_data - 0.5 * mid_prod.astype(bf16).astype(f32)

    coarse_part = dot_turned(mid_residual.astype(bf16), coarse_kernel)
    coarse_part = coarse_part.reshape(BLOCK, SIDE, -1).transpose(1, 0, 2)
    coarse_data = (scale_e2 * exchanged(coarse_part, COL).sum(axis=0)).astype(bf16)
    coarse_data = gathered(coarse_data, COL).transpose(1, 0, 2).reshape(BLOCK, coarse)
    halfway = jnp.dot(coarse_data, factor_down, preferred_element_type=f32).astype(bf16)
    halfway = gathered(halfway, COL)
    coarse_here = jnp.einsum("kfj,kij->fi", halfway, factor_across, preferred_element_type=f32)
    coarse_low = gathered(coarse_here.astype(bf16), COL).transpose(1, 0, 2).reshape(BLOCK, coarse)
    correction = jnp.dot(coarse_low, coarse_kernel, preferred_element_type=f32)
    mid_new = 0.5 * mid_data + scale_e2 * correction

    new_halves = gathered_row(mid_new.astype(bf16))
    fine_part = product_of_tiles(list_e1, tiles_out, new_halves, rows_fine, False, True)
    fine_sum = exchanged(fine_part, COL).astype(f32).sum(axis=0)
    fine_sum = in_field_order(fine_sum.reshape(2, half, BLOCK, share), core)
    own_data = lax.dynamic_slice_in_dim(values, col_id * share, share, 0).astype(f32)
    fine_coef = 0.5 * own_data + scale_e1 * fine_sum

    mid_coef = in_field_order(jnp.stack(gathered_row(mid_new)), core)
    coarse_coef = gathered(turned(coarse_here), COL).transpose(2, 0, 1).reshape(-1, fields)
    total = gathered(squares[None], ALL).sum()
    norm = total / (rows_fine * SIDE * fields)
    return (fine_coef, mid_coef, coarse_coef, jnp.stack([norm]))


def solution(mesh):
    fine_mesh = Mesh(mesh.devices.reshape(4, 2, 2, 4, 4), ALL)
    return jax.shard_map(
        per_device,
        mesh=fine_mesh,
        in_specs=(
            P(ROW, None),
            P(None, ROW),
            P(None, ROW),
            P(None, ROW),
            P(ROW, COL, None, None),
            P(ROW, COL, None, None),
            P(ROW, COL, None, None),
            P(ROW, COL),
        ),
        out_specs=(P(ALL, None), P(COL, None), P(ROW, None), P()),
        check_vma=False,
    )
```

```python
import jax
import jax.numpy as jnp
from jax import lax
from jax.experimental import pallas as pl
from jax.experimental.pallas import tpu as pltpu
from jax.sharding import Mesh
from jax.sharding import PartitionSpec as P

TILE = 128
SIDE = 16
HALF = 8
BLOCK = 8
FIELDS = SIDE * BLOCK
GROUP = 16

support_fine = 0.35
support_mid = 0.55
support_coarse = 0.8

ROW = ("y", "zh", "k")
YZ = ("y", "zh")
COL = ("x", "zl")
ALL = ROW + COL

bf16 = jnp.bfloat16
f32 = jnp.float32

VMEM = pl.BlockSpec(memory_space=pltpu.VMEM)
SMEM = pl.BlockSpec(memory_space=pltpu.SMEM)


def room(mebibytes):
    return pltpu.CompilerParams(vmem_limit_bytes=mebibytes * 1024 * 1024)


def hint(microseconds):
    return pl.CostEstimate(
        flops=0, transcendentals=0, bytes_accessed=int(microseconds * 3.0e6)
    )


def turned(x):
    pairs = [(c * SIDE + r, r * SIDE + c) for r in range(SIDE) for c in range(SIDE)]
    return lax.ppermute(x, ALL, pairs)


def place_of_block(block, core):
    return ((block % 2) ^ core) * HALF + block // 2


def turned_blocks(x):
    pairs = [
        (c * SIDE + place_of_block(r, c % 2), r * SIDE + c) for r in range(SIDE) for c in range(SIDE)
    ]
    return lax.ppermute(x, ALL, pairs)


def from_partner(x):
    return lax.ppermute(x, "k", [(0, 1), (1, 0)])


def exchanged(x, axes):
    return lax.all_to_all(x, axes, split_axis=0, concat_axis=0, tiled=True)


def gathered(x, axes):
    return exchanged(jnp.broadcast_to(x, (lax.axis_size(axes), *x.shape)), axes)


def pair_sum(own, other):
    return (own.astype(f32) + from_partner(other).astype(f32)).astype(bf16)


def after(x, *others):
    return lax.optimization_barrier((x, *others))[0]


def parts_of(x):
    high = lax.reduce_precision(x, 8, 7)
    rest = x - high
    middle = lax.reduce_precision(rest, 8, 7)
    return jnp.stack([high, middle, rest - middle]).astype(bf16)


def stretch_of(support):
    return (4.0 / support**5) ** 0.2


def along(points, support):
    return (points.astype(f32) * stretch_of(support)).reshape(2, -1, 1, TILE)


def wendland(left, right, support):
    across, upward = left[0] - right[0], left[1] - right[1]
    square = jnp.maximum(across * across + upward * upward, 1e-30)
    edge = support * stretch_of(support)
    margin = jnp.maximum(edge - square * lax.rsqrt(square), 0.0)
    margin2 = margin * margin
    ratio = 5.0 / edge**4
    return (margin2 * margin2 * (ratio - margin)).astype(bf16)


def at_tile(i):
    return pl.ds(pl.multiple_of(i * TILE, TILE), TILE)


def spread(points, support):
    rows = along(points, support)
    tiles = rows.shape[1]

    def kernel(row_ref, out_ref):
        for axis in range(2):
            for t in range(tiles):
                out_ref[axis, t] = jnp.broadcast_to(row_ref[axis, t], (TILE, TILE)).T

    return pl.pallas_call(
        kernel,
        out_shape=jax.ShapeDtypeStruct((2, tiles, TILE, TILE), f32),
        in_specs=[VMEM],
        out_specs=VMEM,
        compiler_params=room(12),
        cost_estimate=hint(tiles / 8),
        name="spread",
    )(rows)


def add_tiles(list_ref, contracted, left_ref, right_ref, vector, total, support):
    listed = list_ref.shape[1]

    def step(g, carry):
        products = []
        for u in range(GROUP):
            j = list_ref[contracted, g * GROUP + u]
            i = list_ref[1 - contracted, g * GROUP + u]
            tile = wendland(
                (left_ref[0, j], left_ref[1, j]), (right_ref[0, i], right_ref[1, i]), support
            )
            product = jnp.dot(vector[:, at_tile(j)], tile, preferred_element_type=f32)
            products.append((i, product))
        for i, product in products:
            total[i] += product
        return carry

    lax.fori_loop(0, listed // GROUP, step, 0)


def product_a0(listing, place, left, right, vector):
    listed = listing.shape[1]
    tiles = right.shape[1]

    def kernel(list_ref, place_ref, left_ref, right_ref, vector_ref, own_ref, other_ref, total):
        me = place_ref[0]
        weight = jnp.where(place_ref[1] == place_ref[2], -2.0 / scale_of(tiles, listed), 0.0)
        for i in range(tiles):
            at = pl.ds(i * TILE, TILE)
            total[i] = vector_ref[:, at].astype(f32) * weight
        add_tiles(list_ref, 1, left_ref, right_ref, vector_ref, total, support_fine)
        for half in range(HALF):
            for i in range(tiles):
                at = pl.ds(i * TILE, TILE)
                own = pl.ds(pl.multiple_of((2 * half + me) * BLOCK, BLOCK), BLOCK)
                other = pl.ds(pl.multiple_of((2 * half + 1 - me) * BLOCK, BLOCK), BLOCK)
                own_ref[half, :, at] = total[i, own, :].astype(bf16)
                other_ref[half, :, at] = total[i, other, :].astype(bf16)

    half = jax.ShapeDtypeStruct((HALF, BLOCK, tiles * TILE), bf16)
    return pl.pallas_call(
        kernel,
        out_shape=(half, half),
        in_specs=[SMEM, SMEM, VMEM, VMEM, VMEM],
        out_specs=(VMEM, VMEM),
        scratch_shapes=[pltpu.VMEM((tiles, FIELDS, TILE), f32)],
        compiler_params=room(18),
        cost_estimate=hint(20),
        name="product_a0",
    )(listing, place, left, right, vector)


def product(listing, contracted, left, right, halves, support, form):
    listed = listing.shape[1]
    tiles = right.shape[1]
    length = left.shape[1] * TILE

    def kernel(list_ref, left_ref, right_ref, own_ref, other_ref, *rest):
        *outs, vector, total = rest
        total[...] = jnp.zeros_like(total)
        for ref, first in ((own_ref, 0), (other_ref, FIELDS // 2)):
            rows = ref[:, :, pl.ds(0, length)].reshape(FIELDS // 2, length)
            vector[pl.ds(first, FIELDS // 2), :] = rows.astype(bf16)
        add_tiles(list_ref, contracted, left_ref, right_ref, vector, total, support)
        for i in range(tiles):
            low = total[i].astype(bf16)
            if form == "shares":
                each = tiles // SIDE
                outs[0][i // each, :, pl.ds(i % each * TILE, TILE)] = low
            elif form == "blocks":
                outs[0][:, :, pl.ds(i * TILE, TILE)] = low.reshape(SIDE, BLOCK, TILE)
            else:
                pair = low.reshape(2, HALF, BLOCK, TILE)
                outs[0][:, :, pl.ds(i * TILE, TILE)] = pair[0]
                outs[1][:, :, pl.ds(i * TILE, TILE)] = pair[1]

    size = tiles * TILE
    if form == "shares":
        shapes = [(SIDE, FIELDS, size // SIDE)]
    elif form == "blocks":
        shapes = [(SIDE, BLOCK, size)]
    else:
        shapes = [(HALF, BLOCK, size)] * 2
    return pl.pallas_call(
        kernel,
        out_shape=[jax.ShapeDtypeStruct(shape, bf16) for shape in shapes],
        in_specs=[SMEM, VMEM, VMEM, VMEM, VMEM],
        out_specs=[VMEM] * len(shapes),
        scratch_shapes=[
            pltpu.VMEM((FIELDS, length), bf16),
            pltpu.VMEM((tiles, FIELDS, TILE), f32),
        ],
        compiler_params=room(18),
        cost_estimate=hint(listed / 18),
        name="product_" + form,
    )(listing, left, right, *halves)


def all_pairs(left, right, support):
    rows, cols = left.shape[1], right.shape[1]

    def kernel(left_ref, right_ref, out_ref):
        for j in range(cols):
            out_ref[:, pl.ds(j * TILE, TILE)] = wendland(
                (left_ref[0, 0], left_ref[1, 0]), (right_ref[0, j], right_ref[1, j]), support
            )

    return pl.pallas_call(
        kernel,
        out_shape=jax.ShapeDtypeStruct((rows * TILE, cols * TILE), bf16),
        grid=(rows,),
        in_specs=[pl.BlockSpec((2, 1, TILE, TILE), lambda i: (0, i, 0, 0)), VMEM],
        out_specs=pl.BlockSpec((TILE, cols * TILE), lambda i: (i, 0)),
        compiler_params=room(16),
        cost_estimate=hint(8),
        name="all_pairs",
    )(left, right)


def coarse_product(matrix, vector):
    rows, cols = matrix.shape

    def kernel(matrix_ref, vector_ref, out_ref, turned_ref):
        for t in range(cols // TILE):
            at = pl.ds(t * TILE, TILE)
            lines = vector_ref[:, at]
            full = jnp.concatenate([lines, jnp.zeros((TILE - BLOCK, TILE), f32)], axis=0)
            turned_ref[at, :] = full.T.astype(bf16)
        for q in range(rows // TILE):
            at = pl.ds(q * TILE, TILE)
            part = jnp.dot(matrix_ref[at, :], turned_ref[...], preferred_element_type=f32)
            out_ref[q] = part.T[:BLOCK, :]

    return pl.pallas_call(
        kernel,
        out_shape=jax.ShapeDtypeStruct((rows // TILE, BLOCK, TILE), f32),
        in_specs=[VMEM, VMEM],
        out_specs=VMEM,
        scratch_shapes=[pltpu.VMEM((cols, TILE), bf16)],
        compiler_params=room(12),
        cost_estimate=hint(3),
        name="coarse_product",
    )(matrix, vector)


def prolong(matrix, coarse_coef, mid_data, scale):
    rows, cols = matrix.shape
    two = 2 * TILE

    def kernel(matrix_ref, coef_ref, mid_ref, out_ref):
        total = jnp.zeros((BLOCK, cols), f32)
        for q in range(rows // two):
            pair = jnp.concatenate([coef_ref[2 * q], coef_ref[2 * q + 1]], axis=1)
            out_ref[q, :, pl.ds(cols, two)] = pair
            total += jnp.dot(
                pair.astype(bf16), matrix_ref[pl.ds(q * two, two), :], preferred_element_type=f32
            )
        coef = 0.5 * mid_ref[...] + scale * total
        for q in range(rows // two):
            out_ref[q, :, pl.ds(0, cols)] = coef

    return pl.pallas_call(
        kernel,
        out_shape=jax.ShapeDtypeStruct((rows // two, BLOCK, cols + two), f32),
        in_specs=[VMEM, VMEM, VMEM],
        out_specs=VMEM,
        compiler_params=room(12),
        cost_estimate=hint(3),
        name="prolong",
    )(matrix, coarse_coef, mid_data)


def in_field_order(x, core):
    n = x.shape[-1]
    x = jnp.where(core == 0, x, x[::-1])
    return x.transpose(3, 1, 0, 2).reshape(n, FIELDS)


def scale_of(tiles, listed):
    return (tiles * TILE / (SIDE * listed * TILE * TILE)) ** 0.5


def per_device(values, points0, points1, points2, tiles_a0, tiles_e1, tiles_a1, factor):
    core = lax.axis_index("k")
    col_id = lax.axis_index(COL)
    row_id = lax.axis_index(ROW)
    rows_fine, fields = values.shape
    rows_mid = points1.shape[1]
    rows_coarse = points2.shape[1]
    coarse = rows_coarse * SIDE
    share = rows_fine // SIDE
    tiles_fine, tiles_mid = rows_fine // TILE, rows_mid // TILE
    list_a0, list_e1, list_a1 = tiles_a0[0, 0], tiles_e1[0, 0], tiles_a1[0, 0]
    scale_a0 = scale_of(tiles_fine, list_a0.shape[1])
    scale_e1 = scale_of(tiles_fine, list_e1.shape[1])
    scale_a1 = scale_of(tiles_mid, list_a1.shape[1])
    scale_e2 = (1.0 / (rows_mid * SIDE)) ** 0.5

    lists = jnp.concatenate([list_a0, list_e1, list_a1], axis=1)
    sent = [points0, points1, lists, factor]
    lines = [a.astype(bf16).reshape(-1, TILE) for a in sent]
    ends = [0]
    for a in lines:
        ends.append(ends[-1] + a.shape[0])
    there = turned(jnp.concatenate(lines, axis=0))
    came = [there[b:e].reshape(a.shape) for a, b, e in zip(sent, ends, ends[1:])]
    fine_there, mid_there, lists, factor_there = came
    cuts = (list_a0.shape[1], list_a0.shape[1] + list_e1.shape[1])
    turned_a0, turned_e1, turned_a1 = jnp.split(lists.astype(jnp.int32), cuts, axis=1)
    place = jnp.stack([core, row_id, col_id]).astype(jnp.int32)

    centres = jnp.pad(points2, ((0, 2 * BLOCK - 2), (0, 0)))
    common = gathered(jnp.concatenate([factor, factor_there, centres], axis=0), YZ)
    own, other = product_a0(
        turned_a0, place, spread(points0, support_fine), along(fine_there, support_fine), values.T
    )
    own, other, common = lax.optimization_barrier((own, other, common))
    pair = pair_sum(own, other)

    arrived = exchanged(pair, YZ)
    fine_later, mid_here, mid_later, common, pair = lax.optimization_barrier(
        (fine_there, points1, mid_there, common, pair)
    )
    spread_fine = spread(fine_later, support_mid)
    spread_here = spread(mid_here, support_mid)
    spread_there = spread(mid_later, support_mid)
    residual = (-0.5 * scale_a0) * arrived.astype(f32).sum(axis=0)
    residual, spread_fine, spread_here, spread_there, common, mid_later = lax.optimization_barrier(
        (residual, spread_fine, spread_here, spread_there, common, mid_later)
    )
    partner = from_partner(common)

    def in_row_order(first, size):
        mine, its = common[:, first : first + size], partner[:, first : first + size]
        return jnp.stack([jnp.where(core == 0, mine, its), jnp.where(core == 0, its, mine)], axis=1)

    factor_down = in_row_order(0, rows_coarse).reshape(coarse, -1)
    factor_across = in_row_order(rows_coarse, rows_coarse).reshape(SIDE, rows_coarse, -1)
    centres = in_row_order(2 * rows_coarse, 2 * BLOCK).reshape(SIDE, 2 * BLOCK, -1)[:, :2]
    centres = centres.transpose(1, 0, 2).reshape(2, coarse)
    coarse_kernel = all_pairs(
        spread(centres, support_coarse), along(mid_later, support_coarse), support_coarse
    )

    squares = jnp.sum(residual * residual, axis=0).reshape(-1, TILE).sum(axis=0)
    squares = jnp.pad(parts_of(squares), ((0, BLOCK - 3), (0, 0)))
    fine_own = gathered(jnp.concatenate([residual.astype(bf16), squares], axis=1), YZ)
    fine_own, coarse_kernel, factor_down, factor_across = lax.optimization_barrier(
        (fine_own, coarse_kernel, factor_down, factor_across)
    )
    fine_other = from_partner(fine_own)
    squares = sum(h[:, :, rows_fine:].astype(f32).sum(axis=(0, 1)) for h in (fine_own, fine_other))

    (restricted,) = product(
        turned_e1, 0, spread_fine, along(points1, support_mid), (fine_own, fine_other), support_mid, "blocks"
    )
    mid_share = scale_e1 * exchanged(restricted, COL).astype(f32).sum(axis=0)
    mid_all = gathered(mid_share.astype(bf16), COL)
    mid_data = turned_blocks(mid_share)

    mid_own, mid_other = product(
        turned_a1,
        1,
        spread_here,
        along(mid_there, support_mid),
        (mid_all[:HALF], mid_all[HALF:]),
        support_mid,
        "halves",
    )
    mid_prod = scale_a1 * exchanged(pair_sum(mid_own, mid_other), YZ).astype(f32).sum(axis=0)
    mid_residual = mid_data - 0.5 * mid_prod.astype(bf16).astype(f32)

    coarse_part = coarse_product(coarse_kernel, mid_residual)
    coarse_data = (scale_e2 * exchanged(coarse_part, COL).sum(axis=0)).astype(bf16)
    squares = jnp.pad(parts_of(squares), ((0, BLOCK - 3), (0, 0)))
    coarse_data = gathered(jnp.concatenate([coarse_data, squares], axis=0), COL)
    norm = coarse_data[:, BLOCK:].astype(f32).sum() / (rows_fine * SIDE * fields)
    coarse_data = coarse_data[:, :BLOCK].transpose(1, 0, 2).reshape(BLOCK, coarse)
    halfway = jnp.dot(coarse_data, factor_down, preferred_element_type=f32).astype(bf16)
    halfway = gathered(halfway, COL)
    coarse_here = jnp.einsum("kfj,kij->fi", halfway, factor_across, preferred_element_type=f32)
    coarse_all = gathered(coarse_here, COL)

    new = prolong(coarse_kernel, coarse_all, mid_data, scale_e2)
    new_own = exchanged(new, YZ)
    new_other = from_partner(new_own)
    (fine_part,) = product(
        list_e1,
        1,
        spread_there,
        along(points0, support_mid),
        (new_own, new_other),
        support_mid,
        "shares",
    )
    fine_sum = exchanged(fine_part, COL).astype(f32).sum(axis=0)
    fine_sum = in_field_order(fine_sum.reshape(2, HALF, BLOCK, share), core)
    own_data = lax.dynamic_slice_in_dim(values, col_id * share, share, 0).astype(f32)
    fine_coef = 0.5 * own_data + scale_e1 * fine_sum

    both = jnp.stack([new_own, new_other])
    mid_coef = in_field_order(both[..., :rows_mid], core)
    coarse_coef = lax.dynamic_slice_in_dim(both, rows_mid + core * rows_coarse, rows_coarse, 3)
    coarse_coef = in_field_order(coarse_coef, core)
    return (fine_coef, mid_coef, coarse_coef, jnp.stack([norm]))


def solution(mesh):
    fine_mesh = Mesh(mesh.devices.reshape(4, 2, 2, 4, 4), ALL)
    return jax.shard_map(
        per_device,
        mesh=fine_mesh,
        in_specs=(
            P(ROW, None),
            P(None, ROW),
            P(None, ROW),
            P(None, ROW),
            P(ROW, COL, None, None),
            P(ROW, COL, None, None),
            P(ROW, COL, None, None),
            P(ROW, COL),
        ),
        out_specs=(P(ALL, None), P(COL, None), P(ROW, None), P()),
        check_vma=False,
    )
```

```python
import jax
import jax.numpy as jnp
from jax import lax
from jax.experimental import pallas as pl
from jax.experimental.pallas import tpu as pltpu
from jax.sharding import Mesh
from jax.sharding import PartitionSpec as P

TILE = 128
SIDE = 16
HALF = 8
BLOCK = 8
FIELDS = SIDE * BLOCK
GROUP = 16

support_fine = 0.35
support_mid = 0.55
support_coarse = 0.8

ROW = ("y", "zh", "k")
YZ = ("y", "zh")
COL = ("x", "zl")
ALL = ROW + COL

bf16 = jnp.bfloat16
f32 = jnp.float32

VMEM = pl.BlockSpec(memory_space=pltpu.VMEM)
SMEM = pl.BlockSpec(memory_space=pltpu.SMEM)


def room(mebibytes):
    return pltpu.CompilerParams(vmem_limit_bytes=mebibytes * 1024 * 1024)


def hint(microseconds):
    return pl.CostEstimate(
        flops=0, transcendentals=0, bytes_accessed=int(microseconds * 3.0e6)
    )


def turned(x):
    pairs = [(c * SIDE + r, r * SIDE + c) for r in range(SIDE) for c in range(SIDE)]
    return lax.ppermute(x, ALL, pairs)


def place_of_block(block, core):
    return ((block % 2) ^ core) * HALF + block // 2


def turned_blocks(x):
    pairs = [
        (c * SIDE + place_of_block(r, c % 2), r * SIDE + c) for r in range(SIDE) for c in range(SIDE)
    ]
    return lax.ppermute(x, ALL, pairs)


def from_partner(x):
    return lax.ppermute(x, "k", [(0, 1), (1, 0)])


def exchanged(x, axes):
    return lax.all_to_all(x, axes, split_axis=0, concat_axis=0, tiled=True)


def pair_sum(own, other):
    return (own.astype(f32) + from_partner(other).astype(f32)).astype(bf16)


def stretch_of(support):
    return (4.0 / support**5) ** 0.2


def wendland(left, right, support):
    across, upward = left[0] - right[0], left[1] - right[1]
    square = jnp.maximum(across * across + upward * upward, 1e-30)
    edge = support * stretch_of(support)
    margin = jnp.maximum(edge - square * lax.rsqrt(square), 0.0)
    margin2 = margin * margin
    ratio = 5.0 / edge**4
    return (margin2 * margin2 * (ratio - margin)).astype(bf16)


def at_tile(i):
    return pl.ds(pl.multiple_of(i * TILE, TILE), TILE)


def call(kernel, shapes, operands, name, mebibytes, microseconds, scratch=(), scalars=0):
    out = pl.pallas_call(
        kernel,
        out_shape=[jax.ShapeDtypeStruct(shape, kind) for shape, kind in shapes],
        in_specs=[SMEM] * scalars + [VMEM] * (len(operands) - scalars),
        out_specs=[VMEM] * len(shapes),
        scratch_shapes=list(scratch),
        compiler_params=room(mebibytes),
        cost_estimate=hint(microseconds),
        name=name,
    )(*operands)
    return out if len(shapes) > 1 else out[0]


def rows_of(listed):
    return -(-listed // TILE)


def in_rows(listing):
    rows = rows_of(listing.shape[1])
    padded = jnp.pad(listing, ((0, 0), (0, rows * TILE - listing.shape[1])))
    return padded.reshape(2 * rows, TILE)


def packed(points0, points1, lists, factor):
    fine, mid = points0.shape[1] // TILE, points1.shape[1] // TILE
    used = 2 * (fine + mid) + lists.shape[0]
    above = -(-used // SIDE) * SIDE

    def kernel(fine_ref, mid_ref, list_ref, factor_ref, out_ref):
        lines = []
        for ref, tiles in ((fine_ref, fine), (mid_ref, mid)):
            whole = ref[...].astype(f32)
            lines += [
                whole[a : a + 1, t * TILE : (t + 1) * TILE] for a in range(2) for t in range(tiles)
            ]
        lines.append(list_ref[...].astype(f32))
        if above > used:
            lines.append(jnp.zeros((above - used, TILE), f32))
        out_ref[pl.ds(0, above), :] = jnp.concatenate(lines, axis=0).astype(bf16)
        out_ref[pl.ds(above, TILE), :] = factor_ref[...]

    shapes = [((above + TILE, TILE), bf16)]
    return call(kernel, shapes, (points0, points1, lists, factor), "packed", 8, 1)


def unpacked(there, factor, centres, fine, mid, listed):
    used = 2 * (fine + mid) + listed
    above = -(-used // SIDE) * SIDE
    size = 2 * TILE + SIDE

    def kernel(there_ref, factor_ref, centre_ref, fine_ref, mid_ref, list_ref, common_ref):
        lines = there_ref[pl.ds(0, above), :].astype(f32)
        at = 0
        for ref, tiles in ((fine_ref, fine), (mid_ref, mid)):
            for a in range(2):
                for t in range(tiles):
                    ref[a, t] = lines[at : at + 1]
                    at += 1
        list_ref[...] = lines[at : at + listed].astype(jnp.int32)
        for chip in range(HALF):
            common_ref[chip, pl.ds(0, TILE), :] = factor_ref[...]
            common_ref[chip, pl.ds(TILE, TILE), :] = there_ref[pl.ds(above, TILE), :]
            common_ref[chip, pl.ds(2 * TILE, SIDE), :] = centre_ref[...]

    shapes = [
        ((2, fine, 1, TILE), f32),
        ((2, mid, 1, TILE), f32),
        ((listed, TILE), jnp.int32),
        ((HALF, size, TILE), bf16),
    ]
    return call(kernel, shapes, (there, factor, centres), "unpacked", 8, 1)


def set_points(left_ref, right_ref, left, right, support):
    stretch = stretch_of(support)
    for axis in range(2):
        for t in range(left.shape[1]):
            row = left_ref[axis, t] * stretch
            left[axis, t] = jnp.broadcast_to(row, (TILE, TILE)).T
        for t in range(right.shape[1]):
            right[axis, t] = right_ref[axis, t] * stretch


def point_scratch(left, right):
    return [pltpu.VMEM((2, left, TILE, TILE), f32), pltpu.VMEM((2, right, 1, TILE), f32)]


def add_tiles(list_ref, listed, first, contracted, left, right, vector, total, support):
    rows = rows_of(listed)
    steps = TILE // GROUP
    line_j = first + contracted * rows
    line_i = first + (1 - contracted) * rows

    def step(g, carry):
        row, lane = g // steps, g % steps * GROUP
        products = []
        for u in range(GROUP):
            j = list_ref[line_j + row, lane + u]
            i = list_ref[line_i + row, lane + u]
            tile = wendland((left[0, j], left[1, j]), (right[0, i], right[1, i]), support)
            product = jnp.dot(vector[:, at_tile(j)], tile, preferred_element_type=f32)
            products.append((i, product))
        for i, product in products:
            total[i] += product
        return carry

    lax.fori_loop(0, listed // GROUP, step, 0)


def product_a0(lists, place, left, right, vector, listed):
    tiles = right.shape[1]

    def kernel(
        list_ref, place_ref, left_ref, right_ref, vector_ref, own_ref, other_ref, left, right, total
    ):
        set_points(left_ref, right_ref, left, right, support_fine)
        me = place_ref[0]
        weight = jnp.where(place_ref[1] == place_ref[2], -2.0 / scale_of(tiles, listed), 0.0)
        for i in range(tiles):
            at = pl.ds(i * TILE, TILE)
            total[i] = vector_ref[:, at].astype(f32) * weight
        add_tiles(list_ref, listed, 0, 1, left, right, vector_ref, total, support_fine)
        for half in range(HALF):
            for i in range(tiles):
                at = pl.ds(i * TILE, TILE)
                own = pl.ds(pl.multiple_of((2 * half + me) * BLOCK, BLOCK), BLOCK)
                other = pl.ds(pl.multiple_of((2 * half + 1 - me) * BLOCK, BLOCK), BLOCK)
                own_ref[half, :, at] = total[i, own, :].astype(bf16)
                other_ref[half, :, at] = total[i, other, :].astype(bf16)

    half = ((HALF, BLOCK, tiles * TILE), bf16)
    scratch = [*point_scratch(left.shape[1], tiles), pltpu.VMEM((tiles, FIELDS, TILE), f32)]
    operands = (lists, place, left, right, vector)
    return call(kernel, [half, half], operands, "product_a0", 16, 20, scratch, 2)


def product(lists, listed, first, contracted, left, right, halves, support, form):
    tiles = right.shape[1]
    length = left.shape[1] * TILE

    def kernel(list_ref, left_ref, right_ref, own_ref, other_ref, *rest):
        *outs, left, right, vector, total = rest
        set_points(left_ref, right_ref, left, right, support)
        total[...] = jnp.zeros_like(total)
        for ref, at in ((own_ref, 0), (other_ref, FIELDS // 2)):
            rows = ref[:, :, pl.ds(0, length)].reshape(FIELDS // 2, length)
            vector[pl.ds(at, FIELDS // 2), :] = rows
        add_tiles(list_ref, listed, first, contracted, left, right, vector, total, support)
        for i in range(tiles):
            low = total[i].astype(bf16)
            if form == "shares":
                each = tiles // SIDE
                outs[0][i // each, :, pl.ds(i % each * TILE, TILE)] = low
            elif form == "blocks":
                outs[0][:, :, pl.ds(i * TILE, TILE)] = low.reshape(SIDE, BLOCK, TILE)
            else:
                pair = low.reshape(2, HALF, BLOCK, TILE)
                outs[0][:, :, pl.ds(i * TILE, TILE)] = pair[0]
                outs[1][:, :, pl.ds(i * TILE, TILE)] = pair[1]

    size = tiles * TILE
    if form == "shares":
        shapes = [((SIDE, FIELDS, size // SIDE), bf16)]
    elif form == "blocks":
        shapes = [((SIDE, BLOCK, size), bf16)]
    else:
        shapes = [((HALF, BLOCK, size), bf16)] * 2
    scratch = [
        *point_scratch(left.shape[1], tiles),
        pltpu.VMEM((FIELDS, length), bf16),
        pltpu.VMEM((tiles, FIELDS, TILE), f32),
    ]
    operands = (lists, left, right, *halves)
    return call(kernel, shapes, operands, "product_" + form, 16, listed / 18, scratch, 1)


def all_pairs(left, right, support):
    rows, cols = left.shape[1], right.shape[1]

    def kernel(left_ref, right_ref, out_ref):
        stretch = stretch_of(support)
        ys = [jnp.broadcast_to(left_ref[a, 0] * stretch, (TILE, TILE)).T for a in range(2)]
        for j in range(cols):
            out_ref[:, pl.ds(j * TILE, TILE)] = wendland(
                ys, (right_ref[0, j] * stretch, right_ref[1, j] * stretch), support
            )

    return pl.pallas_call(
        kernel,
        out_shape=jax.ShapeDtypeStruct((rows * TILE, cols * TILE), bf16),
        grid=(rows,),
        in_specs=[pl.BlockSpec((2, 1, 1, TILE), lambda i: (0, i, 0, 0)), VMEM],
        out_specs=pl.BlockSpec((TILE, cols * TILE), lambda i: (i, 0)),
        compiler_params=room(8),
        cost_estimate=hint(6),
        name="all_pairs",
    )(left, right)


def residual_of(arrived, scale):
    chips, _, n = arrived.shape

    def kernel(arrived_ref, out_ref):
        squares = jnp.zeros((1, TILE), f32)
        for t in range(n // TILE):
            at = pl.ds(t * TILE, TILE)
            part = scale * arrived_ref[:, :, at].astype(f32).sum(axis=0)
            squares += jnp.sum(part * part, axis=0, keepdims=True)
            low = part.astype(bf16)
            for chip in range(chips):
                out_ref[chip, :, at] = low
        tail = three_rows(squares)
        for chip in range(chips):
            out_ref[chip, :, pl.ds(n, TILE)] = tail

    return call(kernel, [((chips, BLOCK, n + TILE), bf16)], (arrived,), "residual_of", 8, 1)


def three_rows(x):
    high = x.astype(bf16).astype(f32)
    rest = x - high
    middle = rest.astype(bf16).astype(f32)
    rows = [high, middle, rest - middle, jnp.zeros((BLOCK - 3, TILE), f32)]
    return jnp.concatenate(rows, axis=0).astype(bf16)


def mid_of(arrived, scale):
    peers, _, n = arrived.shape

    def kernel(arrived_ref, out_ref, low_ref):
        part = scale * arrived_ref[...].astype(f32).sum(axis=0)
        out_ref[...] = part
        low = part.astype(bf16)
        for peer in range(peers):
            low_ref[peer] = low

    shapes = [((BLOCK, n), f32), ((peers, BLOCK, n), bf16)]
    return call(kernel, shapes, (arrived,), "mid_of", 8, 1)


def coarse_product(matrix, arrived, mid_data, scale):
    rows, cols = matrix.shape

    def kernel(matrix_ref, arrived_ref, mid_ref, out_ref, turned_ref):
        @pl.when(pl.program_id(0) == 0)
        def _():
            whole = (scale * arrived_ref[...].astype(f32).sum(axis=0)).astype(bf16).astype(f32)
            whole = mid_ref[...] - 0.5 * whole
            for t in range(cols // TILE):
                lines = whole[:, t * TILE : (t + 1) * TILE]
                full = jnp.concatenate([lines, jnp.zeros((TILE - BLOCK, TILE), f32)], axis=0)
                turned_ref[pl.ds(t * TILE, TILE), :] = full.T.astype(bf16)

        for q in range(2):
            at = pl.ds(q * TILE, TILE)
            part = jnp.dot(matrix_ref[at, :], turned_ref[...], preferred_element_type=f32)
            out_ref[q] = part.T[:BLOCK, :]

    return pl.pallas_call(
        kernel,
        out_shape=jax.ShapeDtypeStruct((rows // TILE, BLOCK, TILE), f32),
        grid=(rows // TILE // 2,),
        in_specs=[pl.BlockSpec((2 * TILE, cols), lambda q: (q, 0)), VMEM, VMEM],
        out_specs=pl.BlockSpec((2, BLOCK, TILE), lambda q: (q, 0, 0)),
        scratch_shapes=[pltpu.VMEM((cols, TILE), bf16)],
        compiler_params=room(8),
        cost_estimate=hint(3),
        name="coarse_product",
    )(matrix, arrived, mid_data)


def coarse_data_of(arrived, own, other, scale):
    peers = arrived.shape[0]
    n = own.shape[2] - TILE

    def kernel(arrived_ref, own_ref, other_ref, out_ref):
        data = (scale * arrived_ref[...].sum(axis=0)).astype(bf16)
        squares = jnp.zeros((1, TILE), f32)
        for ref in (own_ref, other_ref):
            tails = ref[...].astype(f32).sum(axis=0)
            squares += jnp.sum(tails, axis=0, keepdims=True)
        tail = three_rows(squares)
        for peer in range(peers):
            out_ref[peer, 0] = data
            out_ref[peer, 1] = tail

    tails = (own[:, :, n:], other[:, :, n:])
    shapes = [((peers, 2, BLOCK, TILE), bf16)]
    return call(kernel, shapes, (arrived, *tails), "coarse_data_of", 8, 1)


def halfway_of(gathered_data, factor_down):
    peers = gathered_data.shape[0]

    def kernel(data_ref, factor_ref, out_ref):
        total = jnp.zeros((BLOCK, TILE), f32)
        for q in range(peers // 2):
            pair = jnp.concatenate([data_ref[2 * q, 0], data_ref[2 * q + 1, 0]], axis=1)
            rows = factor_ref[pl.ds(q * 2 * TILE, 2 * TILE), :]
            total += jnp.dot(pair, rows, preferred_element_type=f32)
        low = total.astype(bf16)
        for peer in range(peers):
            out_ref[peer] = low

    shapes = [((peers, BLOCK, TILE), bf16)]
    return call(kernel, shapes, (gathered_data, factor_down), "halfway_of", 8, 1)


def coarse_coef_of(halfway, factor_across):
    peers = halfway.shape[0]

    def kernel(half_ref, factor_ref, out_ref):
        total = jnp.zeros((BLOCK, TILE), f32)
        for q in range(peers):
            total += lax.dot_general(
                half_ref[q], factor_ref[q], (((1,), (1,)), ((), ())), preferred_element_type=f32
            )
        for peer in range(peers):
            out_ref[peer] = total

    shapes = [((peers, BLOCK, TILE), f32)]
    return call(kernel, shapes, (halfway, factor_across), "coarse_coef_of", 8, 1)


def prolong(matrix, coarse_coef, mid_data, scale):
    rows, cols = matrix.shape
    two = 2 * TILE
    steps = rows // two

    def kernel(matrix_ref, coef_ref, mid_ref, out_ref, total):
        q = pl.program_id(0)

        @pl.when(q == 0)
        def _():
            total[...] = jnp.zeros_like(total)

        pair = jnp.concatenate([coef_ref[0], coef_ref[1]], axis=1).astype(bf16)
        out_ref[q, :, pl.ds(cols, two)] = pair
        total[...] += jnp.dot(pair, matrix_ref[...], preferred_element_type=f32)

        @pl.when(q == steps - 1)
        def _():
            low = (0.5 * mid_ref[...] + scale * total[...]).astype(bf16)
            for chip in range(steps):
                out_ref[chip, :, pl.ds(0, cols)] = low

    return pl.pallas_call(
        kernel,
        out_shape=jax.ShapeDtypeStruct((steps, BLOCK, cols + two), bf16),
        grid=(steps,),
        in_specs=[
            pl.BlockSpec((two, cols), lambda q: (q, 0)),
            pl.BlockSpec((2, BLOCK, TILE), lambda q: (q, 0, 0)),
            VMEM,
        ],
        out_specs=VMEM,
        scratch_shapes=[pltpu.VMEM((BLOCK, cols), f32)],
        compiler_params=room(8),
        cost_estimate=hint(3),
        name="prolong",
    )(matrix, coarse_coef, mid_data)


def fine_of(arrived, data, core, scale):
    n = arrived.shape[2]

    def kernel(core_ref, arrived_ref, data_ref, out_ref, summed):
        me = core_ref[0]
        summed[...] = arrived_ref[...].astype(f32).sum(axis=0)
        rows = []
        for block in range(SIDE):
            at = ((block % 2) ^ me) * HALF + block // 2
            rows.append(summed[pl.ds(pl.multiple_of(at * BLOCK, BLOCK), BLOCK), :])
        whole = jnp.concatenate(rows, axis=0)
        for t in range(n // TILE):
            at = pl.ds(t * TILE, TILE)
            data = data_ref[at, :].astype(f32)
            out_ref[at, :] = 0.5 * data + scale * whole[:, t * TILE : (t + 1) * TILE].T

    scratch = [pltpu.VMEM((FIELDS, n), f32)]
    return call(kernel, [((n, FIELDS), f32)], (core, arrived, data), "fine_of", 8, 2, scratch, 1)


def in_field_order(x, core):
    n = x.shape[-1]
    x = jnp.where(core == 0, x, x[::-1])
    return x.transpose(3, 1, 0, 2).reshape(n, FIELDS)


def scale_of(tiles, listed):
    return (tiles * TILE / (SIDE * listed * TILE * TILE)) ** 0.5


def per_device(values, points0, points1, points2, tiles_a0, tiles_e1, tiles_a1, factor):
    core = lax.axis_index("k")
    col_id = lax.axis_index(COL)
    row_id = lax.axis_index(ROW)
    rows_fine, fields = values.shape
    rows_mid = points1.shape[1]
    rows_coarse = points2.shape[1]
    coarse = rows_coarse * SIDE
    share = rows_fine // SIDE
    tiles_fine, tiles_mid = rows_fine // TILE, rows_mid // TILE
    list_a0, list_e1, list_a1 = tiles_a0[0, 0], tiles_e1[0, 0], tiles_a1[0, 0]
    scale_a0 = scale_of(tiles_fine, list_a0.shape[1])
    scale_e1 = scale_of(tiles_fine, list_e1.shape[1])
    scale_a1 = scale_of(tiles_mid, list_a1.shape[1])
    scale_e2 = (1.0 / (rows_mid * SIDE)) ** 0.5

    listed_a0, listed_e1, listed_a1 = (a.shape[1] for a in (list_a0, list_e1, list_a1))

    own_e1 = in_rows(list_e1)
    lists = jnp.concatenate([in_rows(list_a0), own_e1, in_rows(list_a1)], axis=0)
    there = turned(packed(points0, points1, lists, factor))
    centres = jnp.pad(points2, ((0, 2 * BLOCK - 2), (0, 0)))
    place = jnp.stack([core, row_id, col_id]).astype(jnp.int32)
    fine_here = points0.astype(f32).reshape(2, tiles_fine, 1, TILE)
    mid_here = points1.astype(f32).reshape(2, tiles_mid, 1, TILE)
    there, vector, centres, fine_here, mid_here = lax.optimization_barrier(
        (there, values.T, centres, fine_here, mid_here)
    )
    fine_there, mid_there, lists, common = unpacked(
        there, factor, centres, tiles_fine, tiles_mid, lists.shape[0]
    )
    first_e1 = 2 * rows_of(listed_a0)
    first_a1 = first_e1 + 2 * rows_of(listed_e1)

    common = exchanged(common, YZ)
    own, other = product_a0(lists, place, fine_here, fine_there, vector, listed_a0)
    own, other, common = lax.optimization_barrier((own, other, common))
    arrived = exchanged(pair_sum(own, other), YZ)

    fine_all, common, mid_later = lax.optimization_barrier(
        (residual_of(arrived, -0.5 * scale_a0), common, mid_there)
    )
    partner = from_partner(common)

    def in_row_order(at, size):
        mine, its = common[:, at : at + size], partner[:, at : at + size]
        return jnp.stack([jnp.where(core == 0, mine, its), jnp.where(core == 0, its, mine)], axis=1)

    factor_down = in_row_order(0, rows_coarse).reshape(coarse, -1)
    factor_across = in_row_order(rows_coarse, rows_coarse).reshape(SIDE, rows_coarse, -1)
    centres = in_row_order(2 * rows_coarse, 2 * BLOCK).reshape(SIDE, 2 * BLOCK, -1)[:, :2]
    centres = centres.astype(f32).transpose(1, 0, 2)[:, :, None]
    coarse_kernel = all_pairs(centres, mid_later, support_coarse)
    fine_own, coarse_kernel, factor_down, factor_across = lax.optimization_barrier(
        (exchanged(fine_all, YZ), coarse_kernel, factor_down, factor_across)
    )
    fine_other = from_partner(fine_own)

    restricted = product(
        lists, listed_e1, first_e1, 0, fine_there, mid_here, (fine_own, fine_other), support_mid, "blocks"
    )
    mid_share, mid_all = mid_of(exchanged(restricted, COL), scale_e1)
    mid_all = exchanged(mid_all, COL)
    mid_data = turned_blocks(mid_share)

    mid_halves = (mid_all[:HALF], mid_all[HALF:])
    mid_own, mid_other = product(
        lists, listed_a1, first_a1, 1, mid_here, mid_there, mid_halves, support_mid, "halves"
    )
    arrived = exchanged(pair_sum(mid_own, mid_other), YZ)

    coarse_part = coarse_product(coarse_kernel, arrived, mid_data, scale_a1)
    coarse_data = coarse_data_of(exchanged(coarse_part, COL), fine_own, fine_other, scale_e2)
    coarse_data = exchanged(coarse_data, COL)
    halfway = exchanged(halfway_of(coarse_data, factor_down), COL)
    coarse_all = exchanged(coarse_coef_of(halfway, factor_across), COL)

    new_own = exchanged(prolong(coarse_kernel, coarse_all, mid_data, scale_e2), YZ)
    new_other = from_partner(new_own)
    fine_part = product(
        own_e1, listed_e1, 0, 1, mid_there, fine_here, (new_own, new_other), support_mid, "shares"
    )
    own_data = lax.dynamic_slice_in_dim(values, col_id * share, share, 0)
    fine_coef = fine_of(exchanged(fine_part, COL), own_data, place, scale_e1)

    both = jnp.stack([new_own, new_other]).astype(f32)
    mid_coef = in_field_order(both[..., :rows_mid], core)
    coarse_coef = lax.dynamic_slice_in_dim(both, rows_mid + core * rows_coarse, rows_coarse, 3)
    coarse_coef = in_field_order(coarse_coef, core)
    norm = coarse_data[:, 1].astype(f32).sum() / (rows_fine * SIDE * fields)
    return (fine_coef, mid_coef, coarse_coef, jnp.stack([norm]))


def solution(mesh):
    fine_mesh = Mesh(mesh.devices.reshape(4, 2, 2, 4, 4), ALL)
    return jax.shard_map(
        per_device,
        mesh=fine_mesh,
        in_specs=(
            P(ROW, None),
            P(None, ROW),
            P(None, ROW),
            P(None, ROW),
            P(ROW, COL, None, None),
            P(ROW, COL, None, None),
            P(ROW, COL, None, None),
            P(ROW, COL),
        ),
        out_specs=(P(ALL, None), P(COL, None), P(ROW, None), P()),
        check_vma=False,
    )
```

```python
import jax
import jax.numpy as jnp
from jax import lax
from jax.experimental import pallas as pl
from jax.experimental.pallas import tpu as pltpu
from jax.sharding import Mesh
from jax.sharding import PartitionSpec as P

TILE = 128
SIDE = 16
HALF = 8
LINE = 4
QUARTER = 8
BLOCK = 8
FIELDS = SIDE * BLOCK
GROUP = 16

support_fine = 0.35
support_mid = 0.55
support_coarse = 0.8

ROW = ("y", "zh", "k")
YZ = ("y", "zh")
YZL = ("y", "zh", "zl")
COL = ("x", "zl")
ALL = ROW + COL

bf16 = jnp.bfloat16
f32 = jnp.float32

VMEM = pl.BlockSpec(memory_space=pltpu.VMEM)
SMEM = pl.BlockSpec(memory_space=pltpu.SMEM)
HBM = pl.BlockSpec(memory_space=pltpu.HBM)


def room(mebibytes):
    return pltpu.CompilerParams(vmem_limit_bytes=mebibytes * 1024 * 1024)


def hint(microseconds):
    return pl.CostEstimate(
        flops=0, transcendentals=0, bytes_accessed=int(microseconds * 3.0e6)
    )


def turned(x):
    pairs = [(c * SIDE + r, r * SIDE + c) for r in range(SIDE) for c in range(SIDE)]
    return lax.ppermute(x, ALL, pairs)


def place_of_block(block, core):
    return ((block % 2) ^ core) * HALF + block // 2


def turned_blocks(x):
    pairs = [
        (c * SIDE + place_of_block(r, c % 2), r * SIDE + c) for r in range(SIDE) for c in range(SIDE)
    ]
    return lax.ppermute(x, ALL, pairs)


def from_partner(x):
    return lax.ppermute(x, "k", [(0, 1), (1, 0)])


def exchanged(x, axes):
    return lax.all_to_all(x, axes, split_axis=0, concat_axis=0, tiled=True)


def pair_sum(own, other):
    return (own.astype(f32) + from_partner(other).astype(f32)).astype(bf16)


def stretch_of(support):
    return (4.0 / support**5) ** 0.2


def wendland(left, right, support):
    across, upward = left[0] - right[0], left[1] - right[1]
    square = jnp.maximum(across * across + upward * upward, 1e-30)
    edge = support * stretch_of(support)
    margin = jnp.maximum(edge - square * lax.rsqrt(square), 0.0)
    margin2 = margin * margin
    ratio = 5.0 / edge**4
    return (margin2 * margin2 * (ratio - margin)).astype(bf16)


def at_tile(i):
    return pl.ds(pl.multiple_of(i * TILE, TILE), TILE)


def call(kernel, shapes, operands, name, mebibytes, microseconds, scratch=(), scalars=0):
    out = pl.pallas_call(
        kernel,
        out_shape=[jax.ShapeDtypeStruct(shape, kind) for shape, kind in shapes],
        in_specs=[SMEM] * scalars + [VMEM] * (len(operands) - scalars),
        out_specs=[VMEM] * len(shapes),
        scratch_shapes=list(scratch),
        compiler_params=room(mebibytes),
        cost_estimate=hint(microseconds),
        name=name,
    )(*operands)
    return out if len(shapes) > 1 else out[0]


def rows_of(listed):
    return -(-listed // TILE)


def in_rows(listing):
    rows = rows_of(listing.shape[1])
    padded = jnp.pad(listing, ((0, 0), (0, rows * TILE - listing.shape[1])))
    return padded.reshape(2 * rows, TILE)


def packed(points0, points1, lists, factor):
    fine, mid = points0.shape[1] // TILE, points1.shape[1] // TILE
    used = 2 * (fine + mid) + lists.shape[0]
    above = -(-used // SIDE) * SIDE

    def kernel(fine_ref, mid_ref, list_ref, factor_ref, out_ref):
        lines = []
        for ref, tiles in ((fine_ref, fine), (mid_ref, mid)):
            whole = ref[...].astype(f32)
            lines += [
                whole[a : a + 1, t * TILE : (t + 1) * TILE] for a in range(2) for t in range(tiles)
            ]
        lines.append(list_ref[...].astype(f32))
        if above > used:
            lines.append(jnp.zeros((above - used, TILE), f32))
        out_ref[pl.ds(0, above), :] = jnp.concatenate(lines, axis=0).astype(bf16)
        out_ref[pl.ds(above, TILE), :] = factor_ref[...]

    shapes = [((above + TILE, TILE), bf16)]
    return call(kernel, shapes, (points0, points1, lists, factor), "packed", 8, 1)


def unpacked(there, factor, local, fine, mid, listed):
    used = 2 * (fine + mid) + listed
    above = -(-used // SIDE) * SIDE
    size = 2 * TILE + local.shape[0]

    def kernel(there_ref, factor_ref, local_ref, fine_ref, mid_ref, list_ref, common_ref):
        lines = there_ref[pl.ds(0, above), :].astype(f32)
        at = 0
        for ref, tiles in ((fine_ref, fine), (mid_ref, mid)):
            for a in range(2):
                for t in range(tiles):
                    ref[a, t] = lines[at : at + 1]
                    at += 1
        list_ref[...] = lines[at : at + listed].astype(jnp.int32)
        for chip in range(HALF):
            common_ref[chip, pl.ds(0, TILE), :] = factor_ref[...]
            common_ref[chip, pl.ds(TILE, TILE), :] = there_ref[pl.ds(above, TILE), :]
            common_ref[chip, pl.ds(2 * TILE, local.shape[0]), :] = local_ref[...]

    shapes = [
        ((2, fine, 1, TILE), f32),
        ((2, mid, 1, TILE), f32),
        ((listed, TILE), jnp.int32),
        ((HALF, size, TILE), bf16),
    ]
    return call(kernel, shapes, (there, factor, local), "unpacked", 8, 1)


def set_points(left_ref, right_ref, left, right, support):
    stretch = stretch_of(support)
    for axis in range(2):
        for t in range(left.shape[1]):
            row = left_ref[axis, t] * stretch
            left[axis, t] = jnp.broadcast_to(row, (TILE, TILE)).T
        for t in range(right.shape[1]):
            right[axis, t] = right_ref[axis, t] * stretch


def point_scratch(left, right):
    return [pltpu.VMEM((2, left, TILE, TILE), f32), pltpu.VMEM((2, right, 1, TILE), f32)]


def add_tiles(list_ref, listed, first, contracted, left, right, vector, total, support):
    rows = rows_of(listed)
    steps = TILE // GROUP
    line_j = first + contracted * rows
    line_i = first + (1 - contracted) * rows

    def step(g, carry):
        row, lane = g // steps, g % steps * GROUP
        products = []
        for u in range(GROUP):
            j = list_ref[line_j + row, lane + u]
            i = list_ref[line_i + row, lane + u]
            tile = wendland((left[0, j], left[1, j]), (right[0, i], right[1, i]), support)
            product = jnp.dot(vector[:, at_tile(j)], tile, preferred_element_type=f32)
            products.append((i, product))
        for i, product in products:
            total[i] += product
        return carry

    lax.fori_loop(0, listed // GROUP, step, 0)


def product_a0(lists, place, left, right, vector, listed):
    tiles = right.shape[1]

    def kernel(
        list_ref, place_ref, left_ref, right_ref, vector_ref, own_ref, other_ref, left, right, total
    ):
        set_points(left_ref, right_ref, left, right, support_fine)
        me = place_ref[0]
        weight = jnp.where(place_ref[1] == place_ref[2], -2.0 / scale_of(tiles, listed), 0.0)
        for i in range(tiles):
            at = pl.ds(i * TILE, TILE)
            total[i] = vector_ref[:, at].astype(f32) * weight
        add_tiles(list_ref, listed, 0, 1, left, right, vector_ref, total, support_fine)
        for half in range(HALF):
            for i in range(tiles):
                at = pl.ds(i * TILE, TILE)
                own = pl.ds(pl.multiple_of((2 * half + me) * BLOCK, BLOCK), BLOCK)
                other = pl.ds(pl.multiple_of((2 * half + 1 - me) * BLOCK, BLOCK), BLOCK)
                own_ref[half, :, at] = total[i, own, :].astype(bf16)
                other_ref[half, :, at] = total[i, other, :].astype(bf16)

    half = ((HALF, BLOCK, tiles * TILE), bf16)
    scratch = [*point_scratch(left.shape[1], tiles), pltpu.VMEM((tiles, FIELDS, TILE), f32)]
    operands = (lists, place, left, right, vector)
    return call(kernel, [half, half], operands, "product_a0", 16, 20, scratch, 2)


def product(lists, listed, first, contracted, left, right, halves, support, tail=None):
    tiles = right.shape[1]
    length = left.shape[1] * TILE
    size = tiles * TILE

    def kernel(list_ref, left_ref, right_ref, own_ref, other_ref, *rest):
        *given, left, right, vector, total = rest
        set_points(left_ref, right_ref, left, right, support)
        total[...] = jnp.zeros_like(total)
        for ref, at in ((own_ref, 0), (other_ref, FIELDS // 2)):
            rows = ref[:, :, pl.ds(0, length)].reshape(FIELDS // 2, length)
            vector[pl.ds(at, FIELDS // 2), :] = rows
        add_tiles(list_ref, listed, first, contracted, left, right, vector, total, support)
        for i in range(tiles):
            low = total[i].astype(bf16)
            at = pl.ds(i * TILE, TILE)
            if tail is not None:
                given[1][:, :, at] = low.reshape(SIDE, BLOCK, TILE)
            else:
                pair = low.reshape(2, HALF, BLOCK, TILE)
                given[0][:, :, at] = pair[0]
                given[1][:, :, at] = pair[1]
        if tail is not None:
            for peer in range(SIDE):
                given[1][peer, :, pl.ds(size, TILE)] = given[0][...]

    scratch = [
        *point_scratch(left.shape[1], tiles),
        pltpu.VMEM((FIELDS, length), bf16),
        pltpu.VMEM((tiles, FIELDS, TILE), f32),
    ]
    operands = (lists, left, right, *halves)
    if tail is not None:
        shapes = [((SIDE, BLOCK, size + TILE), bf16)]
        operands = (*operands, tail)
    else:
        shapes = [((HALF, BLOCK, size), bf16)] * 2
    return call(kernel, shapes, operands, "product", 16, listed / 18, scratch, 1)


def quarter_of(lists, place, blocks, rows):
    listed, tiles = rows
    lines = rows_of(LINE * QUARTER * tiles)
    held = rows_of(listed)

    def kernel(list_ref, place_ref, out_ref):
        zl = place_ref[3]

        def put(at, i, j):
            out_ref[at // TILE, at % TILE] = i
            out_ref[lines + at // TILE, at % TILE] = j

        count = jnp.int32(0)
        for block in range(blocks):

            def step(t, count):
                for u in range(GROUP):
                    e = t * GROUP + u
                    i = list_ref[block * 2 * held + e // TILE, e % TILE]
                    j = list_ref[block * 2 * held + held + e // TILE, e % TILE]
                    put(count, i // (2 * LINE) * 2 + i % 2, block * tiles + j)
                    count = count + (i // 2 % LINE == zl).astype(jnp.int32)
                return count

            count = lax.fori_loop(0, listed // GROUP, step, count)
        for u in range(GROUP):
            put(count + u, jnp.int32(QUARTER), jnp.int32(0))
        out_ref[2 * lines, 0] = (count + GROUP - 1) // GROUP

    lines = lines + 1
    return pl.pallas_call(
        kernel,
        out_shape=jax.ShapeDtypeStruct((2 * lines + 1, TILE), jnp.int32),
        in_specs=[SMEM, SMEM],
        out_specs=SMEM,
        compiler_params=room(4),
        cost_estimate=hint(7),
        name="quarter_of",
    )(lists, place)


def product_quarter(lists, left, right, own, other, support):
    lines = (lists.shape[0] - 1) // 2
    tiles = right.shape[1]
    length = left.shape[1] * TILE // LINE
    steps = TILE // GROUP

    def kernel(list_ref, left_ref, right_ref, own_ref, other_ref, out_ref, left, right, vector, total):
        set_points(left_ref, right_ref, left, right, support)
        total[...] = jnp.zeros_like(total)
        for ref, first in ((own_ref, 0), (other_ref, FIELDS // 2)):
            for chip in range(HALF):
                for zl in range(LINE):
                    at = pl.ds(first + chip * BLOCK, BLOCK)
                    part = ref[chip * LINE + zl, :, pl.ds(0, length)]
                    vector[at, pl.ds(zl * length, length)] = part

        def step(g, carry):
            row, lane = g // steps, g % steps * GROUP
            products = []
            for u in range(GROUP):
                i = list_ref[row, lane + u]
                j = list_ref[lines + row, lane + u]
                tile = wendland((left[0, j], left[1, j]), (right[0, i], right[1, i]), support)
                product = jnp.dot(vector[:, at_tile(j)], tile, preferred_element_type=f32)
                products.append((i, product))
            for i, product in products:
                total[i] += product
            return carry

        lax.fori_loop(0, list_ref[2 * lines, 0], step, 0)
        for i in range(QUARTER):
            out_ref[i // 2, :, pl.ds(i % 2 * TILE, TILE)] = total[i].astype(bf16)

    scratch = [
        *point_scratch(left.shape[1], tiles),
        pltpu.VMEM((FIELDS, length * LINE), bf16),
        pltpu.VMEM((tiles, FIELDS, TILE), f32),
    ]
    operands = (lists, left, right, own, other)
    shapes = [((QUARTER // 2, FIELDS, 2 * TILE), bf16)]
    return call(kernel, shapes, operands, "product_quarter", 20, 10, scratch, 1)


def all_pairs(left, right, support):
    rows, cols = left.shape[1], right.shape[1]

    def kernel(left_ref, right_ref, out_ref):
        stretch = stretch_of(support)
        ys = [jnp.broadcast_to(left_ref[a, 0] * stretch, (TILE, TILE)).T for a in range(2)]
        for j in range(cols):
            out_ref[:, pl.ds(j * TILE, TILE)] = wendland(
                ys, (right_ref[0, j] * stretch, right_ref[1, j] * stretch), support
            )

    return pl.pallas_call(
        kernel,
        out_shape=jax.ShapeDtypeStruct((rows * TILE, cols * TILE), bf16),
        grid=(rows,),
        in_specs=[pl.BlockSpec((2, 1, 1, TILE), lambda i: (0, i, 0, 0)), VMEM],
        out_specs=pl.BlockSpec((TILE, cols * TILE), lambda i: (i, 0)),
        compiler_params=room(8),
        cost_estimate=hint(6),
        name="all_pairs",
    )(left, right)


def residual_of(arrived, scale):
    chips, _, n = arrived.shape

    def kernel(arrived_ref, out_ref):
        squares = jnp.zeros((1, TILE), f32)
        for t in range(n // TILE):
            at = pl.ds(t * TILE, TILE)
            part = scale * arrived_ref[:, :, at].astype(f32).sum(axis=0)
            squares += jnp.sum(part * part, axis=0, keepdims=True)
            low = part.astype(bf16)
            for chip in range(chips):
                out_ref[chip, :, at] = low
        tail = three_rows(squares)
        for chip in range(chips):
            out_ref[chip, :, pl.ds(n, TILE)] = tail

    return call(kernel, [((chips, BLOCK, n + TILE), bf16)], (arrived,), "residual_of", 8, 1)


def three_rows(x):
    high = x.astype(bf16).astype(f32)
    rest = x - high
    middle = rest.astype(bf16).astype(f32)
    rows = [high, middle, rest - middle, jnp.zeros((BLOCK - 3, TILE), f32)]
    return jnp.concatenate(rows, axis=0).astype(bf16)


def mid_of(arrived, scale):
    peers, _, n = arrived.shape
    n = n - TILE

    def kernel(arrived_ref, out_ref, low_ref):
        part = scale * arrived_ref[:, :, pl.ds(0, n)].astype(f32).sum(axis=0)
        out_ref[...] = part
        low = part.astype(bf16)
        for peer in range(peers):
            low_ref[peer] = low

    shapes = [((BLOCK, n), f32), ((peers, BLOCK, n), bf16)]
    return call(kernel, shapes, (arrived,), "mid_of", 8, 1)


def chunks_of(matrix_ref, held, sems):
    chunks = sems.shape[0]
    size = matrix_ref.shape[0] // chunks
    rows = [pl.ds(q * size, size) for q in range(chunks)]
    return [
        pltpu.make_async_copy(matrix_ref.at[r], held.at[r], sems.at[q]) for q, r in enumerate(rows)
    ]


def call_on_matrix(kernel, shape, kind, matrix, operands, name, scratch):
    chunks = 4
    return pl.pallas_call(
        kernel,
        out_shape=jax.ShapeDtypeStruct(shape, kind),
        in_specs=[HBM] + [VMEM] * len(operands),
        out_specs=VMEM,
        scratch_shapes=[
            pltpu.VMEM(matrix.shape, bf16),
            pltpu.SemaphoreType.DMA((chunks,)),
            *scratch,
        ],
        compiler_params=room(12),
        cost_estimate=hint(3),
        name=name,
    )(pltpu.with_memory_space_constraint(matrix, pltpu.HBM), *operands)


def coarse_product(matrix, arrived, mid_data, scale):
    rows, cols = matrix.shape

    def kernel(matrix_ref, arrived_ref, mid_ref, out_ref, held, sems, turned_ref):
        copies = chunks_of(matrix_ref, held, sems)
        for copy in copies:
            copy.start()
        whole = (scale * arrived_ref[...].astype(f32).sum(axis=0)).astype(bf16).astype(f32)
        whole = mid_ref[...] - 0.5 * whole
        for t in range(cols // TILE):
            lines = whole[:, t * TILE : (t + 1) * TILE]
            full = jnp.concatenate([lines, jnp.zeros((TILE - BLOCK, TILE), f32)], axis=0)
            turned_ref[pl.ds(t * TILE, TILE), :] = full.T.astype(bf16)
        each = rows // TILE // len(copies)
        for c, copy in enumerate(copies):
            copy.wait()
            for q in range(c * each, (c + 1) * each):
                part = jnp.dot(
                    held[pl.ds(q * TILE, TILE), :], turned_ref[...], preferred_element_type=f32
                )
                out_ref[q] = part.T[:BLOCK, :]

    shape = (rows // TILE, BLOCK, TILE)
    scratch = [pltpu.VMEM((cols, TILE), bf16)]
    operands = (arrived, mid_data)
    return call_on_matrix(kernel, shape, f32, matrix, operands, "coarse_product", scratch)


def coarse_data_of(arrived, own, other, scale):
    peers = arrived.shape[0]
    n = own.shape[2] - TILE

    def kernel(arrived_ref, own_ref, other_ref, out_ref):
        data = (scale * arrived_ref[...].sum(axis=0)).astype(bf16)
        squares = jnp.zeros((1, TILE), f32)
        for ref in (own_ref, other_ref):
            tails = ref[...].astype(f32).sum(axis=0)
            squares += jnp.sum(tails, axis=0, keepdims=True)
        tail = three_rows(squares)
        for peer in range(peers):
            out_ref[peer, 0] = data
            out_ref[peer, 1] = tail

    tails = (own[:, :, n:], other[:, :, n:])
    shapes = [((peers, 2, BLOCK, TILE), bf16)]
    return call(kernel, shapes, (arrived, *tails), "coarse_data_of", 8, 1)


def halfway_of(gathered_data, factor_down):
    peers = gathered_data.shape[0]

    def kernel(data_ref, factor_ref, out_ref):
        total = jnp.zeros((BLOCK, TILE), f32)
        for q in range(peers // 2):
            pair = jnp.concatenate([data_ref[2 * q, 0], data_ref[2 * q + 1, 0]], axis=1)
            rows = factor_ref[pl.ds(q * 2 * TILE, 2 * TILE), :]
            total += jnp.dot(pair, rows, preferred_element_type=f32)
        low = total.astype(bf16)
        for peer in range(peers):
            out_ref[peer] = low

    shapes = [((peers, BLOCK, TILE), bf16)]
    return call(kernel, shapes, (gathered_data, factor_down), "halfway_of", 8, 1)


def coarse_coef_of(halfway, factor_across):
    peers = halfway.shape[0]

    def kernel(half_ref, factor_ref, out_ref):
        total = jnp.zeros((BLOCK, TILE), f32)
        for q in range(peers):
            total += lax.dot_general(
                half_ref[q], factor_ref[q], (((1,), (1,)), ((), ())), preferred_element_type=f32
            )
        for peer in range(peers):
            out_ref[peer] = total

    shapes = [((peers, BLOCK, TILE), f32)]
    return call(kernel, shapes, (halfway, factor_across), "coarse_coef_of", 8, 1)


def prolong(matrix, coarse_coef, place, mid_data, scale):
    rows, cols = matrix.shape
    two = 2 * TILE

    def kernel(matrix_ref, coef_ref, low_ref, mid_ref, out_ref, held, sems):
        copies = chunks_of(matrix_ref, held, sems)
        for copy in copies:
            copy.start()
        for chip in range(HALF):
            for zl in range(LINE):
                out_ref[chip * LINE + zl, :, pl.ds(cols, TILE)] = low_ref[chip]
        total = jnp.zeros((BLOCK, cols), f32)
        each = rows // two // len(copies)
        for c, copy in enumerate(copies):
            copy.wait()
            for q in range(c * each, (c + 1) * each):
                pair = jnp.concatenate([coef_ref[2 * q], coef_ref[2 * q + 1]], axis=1)
                total += jnp.dot(
                    pair.astype(bf16), held[pl.ds(q * two, two), :], preferred_element_type=f32
                )
        low = (0.5 * mid_ref[...] + scale * total).astype(bf16)
        for chip in range(HALF * LINE):
            out_ref[chip, :, pl.ds(0, cols)] = low

    sent = coarse_coef.reshape(HALF, 2, BLOCK, TILE).astype(bf16)
    sent = jnp.where(place[3] % 2 == 0, sent[:, 0], sent[:, 1])
    shape = (HALF * LINE, BLOCK, cols + TILE)
    operands = (coarse_coef, sent, mid_data)
    return call_on_matrix(kernel, shape, bf16, matrix, operands, "prolong", ())


def fine_of(arrived, data, core, scale):
    n = arrived.shape[2]

    def kernel(core_ref, arrived_ref, data_ref, out_ref, summed):
        me = core_ref[0]
        summed[...] = arrived_ref[...].astype(f32).sum(axis=0)
        rows = []
        for block in range(SIDE):
            at = ((block % 2) ^ me) * HALF + block // 2
            rows.append(summed[pl.ds(pl.multiple_of(at * BLOCK, BLOCK), BLOCK), :])
        whole = jnp.concatenate(rows, axis=0)
        for t in range(n // TILE):
            at = pl.ds(t * TILE, TILE)
            data = data_ref[at, :].astype(f32)
            out_ref[at, :] = 0.5 * data + scale * whole[:, t * TILE : (t + 1) * TILE].T

    scratch = [pltpu.VMEM((FIELDS, n), f32)]
    return call(kernel, [((n, FIELDS), f32)], (core, arrived, data), "fine_of", 8, 2, scratch, 1)


def in_field_order(x, core):
    n = x.shape[-1]
    x = jnp.where(core == 0, x, x[::-1])
    return x.transpose(3, 1, 0, 2).reshape(n, FIELDS)


def scale_of(tiles, listed):
    return (tiles * TILE / (SIDE * listed * TILE * TILE)) ** 0.5


def per_device(values, points0, points1, points2, tiles_a0, tiles_e1, tiles_a1, factor):
    core = lax.axis_index("k")
    col_id = lax.axis_index(COL)
    row_id = lax.axis_index(ROW)
    rows_fine, fields = values.shape
    rows_mid = points1.shape[1]
    rows_coarse = points2.shape[1]
    coarse = rows_coarse * SIDE
    share = rows_fine // SIDE
    tiles_fine, tiles_mid = rows_fine // TILE, rows_mid // TILE
    list_a0, list_e1, list_a1 = tiles_a0[0, 0], tiles_e1[0, 0], tiles_a1[0, 0]
    scale_a0 = scale_of(tiles_fine, list_a0.shape[1])
    scale_e1 = scale_of(tiles_fine, list_e1.shape[1])
    scale_a1 = scale_of(tiles_mid, list_a1.shape[1])
    scale_e2 = (1.0 / (rows_mid * SIDE)) ** 0.5

    listed_a0, listed_e1, listed_a1 = (a.shape[1] for a in (list_a0, list_e1, list_a1))

    own_e1 = in_rows(list_e1)
    lists = jnp.concatenate([in_rows(list_a0), own_e1, in_rows(list_a1)], axis=0)
    there = turned(packed(points0, points1, lists, factor))
    local = [points2, jnp.zeros((SIDE - 2, TILE), bf16), points1.reshape(2 * tiles_mid, TILE)]
    local = jnp.concatenate(local, axis=0)
    x_id, zl_id = lax.axis_index("x"), lax.axis_index("zl")
    place = jnp.stack([core, row_id, col_id, zl_id]).astype(jnp.int32)
    fine_here = points0.astype(f32).reshape(2, tiles_fine, 1, TILE)
    mid_here = points1.astype(f32).reshape(2, tiles_mid, 1, TILE)
    tail = jnp.pad(own_e1, ((0, BLOCK - own_e1.shape[0]), (0, 0))).astype(bf16)
    there, vector, local, fine_here, mid_here, tail = lax.optimization_barrier(
        (there, values.T, local, fine_here, mid_here, tail)
    )
    fine_there, mid_there, lists, common = unpacked(
        there, factor, local, tiles_fine, tiles_mid, lists.shape[0]
    )
    first_e1 = 2 * rows_of(listed_a0)
    first_a1 = first_e1 + 2 * rows_of(listed_e1)

    common = exchanged(common, YZ)
    own, other = product_a0(lists, place, fine_here, fine_there, vector, listed_a0)
    own, other, common = lax.optimization_barrier((own, other, common))
    arrived = exchanged(pair_sum(own, other), YZ)

    fine_all, common, mid_later, fine_later = lax.optimization_barrier(
        (residual_of(arrived, -0.5 * scale_a0), common, mid_there, fine_here)
    )
    partner = from_partner(common)

    def in_row_order(at, size):
        mine, its = common[:, at : at + size], partner[:, at : at + size]
        return jnp.stack([jnp.where(core == 0, mine, its), jnp.where(core == 0, its, mine)], axis=1)

    factor_down = in_row_order(0, rows_coarse).reshape(coarse, -1)
    factor_across = in_row_order(rows_coarse, rows_coarse).reshape(SIDE, rows_coarse, -1)
    centres = in_row_order(2 * rows_coarse, SIDE).reshape(SIDE, SIDE, -1)[:, :2]
    centres = centres.astype(f32).transpose(1, 0, 2)[:, :, None]
    mid_line = in_row_order(2 * rows_coarse + SIDE, 2 * tiles_mid)
    mid_line = mid_line.reshape(SIDE, 2, tiles_mid, 1, TILE)
    mid_line = lax.dynamic_slice_in_dim(mid_line, x_id * LINE, LINE, 0).astype(f32)
    mid_line = mid_line.transpose(1, 0, 2, 3, 4).reshape(2, LINE * tiles_mid, 1, TILE)
    fine_quarter = fine_later.reshape(2, QUARTER // 2, LINE, 2, 1, TILE)
    fine_quarter = lax.dynamic_index_in_dim(fine_quarter, zl_id, 2, keepdims=False)
    fine_quarter = fine_quarter.reshape(2, QUARTER, 1, TILE)
    fine_quarter = jnp.pad(fine_quarter, ((0, 0), (0, 1), (0, 0), (0, 0)), constant_values=8.0)
    coarse_kernel = all_pairs(centres, mid_later, support_coarse)
    fine_own, coarse_kernel, factor_down, factor_across, mid_line, fine_quarter = (
        lax.optimization_barrier(
            (exchanged(fine_all, YZ), coarse_kernel, factor_down, factor_across, mid_line, fine_quarter)
        )
    )
    fine_other = from_partner(fine_own)

    restricted = product(
        lists, listed_e1, first_e1, 0, fine_there, mid_here, (fine_own, fine_other), support_mid, tail
    )
    restricted = exchanged(restricted, COL)
    mid_share, mid_all = mid_of(restricted, scale_e1)
    line_lists = lax.dynamic_slice_in_dim(restricted[:, :, rows_mid:], x_id * LINE, LINE, 0)
    line_lists = line_lists[:, : own_e1.shape[0]].reshape(-1, TILE).astype(jnp.int32)
    line_lists = quarter_of(line_lists, place, LINE, (listed_e1, tiles_mid))
    mid_all, mid_data, line_lists = lax.optimization_barrier(
        (exchanged(mid_all, COL), turned_blocks(mid_share), line_lists)
    )

    mid_halves = (mid_all[:HALF], mid_all[HALF:])
    mid_own, mid_other = product(
        lists, listed_a1, first_a1, 1, mid_here, mid_there, mid_halves, support_mid
    )
    arrived = exchanged(pair_sum(mid_own, mid_other), YZ)

    coarse_part = coarse_product(coarse_kernel, arrived, mid_data, scale_a1)
    coarse_data = coarse_data_of(exchanged(coarse_part, COL), fine_own, fine_other, scale_e2)
    coarse_data = exchanged(coarse_data, COL)
    halfway = exchanged(halfway_of(coarse_data, factor_down), COL)
    coarse_all = exchanged(coarse_coef_of(halfway, factor_across), COL)

    new_own = exchanged(prolong(coarse_kernel, coarse_all, place, mid_data, scale_e2), YZL)
    new_other = from_partner(new_own)
    fine_part = product_quarter(
        line_lists, mid_line, fine_quarter, new_own, new_other, support_mid
    )
    own_data = lax.dynamic_slice_in_dim(values, col_id * share, share, 0)
    fine_coef = fine_of(exchanged(fine_part, "x"), own_data, place, scale_e1)

    def from_line(zl, at, size):
        both = jnp.stack([new_own, new_other])[..., at : at + size]
        both = both.reshape(2, HALF, LINE, BLOCK, size)
        both = lax.dynamic_index_in_dim(both, zl, 2, keepdims=False)
        return in_field_order(both.astype(f32), core)

    mid_coef = from_line(zl_id, 0, rows_mid)
    coarse_coef = from_line(core, rows_mid, rows_coarse)
    norm = coarse_data[:, 1].astype(f32).sum() / (rows_fine * SIDE * fields)
    return (fine_coef, mid_coef, coarse_coef, jnp.stack([norm]))


def solution(mesh):
    fine_mesh = Mesh(mesh.devices.reshape(4, 2, 2, 4, 4), ALL)
    return jax.shard_map(
        per_device,
        mesh=fine_mesh,
        in_specs=(
            P(ROW, None),
            P(None, ROW),
            P(None, ROW),
            P(None, ROW),
            P(ROW, COL, None, None),
            P(ROW, COL, None, None),
            P(ROW, COL, None, None),
            P(ROW, COL),
        ),
        out_specs=(P(ALL, None), P(COL, None), P(ROW, None), P()),
        check_vma=False,
    )
```

```python
import jax
import jax.numpy as jnp
from jax import lax
from jax.experimental import pallas as pl
from jax.experimental.pallas import tpu as pltpu
from jax.sharding import Mesh
from jax.sharding import PartitionSpec as P

TILE = 128
SIDE = 16
HALF = 8
LINE = 4
QUARTER = 8
BLOCK = 8
FIELDS = SIDE * BLOCK
GROUP = 16

support_fine = 0.35
support_mid = 0.55
support_coarse = 0.8

ROW = ("y", "zh", "k")
YZ = ("y", "zh")
YZL = ("y", "zh", "zl")
COL = ("x", "zl")
ALL = ROW + COL

bf16 = jnp.bfloat16
f32 = jnp.float32

VMEM = pl.BlockSpec(memory_space=pltpu.VMEM)
SMEM = pl.BlockSpec(memory_space=pltpu.SMEM)
HBM = pl.BlockSpec(memory_space=pltpu.HBM)


def room(mebibytes):
    return pltpu.CompilerParams(vmem_limit_bytes=mebibytes * 1024 * 1024)


def hint(microseconds):
    return pl.CostEstimate(
        flops=0, transcendentals=0, bytes_accessed=int(microseconds * 3.0e6)
    )


def turned(x):
    pairs = [(c * SIDE + r, r * SIDE + c) for r in range(SIDE) for c in range(SIDE)]
    return lax.ppermute(x, ALL, pairs)


def place_of_block(block, core):
    return ((block % 2) ^ core) * HALF + block // 2


def turned_blocks(x):
    pairs = [
        (c * SIDE + place_of_block(r, c % 2), r * SIDE + c) for r in range(SIDE) for c in range(SIDE)
    ]
    return lax.ppermute(x, ALL, pairs)


def from_partner(x):
    return lax.ppermute(x, "k", [(0, 1), (1, 0)])


def exchanged(x, axes):
    return lax.all_to_all(x, axes, split_axis=0, concat_axis=0, tiled=True)


def pair_sum(own, other):
    return (own.astype(f32) + from_partner(other).astype(f32)).astype(bf16)


def stretch_of(support):
    return (4.0 / support**5) ** 0.2


def wendland(left, right, support):
    across, upward = left[0] - right[0], left[1] - right[1]
    square = jnp.maximum(across * across + upward * upward, 1e-30)
    edge = support * stretch_of(support)
    margin = jnp.maximum(edge - square * lax.rsqrt(square), 0.0)
    margin2 = margin * margin
    ratio = 5.0 / edge**4
    return (margin2 * margin2 * (ratio - margin)).astype(bf16)


def at_tile(i):
    return pl.ds(pl.multiple_of(i * TILE, TILE), TILE)


def call(kernel, shapes, operands, name, mebibytes, microseconds, scratch=(), scalars=0):
    out = pl.pallas_call(
        kernel,
        out_shape=[jax.ShapeDtypeStruct(shape, kind) for shape, kind in shapes],
        in_specs=[SMEM] * scalars + [VMEM] * (len(operands) - scalars),
        out_specs=[VMEM] * len(shapes),
        scratch_shapes=list(scratch),
        compiler_params=room(mebibytes),
        cost_estimate=hint(microseconds),
        name=name,
    )(*operands)
    return out if len(shapes) > 1 else out[0]


def rows_of(listed):
    return -(-listed // TILE)


def in_rows(listing):
    rows = rows_of(listing.shape[1])
    padded = jnp.pad(listing, ((0, 0), (0, rows * TILE - listing.shape[1])))
    return padded.reshape(2 * rows, TILE)


def packed(points0, points1, lists, factor):
    fine, mid = points0.shape[1] // TILE, points1.shape[1] // TILE
    used = 2 * (fine + mid) + sum(2 * rows_of(a.shape[1]) for a in lists)
    above = -(-used // SIDE) * SIDE

    def kernel(fine_ref, mid_ref, *rest):
        *list_refs, factor_ref, out_ref = rest
        lines = []
        for ref in (fine_ref, mid_ref, *list_refs):
            whole = ref[...].astype(f32)
            length = whole.shape[1]
            short = -length % TILE
            if short:
                whole = jnp.concatenate([whole, jnp.zeros((2, short), f32)], axis=1)
            for a in range(2):
                lines += [whole[a : a + 1, t : t + TILE] for t in range(0, length, TILE)]
        if above > used:
            lines.append(jnp.zeros((above - used, TILE), f32))
        out_ref[pl.ds(0, above), :] = jnp.concatenate(lines, axis=0).astype(bf16)
        out_ref[pl.ds(above, TILE), :] = factor_ref[...]

    shapes = [((above + TILE, TILE), bf16)]
    return call(kernel, shapes, (points0, points1, *lists, factor), "packed", 8, 1)


def unpacked(there, factor, local, fine, mid, listed):
    used = 2 * (fine + mid) + listed
    above = -(-used // SIDE) * SIDE
    size = 2 * TILE + local.shape[0]

    def kernel(there_ref, factor_ref, local_ref, fine_ref, mid_ref, list_ref, common_ref):
        lines = there_ref[pl.ds(0, above), :].astype(f32)
        at = 0
        for ref, tiles in ((fine_ref, fine), (mid_ref, mid)):
            for a in range(2):
                for t in range(tiles):
                    ref[a, t] = lines[at : at + 1]
                    at += 1
        list_ref[...] = lines[at : at + listed].astype(jnp.int32)
        for chip in range(HALF):
            common_ref[chip, pl.ds(0, TILE), :] = factor_ref[...]
            common_ref[chip, pl.ds(TILE, TILE), :] = there_ref[pl.ds(above, TILE), :]
            common_ref[chip, pl.ds(2 * TILE, local.shape[0]), :] = local_ref[...]

    shapes = [
        ((2, fine, 1, TILE), f32),
        ((2, mid, 1, TILE), f32),
        ((listed, TILE), jnp.int32),
        ((HALF, size, TILE), bf16),
    ]
    return call(kernel, shapes, (there, factor, local), "unpacked", 8, 1)


def in_row_order(place, common, partner, mid):
    at_centres, at_mid = 2 * TILE, 2 * TILE + SIDE

    def kernel(place_ref, own_ref, other_ref, down_ref, across_ref, centre_ref, line_ref):
        core, x = place_ref[0], place_ref[4]

        def rows(chip, of_core, at, size):
            own, other = own_ref[chip, pl.ds(at, size), :], other_ref[chip, pl.ds(at, size), :]
            return jnp.where(core == of_core, own.astype(f32), other.astype(f32))

        for block in range(SIDE):
            chip, of_core = block // 2, block % 2
            down_ref[pl.ds(block * TILE, TILE), :] = rows(chip, of_core, 0, TILE).astype(bf16)
            across_ref[block] = rows(chip, of_core, TILE, TILE).astype(bf16)
            lines = rows(chip, of_core, at_centres, SIDE)
            for a in range(2):
                centre_ref[a, block] = lines[a : a + 1]
        for q in range(LINE):
            lines = rows(x * (LINE // 2) + q // 2, q % 2, at_mid, 2 * mid)
            for a in range(2):
                for t in range(mid):
                    line_ref[a, q * mid + t] = lines[a * mid + t : a * mid + t + 1]

    shapes = [
        ((SIDE * TILE, TILE), bf16),
        ((SIDE, TILE, TILE), bf16),
        ((2, SIDE, 1, TILE), f32),
        ((2, LINE * mid, 1, TILE), f32),
    ]
    return call(kernel, shapes, (place, common, partner), "in_row_order", 8, 2, (), 1)


def set_points(left_ref, right_ref, left, right, support):
    stretch = stretch_of(support)
    for axis in range(2):
        for t in range(left.shape[1]):
            row = left_ref[axis, t] * stretch
            left[axis, t] = jnp.broadcast_to(row, (TILE, TILE)).T
        for t in range(right.shape[1]):
            right[axis, t] = right_ref[axis, t] * stretch


def point_scratch(left, right):
    return [pltpu.VMEM((2, left, TILE, TILE), f32), pltpu.VMEM((2, right, 1, TILE), f32)]


def add_tiles(list_ref, listed, first, contracted, left, right, vector, total, support):
    rows = rows_of(listed)
    group = 2 * GROUP
    steps = TILE // group
    line_j = first + contracted * rows
    line_i = first + (1 - contracted) * rows

    def step(g, carry):
        row, lane = g // steps, g % steps * group
        products = []
        for u in range(group):
            j = list_ref[line_j + row, lane + u]
            i = list_ref[line_i + row, lane + u]
            tile = wendland((left[0, j], left[1, j]), (right[0, i], right[1, i]), support)
            product = jnp.dot(vector[:, at_tile(j)], tile, preferred_element_type=f32)
            products.append((i, product))
        for i, product in products:
            total[i] += product
        return carry

    lax.fori_loop(0, listed // group, step, 0)


def product_a0(lists, place, left, right, vector, listed):
    tiles = right.shape[1]

    def kernel(
        list_ref, place_ref, left_ref, right_ref, vector_ref, own_ref, other_ref, left, right, total
    ):
        set_points(left_ref, right_ref, left, right, support_fine)
        me = place_ref[0]
        weight = jnp.where(place_ref[1] == place_ref[2], -2.0 / scale_of(tiles, listed), 0.0)
        for i in range(tiles):
            at = pl.ds(i * TILE, TILE)
            total[i] = vector_ref[:, at].astype(f32) * weight
        add_tiles(list_ref, listed, 0, 1, left, right, vector_ref, total, support_fine)
        for half in range(HALF):
            for i in range(tiles):
                at = pl.ds(i * TILE, TILE)
                own = pl.ds(pl.multiple_of((2 * half + me) * BLOCK, BLOCK), BLOCK)
                other = pl.ds(pl.multiple_of((2 * half + 1 - me) * BLOCK, BLOCK), BLOCK)
                own_ref[half, :, at] = total[i, own, :].astype(bf16)
                other_ref[half, :, at] = total[i, other, :].astype(bf16)

    half = ((HALF, BLOCK, tiles * TILE), bf16)
    scratch = [*point_scratch(left.shape[1], tiles), pltpu.VMEM((tiles, FIELDS, TILE), f32)]
    operands = (lists, place, left, right, vector)
    return call(kernel, [half, half], operands, "product_a0", 16, 20, scratch, 2)


def product(lists, listed, first, contracted, left, right, halves, support, tail=None):
    tiles = right.shape[1]
    length = left.shape[1] * TILE
    size = tiles * TILE

    def kernel(list_ref, left_ref, right_ref, own_ref, other_ref, *rest):
        *given, left, right, vector, total = rest
        set_points(left_ref, right_ref, left, right, support)
        total[...] = jnp.zeros_like(total)
        for ref, at in ((own_ref, 0), (other_ref, FIELDS // 2)):
            rows = ref[:, :, pl.ds(0, length)].reshape(FIELDS // 2, length)
            vector[pl.ds(at, FIELDS // 2), :] = rows
        add_tiles(list_ref, listed, first, contracted, left, right, vector, total, support)
        for i in range(tiles):
            low = total[i].astype(bf16)
            at = pl.ds(i * TILE, TILE)
            if tail is not None:
                given[1][:, :, at] = low.reshape(SIDE, BLOCK, TILE)
            else:
                pair = low.reshape(2, HALF, BLOCK, TILE)
                given[0][:, :, at] = pair[0]
                given[1][:, :, at] = pair[1]
        if tail is not None:
            for peer in range(SIDE):
                given[1][peer, :, pl.ds(size, TILE)] = given[0][...]

    scratch = [
        *point_scratch(left.shape[1], tiles),
        pltpu.VMEM((FIELDS, length), bf16),
        pltpu.VMEM((tiles, FIELDS, TILE), f32),
    ]
    operands = (lists, left, right, *halves)
    if tail is not None:
        shapes = [((SIDE, BLOCK, size + TILE), bf16)]
        operands = (*operands, tail)
    else:
        shapes = [((HALF, BLOCK, size), bf16)] * 2
    return call(kernel, shapes, operands, "product", 16, listed / 18, scratch, 1)


def quarter_of(lists, place, blocks, listed, tiles):
    held = rows_of(listed)
    size = rows_of(LINE * QUARTER * tiles) * TILE

    def kernel(place_ref, list_ref, out_ref):
        zl = place_ref[3]
        row = lax.broadcasted_iota(jnp.int32, (TILE, TILE), 0)
        col = lax.broadcasted_iota(jnp.int32, (TILE, TILE), 1)
        before = (row < col).astype(bf16)
        slot = lax.broadcasted_iota(jnp.int32, (size, TILE), 0).astype(f32)
        lane = lax.broadcasted_iota(jnp.int32, (1, TILE), 1)
        count = jnp.zeros((1, 1), f32)
        total = jnp.zeros((BLOCK, size), f32)
        for block in range(blocks):
            for part in range(held):
                at = block * 2 * held + part
                i = list_ref[at : at + 1, :]
                j = list_ref[at + held : at + held + 1, :] + block * tiles
                real = jnp.where(lane + part * TILE < listed, 1.0, 0.0)
                flag = jnp.where(((i >> 1) & (LINE - 1)) == zl, real, 0.0)
                rank = count + jnp.dot(
                    jnp.broadcast_to(flag, (BLOCK, TILE)).astype(bf16),
                    before,
                    preferred_element_type=f32,
                )[:1]
                here = jnp.where(slot == jnp.where(flag > 0.5, rank, -1.0), 1.0, 0.0).astype(bf16)
                lines = [((i >> 3) * 2 + (i & 1)).astype(f32), j.astype(f32)]
                lines.append(jnp.zeros((BLOCK - 2, TILE), f32))
                lines = jnp.concatenate(lines, axis=0).astype(bf16)
                total += lax.dot_general(
                    lines, here, (((1,), (1,)), ((), ())), preferred_element_type=f32
                )
                count += jnp.sum(flag, axis=1, keepdims=True)
        slots = lax.broadcasted_iota(jnp.int32, (1, size), 1).astype(f32)
        out_ref[0:1, :] = jnp.where(slots < count, total[0:1], float(QUARTER)).astype(jnp.int32)
        out_ref[1:2, :] = total[1:2].astype(jnp.int32)
        groups = ((count + (GROUP - 1)) * (1.0 / GROUP)).astype(jnp.int32)
        out_ref[2:3, :] = jnp.broadcast_to(groups, (1, size))
        out_ref[3:, :] = jnp.zeros((BLOCK - 3, size), jnp.int32)

    shapes = [((BLOCK, size), jnp.int32)]
    return call(kernel, shapes, (place, lists), "quarter_of", 8, 3, (), 1)


def product_quarter(lists, left, right, own, other, support):
    tiles = right.shape[1]
    length = left.shape[1] * TILE // LINE

    def kernel(list_ref, left_ref, right_ref, own_ref, other_ref, out_ref, left, right, vector, total):
        set_points(left_ref, right_ref, left, right, support)
        total[...] = jnp.zeros_like(total)
        for ref, first in ((own_ref, 0), (other_ref, FIELDS // 2)):
            for chip in range(HALF):
                for zl in range(LINE):
                    at = pl.ds(first + chip * BLOCK, BLOCK)
                    part = ref[chip * LINE + zl, :, pl.ds(0, length)]
                    vector[at, pl.ds(zl * length, length)] = part

        def step(g, carry):
            products = []
            for u in range(GROUP):
                i = list_ref[0, g * GROUP + u]
                j = list_ref[1, g * GROUP + u]
                tile = wendland((left[0, j], left[1, j]), (right[0, i], right[1, i]), support)
                product = jnp.dot(vector[:, at_tile(j)], tile, preferred_element_type=f32)
                products.append((i, product))
            for i, product in products:
                total[i] += product
            return carry

        lax.fori_loop(0, list_ref[2, 0], step, 0)
        for i in range(QUARTER):
            out_ref[i // 2, :, pl.ds(i % 2 * TILE, TILE)] = total[i].astype(bf16)

    scratch = [
        *point_scratch(left.shape[1], tiles),
        pltpu.VMEM((FIELDS, length * LINE), bf16),
        pltpu.VMEM((tiles, FIELDS, TILE), f32),
    ]
    operands = (lists, left, right, own, other)
    shapes = [((QUARTER // 2, FIELDS, 2 * TILE), bf16)]
    return call(kernel, shapes, operands, "product_quarter", 20, 10, scratch, 1)


def all_pairs(left, right, support):
    rows, cols = left.shape[1], right.shape[1]

    def kernel(left_ref, right_ref, out_ref):
        stretch = stretch_of(support)
        ys = [jnp.broadcast_to(left_ref[a, 0] * stretch, (TILE, TILE)).T for a in range(2)]
        for j in range(cols):
            out_ref[:, pl.ds(j * TILE, TILE)] = wendland(
                ys, (right_ref[0, j] * stretch, right_ref[1, j] * stretch), support
            )

    return pl.pallas_call(
        kernel,
        out_shape=jax.ShapeDtypeStruct((rows * TILE, cols * TILE), bf16),
        grid=(rows,),
        in_specs=[pl.BlockSpec((2, 1, 1, TILE), lambda i: (0, i, 0, 0)), VMEM],
        out_specs=pl.BlockSpec((TILE, cols * TILE), lambda i: (i, 0)),
        compiler_params=room(8),
        cost_estimate=hint(6),
        name="all_pairs",
    )(left, right)


def sum_of(arrived):
    _, rows, n = arrived.shape

    def kernel(arrived_ref, out_ref):
        for t in range(0, n, 4 * TILE):
            at = pl.ds(t, 4 * TILE)
            out_ref[:, at] = arrived_ref[:, :, at].astype(f32).sum(axis=0).astype(bf16)

    return call(kernel, [((rows, n), bf16)], (arrived,), "sum_of", 8, 1)


def residual_of(here, there, scale):
    rows, n = here.shape

    def kernel(here_ref, there_ref, out_ref):
        squares = jnp.zeros((1, TILE), f32)
        for t in range(n // TILE):
            at = pl.ds(t * TILE, TILE)
            part = scale * (here_ref[:, at].astype(f32) + there_ref[:, at].astype(f32))
            squares += jnp.sum(part * part, axis=0, keepdims=True)
            low = part.astype(bf16)
            for chip in range(LINE):
                out_ref[chip, :, at] = low
        tail = three_rows(squares)
        for chip in range(LINE):
            out_ref[chip, pl.ds(0, BLOCK), pl.ds(n, TILE)] = tail
            out_ref[chip, pl.ds(BLOCK, BLOCK), pl.ds(n, TILE)] = jnp.zeros_like(tail)

    shapes = [((LINE, rows, n + TILE), bf16)]
    return call(kernel, shapes, (here, there), "residual_of", 8, 1)


def three_rows(x):
    high = x.astype(bf16).astype(f32)
    rest = x - high
    middle = rest.astype(bf16).astype(f32)
    rows = [high, middle, rest - middle, jnp.zeros((BLOCK - 3, TILE), f32)]
    return jnp.concatenate(rows, axis=0).astype(bf16)


def mid_of(arrived, scale):
    peers, _, n = arrived.shape
    n = n - TILE

    def kernel(arrived_ref, out_ref, low_ref):
        part = scale * arrived_ref[:, :, pl.ds(0, n)].astype(f32).sum(axis=0)
        out_ref[...] = part
        low = part.astype(bf16)
        for peer in range(peers):
            low_ref[peer] = low

    shapes = [((BLOCK, n), f32), ((peers, BLOCK, n), bf16)]
    return call(kernel, shapes, (arrived,), "mid_of", 8, 1)


def chunks_of(matrix_ref, held, sems):
    chunks = sems.shape[0]
    size = matrix_ref.shape[0] // chunks
    rows = [pl.ds(q * size, size) for q in range(chunks)]
    return [
        pltpu.make_async_copy(matrix_ref.at[r], held.at[r], sems.at[q]) for q, r in enumerate(rows)
    ]


def call_on_matrix(kernel, shape, kind, matrix, operands, name, scratch):
    chunks = 4
    return pl.pallas_call(
        kernel,
        out_shape=jax.ShapeDtypeStruct(shape, kind),
        in_specs=[HBM] + [VMEM] * len(operands),
        out_specs=VMEM,
        scratch_shapes=[
            pltpu.VMEM(matrix.shape, bf16),
            pltpu.SemaphoreType.DMA((chunks,)),
            *scratch,
        ],
        compiler_params=room(12),
        cost_estimate=hint(3),
        name=name,
    )(pltpu.with_memory_space_constraint(matrix, pltpu.HBM), *operands)


def coarse_product(matrix, arrived, mid_data, scale):
    rows, cols = matrix.shape

    def kernel(matrix_ref, arrived_ref, mid_ref, out_ref, held, sems, turned_ref):
        copies = chunks_of(matrix_ref, held, sems)
        for copy in copies:
            copy.start()
        whole = (scale * arrived_ref[...].astype(f32).sum(axis=0)).astype(bf16).astype(f32)
        whole = mid_ref[...] - 0.5 * whole
        for t in range(cols // TILE):
            lines = whole[:, t * TILE : (t + 1) * TILE]
            full = jnp.concatenate([lines, jnp.zeros((TILE - BLOCK, TILE), f32)], axis=0)
            turned_ref[pl.ds(t * TILE, TILE), :] = full.T.astype(bf16)
        each = rows // TILE // len(copies)
        for c, copy in enumerate(copies):
            copy.wait()
            for q in range(c * each, (c + 1) * each):
                part = jnp.dot(
                    held[pl.ds(q * TILE, TILE), :], turned_ref[...], preferred_element_type=f32
                )
                out_ref[q] = part.T[:BLOCK, :]

    shape = (rows // TILE, BLOCK, TILE)
    scratch = [pltpu.VMEM((cols, TILE), bf16)]
    operands = (arrived, mid_data)
    return call_on_matrix(kernel, shape, f32, matrix, operands, "coarse_product", scratch)


def coarse_data_of(arrived, own, other, scale):
    peers = arrived.shape[0]
    n = own.shape[2] - TILE

    def kernel(arrived_ref, own_ref, other_ref, out_ref):
        data = (scale * arrived_ref[...].sum(axis=0)).astype(bf16)
        squares = jnp.zeros((1, TILE), f32)
        for ref in (own_ref, other_ref):
            tails = ref[...].astype(f32).sum(axis=0)
            squares += jnp.sum(tails, axis=0, keepdims=True)
        tail = three_rows(squares)
        for peer in range(peers):
            out_ref[peer, 0] = data
            out_ref[peer, 1] = tail

    tails = (own[:, :, n:], other[:, :, n:])
    shapes = [((peers, 2, BLOCK, TILE), bf16)]
    return call(kernel, shapes, (arrived, *tails), "coarse_data_of", 8, 1)


def halfway_of(gathered_data, factor_down):
    peers = gathered_data.shape[0]

    def kernel(data_ref, factor_ref, out_ref):
        total = jnp.zeros((BLOCK, TILE), f32)
        for q in range(peers // 2):
            pair = jnp.concatenate([data_ref[2 * q, 0], data_ref[2 * q + 1, 0]], axis=1)
            rows = factor_ref[pl.ds(q * 2 * TILE, 2 * TILE), :]
            total += jnp.dot(pair, rows, preferred_element_type=f32)
        low = total.astype(bf16)
        for peer in range(peers):
            out_ref[peer] = low

    shapes = [((peers, BLOCK, TILE), bf16)]
    return call(kernel, shapes, (gathered_data, factor_down), "halfway_of", 8, 1)


def coarse_coef_of(halfway, factor_across):
    peers = halfway.shape[0]

    def kernel(half_ref, factor_ref, out_ref):
        total = jnp.zeros((BLOCK, TILE), f32)
        for q in range(peers):
            total += lax.dot_general(
                half_ref[q], factor_ref[q], (((1,), (1,)), ((), ())), preferred_element_type=f32
            )
        for peer in range(peers):
            out_ref[peer] = total

    shapes = [((peers, BLOCK, TILE), f32)]
    return call(kernel, shapes, (halfway, factor_across), "coarse_coef_of", 8, 1)


def prolong(matrix, coarse_coef, place, mid_data, scale):
    rows, cols = matrix.shape
    two = 2 * TILE

    def kernel(matrix_ref, coef_ref, low_ref, mid_ref, out_ref, held, sems):
        copies = chunks_of(matrix_ref, held, sems)
        for copy in copies:
            copy.start()
        for chip in range(HALF):
            for zl in range(LINE):
                out_ref[chip * LINE + zl, :, pl.ds(cols, TILE)] = low_ref[chip]
        total = jnp.zeros((BLOCK, cols), f32)
        each = rows // two // len(copies)
        for c, copy in enumerate(copies):
            copy.wait()
            for q in range(c * each, (c + 1) * each):
                pair = jnp.concatenate([coef_ref[2 * q], coef_ref[2 * q + 1]], axis=1)
                total += jnp.dot(
                    pair.astype(bf16), held[pl.ds(q * two, two), :], preferred_element_type=f32
                )
        low = (0.5 * mid_ref[...] + scale * total).astype(bf16)
        for chip in range(HALF * LINE):
            out_ref[chip, :, pl.ds(0, cols)] = low

    sent = coarse_coef.reshape(HALF, 2, BLOCK, TILE).astype(bf16)
    sent = jnp.where(place[3] % 2 == 0, sent[:, 0], sent[:, 1])
    shape = (HALF * LINE, BLOCK, cols + TILE)
    operands = (coarse_coef, sent, mid_data)
    return call_on_matrix(kernel, shape, bf16, matrix, operands, "prolong", ())


def fine_of(arrived, data, core, scale):
    n = arrived.shape[2]

    def kernel(core_ref, arrived_ref, data_ref, out_ref, summed):
        me = core_ref[0]
        summed[...] = arrived_ref[...].astype(f32).sum(axis=0)
        rows = []
        for block in range(SIDE):
            at = ((block % 2) ^ me) * HALF + block // 2
            rows.append(summed[pl.ds(pl.multiple_of(at * BLOCK, BLOCK), BLOCK), :])
        whole = jnp.concatenate(rows, axis=0)
        for t in range(n // TILE):
            at = pl.ds(t * TILE, TILE)
            data = data_ref[at, :].astype(f32)
            out_ref[at, :] = 0.5 * data + scale * whole[:, t * TILE : (t + 1) * TILE].T

    scratch = [pltpu.VMEM((FIELDS, n), f32)]
    return call(kernel, [((n, FIELDS), f32)], (core, arrived, data), "fine_of", 8, 2, scratch, 1)


def in_field_order(x, core):
    n = x.shape[-1]
    x = jnp.where(core == 0, x, x[::-1])
    return x.transpose(3, 1, 0, 2).reshape(n, FIELDS)


def scale_of(tiles, listed):
    return (tiles * TILE / (SIDE * listed * TILE * TILE)) ** 0.5


def per_device(values, points0, points1, points2, tiles_a0, tiles_e1, tiles_a1, factor):
    core = lax.axis_index("k")
    col_id = lax.axis_index(COL)
    row_id = lax.axis_index(ROW)
    rows_fine, fields = values.shape
    rows_mid = points1.shape[1]
    rows_coarse = points2.shape[1]
    coarse = rows_coarse * SIDE
    share = rows_fine // SIDE
    tiles_fine, tiles_mid = rows_fine // TILE, rows_mid // TILE
    list_a0, list_e1, list_a1 = tiles_a0[0, 0], tiles_e1[0, 0], tiles_a1[0, 0]
    scale_a0 = scale_of(tiles_fine, list_a0.shape[1])
    scale_e1 = scale_of(tiles_fine, list_e1.shape[1])
    scale_a1 = scale_of(tiles_mid, list_a1.shape[1])
    scale_e2 = (1.0 / (rows_mid * SIDE)) ** 0.5

    listed_a0, listed_e1, listed_a1 = (a.shape[1] for a in (list_a0, list_e1, list_a1))

    first_e1 = 2 * rows_of(listed_a0)
    first_a1 = first_e1 + 2 * rows_of(listed_e1)

    own_e1 = in_rows(list_e1)
    there = turned(packed(points0, points1, (list_a0, list_e1, list_a1), factor))
    local = [points2, jnp.zeros((SIDE - 2, TILE), bf16), points1.reshape(2 * tiles_mid, TILE)]
    local = jnp.concatenate(local, axis=0)
    x_id, zl_id = lax.axis_index("x"), lax.axis_index("zl")
    place = jnp.stack([core, row_id, col_id, zl_id, x_id]).astype(jnp.int32)
    fine_here = points0.astype(f32).reshape(2, tiles_fine, 1, TILE)
    mid_here = points1.astype(f32).reshape(2, tiles_mid, 1, TILE)
    tail = jnp.pad(own_e1, ((0, BLOCK - own_e1.shape[0]), (0, 0))).astype(bf16)
    there, vector, local, fine_here, mid_here, tail = lax.optimization_barrier(
        (there, values.T, local, fine_here, mid_here, tail)
    )
    fine_there, mid_there, lists, common = unpacked(
        there, factor, local, tiles_fine, tiles_mid, first_a1 + 2 * rows_of(listed_a1)
    )

    common = exchanged(common, YZ)
    own, other = product_a0(lists, place, fine_here, fine_there, vector, listed_a0)
    own, other, common = lax.optimization_barrier((own, other, common))
    pair = pair_sum(own, other).reshape(LINE, 2 * BLOCK, rows_fine)
    arrived = exchanged(pair, "y")

    common, pair = lax.optimization_barrier((common, pair))
    ordered = in_row_order(place, common, from_partner(common), tiles_mid)
    arrived, ordered = lax.optimization_barrier((arrived, ordered))
    factor_down, factor_across, centres, mid_line = ordered
    summed = sum_of(arrived)
    centres, mid_later, fine_later, summed = lax.optimization_barrier(
        (centres, mid_there, fine_here, summed)
    )
    swapped = lax.ppermute(summed, "zh", [(0, 1), (1, 0)])
    coarse_kernel = all_pairs(centres, mid_later, support_coarse)
    swapped, coarse_kernel, fine_later = lax.optimization_barrier(
        (swapped, coarse_kernel, fine_later)
    )
    fine_own = exchanged(residual_of(summed, swapped, -0.5 * scale_a0), "y")
    fine_quarter = fine_later.reshape(2, QUARTER // 2, LINE, 2, 1, TILE)
    fine_quarter = lax.dynamic_index_in_dim(fine_quarter, zl_id, 2, keepdims=False)
    fine_quarter = fine_quarter.reshape(2, QUARTER, 1, TILE)
    fine_quarter = jnp.pad(fine_quarter, ((0, 0), (0, 1), (0, 0), (0, 0)), constant_values=8.0)
    fine_own, fine_quarter = lax.optimization_barrier((fine_own, fine_quarter))
    fine_own = fine_own.reshape(HALF, BLOCK, rows_fine + TILE)
    fine_other = from_partner(fine_own)

    restricted = product(
        lists, listed_e1, first_e1, 0, fine_there, mid_here, (fine_own, fine_other), support_mid, tail
    )
    restricted = exchanged(restricted, COL)
    mid_share, mid_all = mid_of(restricted, scale_e1)
    line_lists = lax.dynamic_slice_in_dim(restricted[:, :, rows_mid:], x_id * LINE, LINE, 0)
    line_lists = line_lists[:, : own_e1.shape[0]].reshape(-1, TILE).astype(jnp.int32)
    line_lists = quarter_of(line_lists, place, LINE, listed_e1, tiles_mid)
    mid_all, mid_data, line_lists = lax.optimization_barrier(
        (exchanged(mid_all, COL), turned_blocks(mid_share), line_lists)
    )

    mid_halves = (mid_all[:HALF], mid_all[HALF:])
    mid_own, mid_other = product(
        lists, listed_a1, first_a1, 1, mid_here, mid_there, mid_halves, support_mid
    )
    arrived = exchanged(pair_sum(mid_own, mid_other), YZ)

    coarse_part = coarse_product(coarse_kernel, arrived, mid_data, scale_a1)
    coarse_data = coarse_data_of(exchanged(coarse_part, COL), fine_own, fine_other, scale_e2)
    coarse_data = exchanged(coarse_data, COL)
    halfway = exchanged(halfway_of(coarse_data, factor_down), COL)
    coarse_all = exchanged(coarse_coef_of(halfway, factor_across), COL)

    new_own = exchanged(prolong(coarse_kernel, coarse_all, place, mid_data, scale_e2), YZL)
    new_other = from_partner(new_own)
    fine_part = product_quarter(
        line_lists, mid_line, fine_quarter, new_own, new_other, support_mid
    )
    own_data = lax.dynamic_slice_in_dim(values, col_id * share, share, 0)
    fine_coef = fine_of(exchanged(fine_part, "x"), own_data, place, scale_e1)

    def from_line(zl, at, size):
        both = jnp.stack([new_own, new_other])[..., at : at + size]
        both = both.reshape(2, HALF, LINE, BLOCK, size)
        both = lax.dynamic_index_in_dim(both, zl, 2, keepdims=False)
        return in_field_order(both.astype(f32), core)

    mid_coef = from_line(zl_id, 0, rows_mid)
    coarse_coef = from_line(core, rows_mid, rows_coarse)
    norm = coarse_data[:, 1].astype(f32).sum() / (rows_fine * SIDE * fields)
    return (fine_coef, mid_coef, coarse_coef, jnp.stack([norm]))


def solution(mesh):
    fine_mesh = Mesh(mesh.devices.reshape(4, 2, 2, 4, 4), ALL)
    return jax.shard_map(
        per_device,
        mesh=fine_mesh,
        in_specs=(
            P(ROW, None),
            P(None, ROW),
            P(None, ROW),
            P(None, ROW),
            P(ROW, COL, None, None),
            P(ROW, COL, None, None),
            P(ROW, COL, None, None),
            P(ROW, COL),
        ),
        out_specs=(P(ALL, None), P(COL, None), P(ROW, None), P()),
        check_vma=False,
    )
```

```python
import jax
import jax.numpy as jnp
from jax import lax
from jax.experimental import pallas as pl
from jax.experimental.pallas import tpu as pltpu
from jax.sharding import Mesh
from jax.sharding import PartitionSpec as P

TILE = 128
SIDE = 16
HALF = 8
LINE = 4
QUARTER = 8
BLOCK = 8
FIELDS = SIDE * BLOCK
GROUP = 16

support_fine = 0.35
support_mid = 0.55
support_coarse = 0.8

ROW = ("y", "zh", "k")
YZ = ("y", "zh")
YZL = ("y", "zh", "zl")
COL = ("x", "zl")
ALL = ROW + COL

bf16 = jnp.bfloat16
f32 = jnp.float32

VMEM = pl.BlockSpec(memory_space=pltpu.VMEM)
SMEM = pl.BlockSpec(memory_space=pltpu.SMEM)
HBM = pl.BlockSpec(memory_space=pltpu.HBM)


def room(mebibytes):
    return pltpu.CompilerParams(vmem_limit_bytes=mebibytes * 1024 * 1024)


def hint(microseconds):
    return pl.CostEstimate(
        flops=0, transcendentals=0, bytes_accessed=int(microseconds * 3.0e6)
    )


def turned(x):
    pairs = [(c * SIDE + r, r * SIDE + c) for r in range(SIDE) for c in range(SIDE)]
    return lax.ppermute(x, ALL, pairs)


def place_of_block(block, core):
    return ((block % 2) ^ core) * HALF + block // 2


def turned_blocks(x):
    pairs = [
        (c * SIDE + place_of_block(r, c % 2), r * SIDE + c) for r in range(SIDE) for c in range(SIDE)
    ]
    return lax.ppermute(x, ALL, pairs)


def from_partner(x):
    return lax.ppermute(x, "k", [(0, 1), (1, 0)])


def exchanged(x, axes):
    return lax.all_to_all(x, axes, split_axis=0, concat_axis=0, tiled=True)


def pair_sum(own, other):
    return (own.astype(f32) + from_partner(other).astype(f32)).astype(bf16)


def stretch_of(support):
    return (4.0 / support**5) ** 0.2


def wendland(left, right, support):
    across, upward = left[0] - right[0], left[1] - right[1]
    square = jnp.maximum(across * across + upward * upward, 1e-30)
    edge = support * stretch_of(support)
    margin = jnp.maximum(edge - square * lax.rsqrt(square), 0.0)
    margin2 = margin * margin
    ratio = 5.0 / edge**4
    return (margin2 * margin2 * (ratio - margin)).astype(bf16)


def at_tile(i):
    return pl.ds(pl.multiple_of(i * TILE, TILE), TILE)


def call(kernel, shapes, operands, name, mebibytes, microseconds, scratch=(), scalars=0):
    out = pl.pallas_call(
        kernel,
        out_shape=[jax.ShapeDtypeStruct(shape, kind) for shape, kind in shapes],
        in_specs=[SMEM] * scalars + [VMEM] * (len(operands) - scalars),
        out_specs=[VMEM] * len(shapes),
        scratch_shapes=list(scratch),
        compiler_params=room(mebibytes),
        cost_estimate=hint(microseconds),
        name=name,
    )(*operands)
    return out if len(shapes) > 1 else out[0]


def rows_of(listed):
    return -(-listed // TILE)


def in_rows(listing):
    rows = rows_of(listing.shape[1])
    padded = jnp.pad(listing, ((0, 0), (0, rows * TILE - listing.shape[1])))
    return padded.reshape(2 * rows, TILE)


def packed(points0, points1, lists, factor):
    fine, mid = points0.shape[1] // TILE, points1.shape[1] // TILE
    used = 2 * (fine + mid) + sum(2 * rows_of(a.shape[1]) for a in lists)
    above = -(-used // SIDE) * SIDE

    operands = (points0, points1, *lists, factor)
    count = len(operands)

    def kernel(*refs):
        given, out_ref, held, sems = refs[:count], refs[count], refs[count + 1 : -1], refs[-1]
        copies = [
            pltpu.make_async_copy(ref, to, sems.at[n]) for n, (ref, to) in enumerate(zip(given, held))
        ]
        for copy in copies:
            copy.start()
        for copy in copies:
            copy.wait()
        lines = []
        for ref in held[:-1]:
            whole = ref[...].astype(f32)
            length = whole.shape[1]
            short = -length % TILE
            if short:
                whole = jnp.concatenate([whole, jnp.zeros((2, short), f32)], axis=1)
            for a in range(2):
                lines += [whole[a : a + 1, t : t + TILE] for t in range(0, length, TILE)]
        if above > used:
            lines.append(jnp.zeros((above - used, TILE), f32))
        out_ref[pl.ds(0, above), :] = jnp.concatenate(lines, axis=0).astype(bf16)
        out_ref[pl.ds(above, TILE), :] = held[-1][...]

    return pl.pallas_call(
        kernel,
        out_shape=jax.ShapeDtypeStruct((above + TILE, TILE), bf16),
        in_specs=[HBM] * count,
        out_specs=VMEM,
        scratch_shapes=[pltpu.VMEM(a.shape, a.dtype) for a in operands]
        + [pltpu.SemaphoreType.DMA((count,))],
        compiler_params=room(8),
        cost_estimate=hint(1),
        name="packed",
    )(*(pltpu.with_memory_space_constraint(a, pltpu.HBM) for a in operands))


def unpacked(there, factor, local, fine, mid, listed):
    used = 2 * (fine + mid) + listed
    above = -(-used // SIDE) * SIDE
    size = 2 * TILE + local.shape[0]

    def kernel(there_ref, factor_ref, local_ref, fine_ref, mid_ref, list_ref, common_ref):
        lines = there_ref[pl.ds(0, above), :].astype(f32)
        at = 0
        for ref, tiles in ((fine_ref, fine), (mid_ref, mid)):
            for a in range(2):
                for t in range(tiles):
                    ref[a, t] = lines[at : at + 1]
                    at += 1
        list_ref[...] = lines[at : at + listed].astype(jnp.int32)
        for chip in range(HALF):
            common_ref[chip, pl.ds(0, TILE), :] = factor_ref[...]
            common_ref[chip, pl.ds(TILE, TILE), :] = there_ref[pl.ds(above, TILE), :]
            common_ref[chip, pl.ds(2 * TILE, local.shape[0]), :] = local_ref[...]

    shapes = [
        ((2, fine, 1, TILE), f32),
        ((2, mid, 1, TILE), f32),
        ((listed, TILE), jnp.int32),
        ((HALF, size, TILE), bf16),
    ]
    return call(kernel, shapes, (there, factor, local), "unpacked", 8, 1)


def in_row_order(place, common, partner, mid):
    at_centres, at_mid = 2 * TILE, 2 * TILE + SIDE

    def kernel(place_ref, own_ref, other_ref, down_ref, across_ref, centre_ref, line_ref):
        core, x = place_ref[0], place_ref[4]

        def rows(chip, of_core, at, size):
            own, other = own_ref[chip, pl.ds(at, size), :], other_ref[chip, pl.ds(at, size), :]
            return jnp.where(core == of_core, own.astype(f32), other.astype(f32))

        for block in range(SIDE):
            chip, of_core = block // 2, block % 2
            down_ref[pl.ds(block * TILE, TILE), :] = rows(chip, of_core, 0, TILE).astype(bf16)
            across_ref[block] = rows(chip, of_core, TILE, TILE).astype(bf16)
            lines = rows(chip, of_core, at_centres, SIDE)
            for a in range(2):
                centre_ref[a, block] = lines[a : a + 1]
        for q in range(LINE):
            lines = rows(x * (LINE // 2) + q // 2, q % 2, at_mid, 2 * mid)
            for a in range(2):
                for t in range(mid):
                    line_ref[a, q * mid + t] = lines[a * mid + t : a * mid + t + 1]

    shapes = [
        ((SIDE * TILE, TILE), bf16),
        ((SIDE, TILE, TILE), bf16),
        ((2, SIDE, 1, TILE), f32),
        ((2, LINE * mid, 1, TILE), f32),
    ]
    return call(kernel, shapes, (place, common, partner), "in_row_order", 8, 2, (), 1)


def set_points(left_ref, right_ref, left, right, support):
    stretch = stretch_of(support)
    for axis in range(2):
        for t in range(left.shape[1]):
            row = left_ref[axis, t] * stretch
            left[axis, t] = jnp.broadcast_to(row, (TILE, TILE)).T
        for t in range(right.shape[1]):
            right[axis, t] = right_ref[axis, t] * stretch


def point_scratch(left, right):
    return [pltpu.VMEM((2, left, TILE, TILE), f32), pltpu.VMEM((2, right, 1, TILE), f32)]


def add_tiles(list_ref, listed, first, contracted, left, right, vector, total, support):
    rows = rows_of(listed)
    group = 2 * GROUP
    steps = TILE // group
    line_j = first + contracted * rows
    line_i = first + (1 - contracted) * rows

    def step(g, carry):
        row, lane = g // steps, g % steps * group
        products = []
        for u in range(group):
            j = list_ref[line_j + row, lane + u]
            i = list_ref[line_i + row, lane + u]
            tile = wendland((left[0, j], left[1, j]), (right[0, i], right[1, i]), support)
            product = jnp.dot(vector[:, at_tile(j)], tile, preferred_element_type=f32)
            products.append((i, product))
        for i, product in products:
            total[i] += product
        return carry

    lax.fori_loop(0, listed // group, step, 0)


def product_a0(lists, place, left, right, vector, listed):
    tiles = right.shape[1]

    def kernel(
        list_ref, place_ref, left_ref, right_ref, vector_ref, own_ref, other_ref, left, right, total
    ):
        set_points(left_ref, right_ref, left, right, support_fine)
        me = place_ref[0]
        weight = jnp.where(place_ref[1] == place_ref[2], -2.0 / scale_of(tiles, listed), 0.0)
        for i in range(tiles):
            at = pl.ds(i * TILE, TILE)
            total[i] = vector_ref[:, at].astype(f32) * weight
        add_tiles(list_ref, listed, 0, 1, left, right, vector_ref, total, support_fine)
        for half in range(HALF):
            for i in range(tiles):
                at = pl.ds(i * TILE, TILE)
                own = pl.ds(pl.multiple_of((2 * half + me) * BLOCK, BLOCK), BLOCK)
                other = pl.ds(pl.multiple_of((2 * half + 1 - me) * BLOCK, BLOCK), BLOCK)
                own_ref[half, :, at] = total[i, own, :].astype(bf16)
                other_ref[half, :, at] = total[i, other, :].astype(bf16)

    half = ((HALF, BLOCK, tiles * TILE), bf16)
    scratch = [*point_scratch(left.shape[1], tiles), pltpu.VMEM((tiles, FIELDS, TILE), f32)]
    operands = (lists, place, left, right, vector)
    return call(kernel, [half, half], operands, "product_a0", 16, 20, scratch, 2)


def product(lists, listed, first, contracted, left, right, halves, support, tail=None):
    tiles = right.shape[1]
    length = left.shape[1] * TILE
    size = tiles * TILE

    def kernel(list_ref, left_ref, right_ref, own_ref, other_ref, *rest):
        *given, left, right, vector, total = rest
        set_points(left_ref, right_ref, left, right, support)
        total[...] = jnp.zeros_like(total)
        for ref, at in ((own_ref, 0), (other_ref, FIELDS // 2)):
            rows = ref[:, :, pl.ds(0, length)].reshape(FIELDS // 2, length)
            vector[pl.ds(at, FIELDS // 2), :] = rows
        add_tiles(list_ref, listed, first, contracted, left, right, vector, total, support)
        for i in range(tiles):
            low = total[i].astype(bf16)
            at = pl.ds(i * TILE, TILE)
            if tail is not None:
                given[1][:, :, at] = low.reshape(SIDE, BLOCK, TILE)
            else:
                pair = low.reshape(2, HALF, BLOCK, TILE)
                given[0][:, :, at] = pair[0]
                given[1][:, :, at] = pair[1]
        if tail is not None:
            for peer in range(SIDE):
                given[1][peer, :, pl.ds(size, TILE)] = given[0][...]

    scratch = [
        *point_scratch(left.shape[1], tiles),
        pltpu.VMEM((FIELDS, length), bf16),
        pltpu.VMEM((tiles, FIELDS, TILE), f32),
    ]
    operands = (lists, left, right, *halves)
    if tail is not None:
        shapes = [((SIDE, BLOCK, size + TILE), bf16)]
        operands = (*operands, tail)
    else:
        shapes = [((HALF, BLOCK, size), bf16)] * 2
    return call(kernel, shapes, operands, "product", 16, listed / 18, scratch, 1)


def quarter_of(lists, place, blocks, listed, tiles):
    held = rows_of(listed)
    size = rows_of(LINE * QUARTER * tiles) * TILE

    def kernel(place_ref, list_ref, out_ref):
        zl = place_ref[3]
        row = lax.broadcasted_iota(jnp.int32, (TILE, TILE), 0)
        col = lax.broadcasted_iota(jnp.int32, (TILE, TILE), 1)
        before = (row < col).astype(bf16)
        slot = lax.broadcasted_iota(jnp.int32, (size, TILE), 0).astype(f32)
        lane = lax.broadcasted_iota(jnp.int32, (1, TILE), 1)
        count = jnp.zeros((1, 1), f32)
        total = jnp.zeros((BLOCK, size), f32)
        for block in range(blocks):
            for part in range(held):
                at = block * 2 * held + part
                i = list_ref[at : at + 1, :]
                j = list_ref[at + held : at + held + 1, :] + block * tiles
                real = jnp.where(lane + part * TILE < listed, 1.0, 0.0)
                flag = jnp.where(((i >> 1) & (LINE - 1)) == zl, real, 0.0)
                rank = count + jnp.dot(
                    jnp.broadcast_to(flag, (BLOCK, TILE)).astype(bf16),
                    before,
                    preferred_element_type=f32,
                )[:1]
                here = jnp.where(slot == jnp.where(flag > 0.5, rank, -1.0), 1.0, 0.0).astype(bf16)
                lines = [((i >> 3) * 2 + (i & 1)).astype(f32), j.astype(f32)]
                lines.append(jnp.zeros((BLOCK - 2, TILE), f32))
                lines = jnp.concatenate(lines, axis=0).astype(bf16)
                total += lax.dot_general(
                    lines, here, (((1,), (1,)), ((), ())), preferred_element_type=f32
                )
                count += jnp.sum(flag, axis=1, keepdims=True)
        slots = lax.broadcasted_iota(jnp.int32, (1, size), 1).astype(f32)
        out_ref[0:1, :] = jnp.where(slots < count, total[0:1], float(QUARTER)).astype(jnp.int32)
        out_ref[1:2, :] = total[1:2].astype(jnp.int32)
        groups = ((count + (GROUP - 1)) * (1.0 / GROUP)).astype(jnp.int32)
        out_ref[2:3, :] = jnp.broadcast_to(groups, (1, size))
        out_ref[3:, :] = jnp.zeros((BLOCK - 3, size), jnp.int32)

    shapes = [((BLOCK, size), jnp.int32)]
    return call(kernel, shapes, (place, lists), "quarter_of", 8, 3, (), 1)


def product_quarter(lists, left, right, own, other, support):
    tiles = right.shape[1]
    length = left.shape[1] * TILE // LINE

    def kernel(list_ref, left_ref, right_ref, own_ref, other_ref, out_ref, left, right, vector, total):
        set_points(left_ref, right_ref, left, right, support)
        total[...] = jnp.zeros_like(total)
        for ref, first in ((own_ref, 0), (other_ref, FIELDS // 2)):
            for chip in range(HALF):
                for zl in range(LINE):
                    at = pl.ds(first + chip * BLOCK, BLOCK)
                    part = ref[chip * LINE + zl, :, pl.ds(0, length)]
                    vector[at, pl.ds(zl * length, length)] = part

        def step(g, carry):
            products = []
            for u in range(GROUP):
                i = list_ref[0, g * GROUP + u]
                j = list_ref[1, g * GROUP + u]
                tile = wendland((left[0, j], left[1, j]), (right[0, i], right[1, i]), support)
                product = jnp.dot(vector[:, at_tile(j)], tile, preferred_element_type=f32)
                products.append((i, product))
            for i, product in products:
                total[i] += product
            return carry

        lax.fori_loop(0, list_ref[2, 0], step, 0)
        for i in range(QUARTER):
            out_ref[i // 2, :, pl.ds(i % 2 * TILE, TILE)] = total[i].astype(bf16)

    scratch = [
        *point_scratch(left.shape[1], tiles),
        pltpu.VMEM((FIELDS, length * LINE), bf16),
        pltpu.VMEM((tiles, FIELDS, TILE), f32),
    ]
    operands = (lists, left, right, own, other)
    shapes = [((QUARTER // 2, FIELDS, 2 * TILE), bf16)]
    return call(kernel, shapes, operands, "product_quarter", 20, 10, scratch, 1)


def all_pairs(left, right, support):
    rows, cols = left.shape[1], right.shape[1]

    def kernel(left_ref, right_ref, out_ref):
        stretch = stretch_of(support)
        ys = [jnp.broadcast_to(left_ref[a, 0] * stretch, (TILE, TILE)).T for a in range(2)]
        for j in range(cols):
            out_ref[:, pl.ds(j * TILE, TILE)] = wendland(
                ys, (right_ref[0, j] * stretch, right_ref[1, j] * stretch), support
            )

    return pl.pallas_call(
        kernel,
        out_shape=pltpu.HBM((rows * TILE, cols * TILE), bf16),
        grid=(rows,),
        in_specs=[pl.BlockSpec((2, 1, 1, TILE), lambda i: (0, i, 0, 0)), VMEM],
        out_specs=pl.BlockSpec((TILE, cols * TILE), lambda i: (i, 0)),
        compiler_params=room(8),
        cost_estimate=hint(6),
        name="all_pairs",
    )(left, right)


def sum_of(arrived):
    _, rows, n = arrived.shape

    def kernel(arrived_ref, out_ref):
        for t in range(0, n, 4 * TILE):
            at = pl.ds(t, 4 * TILE)
            out_ref[:, at] = arrived_ref[:, :, at].astype(f32).sum(axis=0).astype(bf16)

    return call(kernel, [((rows, n), bf16)], (arrived,), "sum_of", 8, 1)


def residual_of(here, there, scale):
    rows, n = here.shape

    def kernel(here_ref, there_ref, out_ref):
        squares = jnp.zeros((1, TILE), f32)
        for t in range(n // TILE):
            at = pl.ds(t * TILE, TILE)
            part = scale * (here_ref[:, at].astype(f32) + there_ref[:, at].astype(f32))
            squares += jnp.sum(part * part, axis=0, keepdims=True)
            low = part.astype(bf16)
            for chip in range(LINE):
                out_ref[chip, :, at] = low
        tail = three_rows(squares)
        for chip in range(LINE):
            out_ref[chip, pl.ds(0, BLOCK), pl.ds(n, TILE)] = tail
            out_ref[chip, pl.ds(BLOCK, BLOCK), pl.ds(n, TILE)] = jnp.zeros_like(tail)

    shapes = [((LINE, rows, n + TILE), bf16)]
    return call(kernel, shapes, (here, there), "residual_of", 8, 1)


def three_rows(x):
    high = x.astype(bf16).astype(f32)
    rest = x - high
    middle = rest.astype(bf16).astype(f32)
    rows = [high, middle, rest - middle, jnp.zeros((BLOCK - 3, TILE), f32)]
    return jnp.concatenate(rows, axis=0).astype(bf16)


def mid_of(arrived, scale):
    peers, _, n = arrived.shape
    n = n - TILE

    def kernel(arrived_ref, out_ref, low_ref):
        part = scale * arrived_ref[:, :, pl.ds(0, n)].astype(f32).sum(axis=0)
        out_ref[...] = part
        low = part.astype(bf16)
        for peer in range(peers):
            low_ref[peer] = low

    shapes = [((BLOCK, n), f32), ((peers, BLOCK, n), bf16)]
    return call(kernel, shapes, (arrived,), "mid_of", 8, 1)


def chunks_of(matrix_ref, held, sems):
    chunks = sems.shape[0]
    size = matrix_ref.shape[0] // chunks
    rows = [pl.ds(q * size, size) for q in range(chunks)]
    return [
        pltpu.make_async_copy(matrix_ref.at[r], held.at[r], sems.at[q]) for q, r in enumerate(rows)
    ]


def call_on_matrix(kernel, shape, kind, matrix, operands, name, scratch):
    chunks = 4
    return pl.pallas_call(
        kernel,
        out_shape=jax.ShapeDtypeStruct(shape, kind),
        in_specs=[HBM] + [VMEM] * len(operands),
        out_specs=VMEM,
        scratch_shapes=[
            pltpu.VMEM(matrix.shape, bf16),
            pltpu.SemaphoreType.DMA((chunks,)),
            *scratch,
        ],
        compiler_params=room(12),
        cost_estimate=hint(3),
        name=name,
    )(pltpu.with_memory_space_constraint(matrix, pltpu.HBM), *operands)


def coarse_product(matrix, arrived, mid_data, scale):
    rows, cols = matrix.shape

    def kernel(matrix_ref, arrived_ref, mid_ref, out_ref, held, sems, turned_ref):
        copies = chunks_of(matrix_ref, held, sems)
        for copy in copies:
            copy.start()
        whole = (scale * arrived_ref[...].astype(f32).sum(axis=0)).astype(bf16).astype(f32)
        whole = mid_ref[...] - 0.5 * whole
        for t in range(cols // TILE):
            lines = whole[:, t * TILE : (t + 1) * TILE]
            full = jnp.concatenate([lines, jnp.zeros((TILE - BLOCK, TILE), f32)], axis=0)
            turned_ref[pl.ds(t * TILE, TILE), :] = full.T.astype(bf16)
        each = rows // TILE // len(copies)
        for c, copy in enumerate(copies):
            copy.wait()
            at = pl.ds(c * each * TILE, each * TILE)
            part = jnp.dot(held[at, :], turned_ref[...], preferred_element_type=f32)
            for q in range(each):
                out_ref[c * each + q] = part[q * TILE : (q + 1) * TILE].T[:BLOCK, :]

    shape = (rows // TILE, BLOCK, TILE)
    scratch = [pltpu.VMEM((cols, TILE), bf16)]
    operands = (arrived, mid_data)
    return call_on_matrix(kernel, shape, f32, matrix, operands, "coarse_product", scratch)


def coarse_data_of(arrived, own, other, scale):
    peers = arrived.shape[0]
    n = own.shape[2] - TILE

    def kernel(arrived_ref, own_ref, other_ref, out_ref):
        data = (scale * arrived_ref[...].sum(axis=0)).astype(bf16)
        squares = jnp.zeros((1, TILE), f32)
        for ref in (own_ref, other_ref):
            tails = ref[...].astype(f32).sum(axis=0)
            squares += jnp.sum(tails, axis=0, keepdims=True)
        tail = three_rows(squares)
        for peer in range(peers):
            out_ref[peer, 0] = data
            out_ref[peer, 1] = tail

    tails = (own[:, :, n:], other[:, :, n:])
    shapes = [((peers, 2, BLOCK, TILE), bf16)]
    return call(kernel, shapes, (arrived, *tails), "coarse_data_of", 8, 1)


def halfway_of(gathered_data, factor_down):
    peers = gathered_data.shape[0]

    def kernel(data_ref, factor_ref, out_ref):
        total = jnp.zeros((BLOCK, TILE), f32)
        for q in range(peers // 2):
            pair = jnp.concatenate([data_ref[2 * q, 0], data_ref[2 * q + 1, 0]], axis=1)
            rows = factor_ref[pl.ds(q * 2 * TILE, 2 * TILE), :]
            total += jnp.dot(pair, rows, preferred_element_type=f32)
        low = total.astype(bf16)
        for peer in range(peers):
            out_ref[peer] = low

    shapes = [((peers, BLOCK, TILE), bf16)]
    return call(kernel, shapes, (gathered_data, factor_down), "halfway_of", 8, 1)


def coarse_coef_of(halfway, factor_across):
    peers = halfway.shape[0]

    def kernel(half_ref, factor_ref, out_ref):
        total = jnp.zeros((BLOCK, TILE), f32)
        for q in range(peers):
            total += lax.dot_general(
                half_ref[q], factor_ref[q], (((1,), (1,)), ((), ())), preferred_element_type=f32
            )
        low = total.astype(bf16)
        for peer in range(peers):
            out_ref[peer] = low

    shapes = [((peers, BLOCK, TILE), bf16)]
    return call(kernel, shapes, (halfway, factor_across), "coarse_coef_of", 8, 1)


def prolong(matrix, coarse_coef, place, mid_data, scale):
    rows, cols = matrix.shape
    two = 2 * TILE

    def kernel(matrix_ref, coef_ref, low_ref, mid_ref, out_ref, held, sems):
        copies = chunks_of(matrix_ref, held, sems)
        for copy in copies:
            copy.start()
        for chip in range(HALF):
            for zl in range(LINE):
                out_ref[chip * LINE + zl, :, pl.ds(cols, TILE)] = low_ref[chip]
        total = jnp.zeros((BLOCK, cols), f32)
        each = rows // two // len(copies)
        for c, copy in enumerate(copies):
            copy.wait()
            for q in range(c * each, (c + 1) * each):
                pair = jnp.concatenate([coef_ref[2 * q], coef_ref[2 * q + 1]], axis=1)
                total += jnp.dot(pair, held[pl.ds(q * two, two), :], preferred_element_type=f32)
        low = (0.5 * mid_ref[...] + scale * total).astype(bf16)
        for chip in range(HALF * LINE):
            out_ref[chip, :, pl.ds(0, cols)] = low

    sent = coarse_coef.reshape(HALF, 2, BLOCK, TILE)
    sent = jnp.where(place[3] % 2 == 0, sent[:, 0], sent[:, 1])
    shape = (HALF * LINE, BLOCK, cols + TILE)
    operands = (coarse_coef, sent, mid_data)
    return call_on_matrix(kernel, shape, bf16, matrix, operands, "prolong", ())


def fine_of(arrived, data, core, scale):
    n = arrived.shape[2]

    def kernel(core_ref, arrived_ref, data_ref, out_ref, summed):
        me = core_ref[0]
        summed[...] = arrived_ref[...].astype(f32).sum(axis=0)
        rows = []
        for block in range(SIDE):
            at = ((block % 2) ^ me) * HALF + block // 2
            rows.append(summed[pl.ds(pl.multiple_of(at * BLOCK, BLOCK), BLOCK), :])
        whole = jnp.concatenate(rows, axis=0)
        for t in range(n // TILE):
            at = pl.ds(t * TILE, TILE)
            data = data_ref[at, :].astype(f32)
            out_ref[at, :] = 0.5 * data + scale * whole[:, t * TILE : (t + 1) * TILE].T

    scratch = [pltpu.VMEM((FIELDS, n), f32)]
    return call(kernel, [((n, FIELDS), f32)], (core, arrived, data), "fine_of", 8, 2, scratch, 1)


def in_field_order(x, core):
    n = x.shape[-1]
    x = jnp.where(core == 0, x, x[::-1])
    return x.transpose(3, 1, 0, 2).reshape(n, FIELDS)


def scale_of(tiles, listed):
    return (tiles * TILE / (SIDE * listed * TILE * TILE)) ** 0.5


def per_device(values, points0, points1, points2, tiles_a0, tiles_e1, tiles_a1, factor):
    core = lax.axis_index("k")
    col_id = lax.axis_index(COL)
    row_id = lax.axis_index(ROW)
    rows_fine, fields = values.shape
    rows_mid = points1.shape[1]
    rows_coarse = points2.shape[1]
    coarse = rows_coarse * SIDE
    share = rows_fine // SIDE
    tiles_fine, tiles_mid = rows_fine // TILE, rows_mid // TILE
    list_a0, list_e1, list_a1 = tiles_a0[0, 0], tiles_e1[0, 0], tiles_a1[0, 0]
    scale_a0 = scale_of(tiles_fine, list_a0.shape[1])
    scale_e1 = scale_of(tiles_fine, list_e1.shape[1])
    scale_a1 = scale_of(tiles_mid, list_a1.shape[1])
    scale_e2 = (1.0 / (rows_mid * SIDE)) ** 0.5

    listed_a0, listed_e1, listed_a1 = (a.shape[1] for a in (list_a0, list_e1, list_a1))

    first_e1 = 2 * rows_of(listed_a0)
    first_a1 = first_e1 + 2 * rows_of(listed_e1)

    own_e1 = in_rows(list_e1)
    there = turned(packed(points0, points1, (list_a0, list_e1, list_a1), factor))
    local = [points2, jnp.zeros((SIDE - 2, TILE), bf16), points1.reshape(2 * tiles_mid, TILE)]
    local = jnp.concatenate(local, axis=0)
    x_id, zl_id = lax.axis_index("x"), lax.axis_index("zl")
    place = jnp.stack([core, row_id, col_id, zl_id, x_id]).astype(jnp.int32)
    fine_here = points0.astype(f32).reshape(2, tiles_fine, 1, TILE)
    mid_here = points1.astype(f32).reshape(2, tiles_mid, 1, TILE)
    tail = jnp.pad(own_e1, ((0, BLOCK - own_e1.shape[0]), (0, 0))).astype(bf16)
    there, vector, local, fine_here, mid_here, tail, place = lax.optimization_barrier(
        (there, values.T, local, fine_here, mid_here, tail, place)
    )
    fine_there, mid_there, lists, common = unpacked(
        there, factor, local, tiles_fine, tiles_mid, first_a1 + 2 * rows_of(listed_a1)
    )

    common = exchanged(common, YZ)
    own, other = product_a0(lists, place, fine_here, fine_there, vector, listed_a0)
    own, other, common = lax.optimization_barrier((own, other, common))
    pair = pair_sum(own, other).reshape(LINE, 2 * BLOCK, rows_fine)
    arrived = exchanged(pair, "y")

    common, pair = lax.optimization_barrier((common, pair))
    ordered = in_row_order(place, common, from_partner(common), tiles_mid)
    arrived, ordered = lax.optimization_barrier((arrived, ordered))
    factor_down, factor_across, centres, mid_line = ordered
    summed = sum_of(arrived)
    centres, mid_later, fine_later, summed = lax.optimization_barrier(
        (centres, mid_there, fine_here, summed)
    )
    swapped = lax.ppermute(summed, "zh", [(0, 1), (1, 0)])
    coarse_kernel = all_pairs(centres, mid_later, support_coarse)
    swapped, coarse_kernel, fine_later = lax.optimization_barrier(
        (swapped, coarse_kernel, fine_later)
    )
    fine_own = exchanged(residual_of(summed, swapped, -0.5 * scale_a0), "y")
    fine_quarter = fine_later.reshape(2, QUARTER // 2, LINE, 2, 1, TILE)
    fine_quarter = lax.dynamic_index_in_dim(fine_quarter, zl_id, 2, keepdims=False)
    fine_quarter = fine_quarter.reshape(2, QUARTER, 1, TILE)
    fine_quarter = jnp.pad(fine_quarter, ((0, 0), (0, 1), (0, 0), (0, 0)), constant_values=8.0)
    fine_own, fine_quarter = lax.optimization_barrier((fine_own, fine_quarter))
    fine_own = fine_own.reshape(HALF, BLOCK, rows_fine + TILE)
    fine_other = from_partner(fine_own)

    restricted = product(
        lists, listed_e1, first_e1, 0, fine_there, mid_here, (fine_own, fine_other), support_mid, tail
    )
    restricted = exchanged(restricted, COL)
    mid_share, mid_all = mid_of(restricted, scale_e1)
    line_lists = lax.dynamic_slice_in_dim(restricted[:, :, rows_mid:], x_id * LINE, LINE, 0)
    line_lists = line_lists[:, : own_e1.shape[0]].reshape(-1, TILE).astype(jnp.int32)
    line_lists = quarter_of(line_lists, place, LINE, listed_e1, tiles_mid)
    mid_all, mid_data, line_lists = lax.optimization_barrier(
        (exchanged(mid_all, COL), turned_blocks(mid_share), line_lists)
    )

    mid_halves = (mid_all[:HALF], mid_all[HALF:])
    mid_own, mid_other = product(
        lists, listed_a1, first_a1, 1, mid_here, mid_there, mid_halves, support_mid
    )
    arrived = exchanged(pair_sum(mid_own, mid_other), YZ)

    coarse_part = coarse_product(coarse_kernel, arrived, mid_data, scale_a1)
    coarse_data = coarse_data_of(exchanged(coarse_part, COL), fine_own, fine_other, scale_e2)
    coarse_data = exchanged(coarse_data, COL)
    halfway = exchanged(halfway_of(coarse_data, factor_down), COL)
    coarse_all = exchanged(coarse_coef_of(halfway, factor_across), COL)

    new_own = exchanged(prolong(coarse_kernel, coarse_all, place, mid_data, scale_e2), YZL)
    new_other = from_partner(new_own)
    fine_part = product_quarter(
        line_lists, mid_line, fine_quarter, new_own, new_other, support_mid
    )
    own_data = lax.dynamic_slice_in_dim(values, col_id * share, share, 0)
    fine_coef = fine_of(exchanged(fine_part, "x"), own_data, place, scale_e1)

    def from_line(zl, at, size):
        both = jnp.stack([new_own, new_other])[..., at : at + size]
        both = both.reshape(2, HALF, LINE, BLOCK, size)
        both = lax.dynamic_index_in_dim(both, zl, 2, keepdims=False)
        return in_field_order(both.astype(f32), core)

    mid_coef = from_line(zl_id, 0, rows_mid)
    coarse_coef = from_line(core, rows_mid, rows_coarse)
    norm = coarse_data[:, 1].astype(f32).sum() / (rows_fine * SIDE * fields)
    return (fine_coef, mid_coef, coarse_coef, jnp.stack([norm]))


def solution(mesh):
    fine_mesh = Mesh(mesh.devices.reshape(4, 2, 2, 4, 4), ALL)
    return jax.shard_map(
        per_device,
        mesh=fine_mesh,
        in_specs=(
            P(ROW, None),
            P(None, ROW),
            P(None, ROW),
            P(None, ROW),
            P(ROW, COL, None, None),
            P(ROW, COL, None, None),
            P(ROW, COL, None, None),
            P(ROW, COL),
        ),
        out_specs=(P(ALL, None), P(COL, None), P(ROW, None), P()),
        check_vma=False,
    )
```

```python
import jax
import jax.numpy as jnp
from jax import lax
from jax.experimental import pallas as pl
from jax.experimental.pallas import tpu as pltpu
from jax.sharding import Mesh
from jax.sharding import PartitionSpec as P

TILE = 128
SIDE = 16
HALF = 8
LINE = 4
QUARTER = 8
BLOCK = 8
FIELDS = SIDE * BLOCK
GROUP = 16

support_fine = 0.35
support_mid = 0.55
support_coarse = 0.8

ROW = ("y", "zh", "k")
YZ = ("y", "zh")
YZL = ("y", "zh", "zl")
COL = ("x", "zl")
ALL = ROW + COL

bf16 = jnp.bfloat16
f32 = jnp.float32

VMEM = pl.BlockSpec(memory_space=pltpu.VMEM)
SMEM = pl.BlockSpec(memory_space=pltpu.SMEM)
HBM = pl.BlockSpec(memory_space=pltpu.HBM)


def room(mebibytes):
    return pltpu.CompilerParams(vmem_limit_bytes=mebibytes * 1024 * 1024)


def hint(microseconds):
    return pl.CostEstimate(
        flops=0, transcendentals=0, bytes_accessed=int(microseconds * 3.0e6)
    )


def turned(x):
    pairs = [(c * SIDE + r, r * SIDE + c) for r in range(SIDE) for c in range(SIDE)]
    return lax.ppermute(x, ALL, pairs)


def place_of_block(block, core):
    return ((block % 2) ^ core) * HALF + block // 2


def turned_blocks(x):
    pairs = [
        (c * SIDE + place_of_block(r, c % 2), r * SIDE + c) for r in range(SIDE) for c in range(SIDE)
    ]
    return lax.ppermute(x, ALL, pairs)


def from_partner(x):
    return lax.ppermute(x, "k", [(0, 1), (1, 0)])


def exchanged(x, axes):
    return lax.all_to_all(x, axes, split_axis=0, concat_axis=0, tiled=True)


def pair_sum(own, other):
    return (own.astype(f32) + from_partner(other).astype(f32)).astype(bf16)


def stretch_of(support):
    return (4.0 / support**5) ** 0.2


def wendland(left, right, support):
    across, upward = left[0] - right[0], left[1] - right[1]
    square = jnp.maximum(across * across + upward * upward, 1e-30)
    edge = support * stretch_of(support)
    margin = jnp.maximum(edge - square * lax.rsqrt(square), 0.0)
    margin2 = margin * margin
    ratio = 5.0 / edge**4
    return (margin2 * margin2 * (ratio - margin)).astype(bf16)


def at_tile(i):
    return pl.ds(pl.multiple_of(i * TILE, TILE), TILE)


def call(kernel, shapes, operands, name, mebibytes, microseconds, scratch=(), scalars=0):
    out = pl.pallas_call(
        kernel,
        out_shape=[jax.ShapeDtypeStruct(shape, kind) for shape, kind in shapes],
        in_specs=[SMEM] * scalars + [VMEM] * (len(operands) - scalars),
        out_specs=[VMEM] * len(shapes),
        scratch_shapes=list(scratch),
        compiler_params=room(mebibytes),
        cost_estimate=hint(microseconds),
        name=name,
    )(*operands)
    return out if len(shapes) > 1 else out[0]


def rows_of(listed):
    return -(-listed // TILE)


def in_rows(listing):
    rows = rows_of(listing.shape[1])
    padded = jnp.pad(listing, ((0, 0), (0, rows * TILE - listing.shape[1])))
    return padded.reshape(2 * rows, TILE)


def packed(points0, points1, lists, factor):
    fine, mid = points0.shape[1] // TILE, points1.shape[1] // TILE
    used = 2 * (fine + mid) + sum(2 * rows_of(a.shape[1]) for a in lists)
    above = -(-used // SIDE) * SIDE

    operands = (points0, points1, *lists, factor)
    count = len(operands)

    def kernel(*refs):
        given, out_ref, held, sems = refs[:count], refs[count], refs[count + 1 : -1], refs[-1]
        copies = [
            pltpu.make_async_copy(ref, to, sems.at[n]) for n, (ref, to) in enumerate(zip(given, held))
        ]
        for copy in copies:
            copy.start()
        for copy in copies:
            copy.wait()
        lines = []
        for ref in held[:-1]:
            whole = ref[...].astype(f32)
            length = whole.shape[1]
            short = -length % TILE
            if short:
                whole = jnp.concatenate([whole, jnp.zeros((2, short), f32)], axis=1)
            for a in range(2):
                lines += [whole[a : a + 1, t : t + TILE] for t in range(0, length, TILE)]
        if above > used:
            lines.append(jnp.zeros((above - used, TILE), f32))
        out_ref[pl.ds(0, above), :] = jnp.concatenate(lines, axis=0).astype(bf16)
        out_ref[pl.ds(above, TILE), :] = held[-1][...]

    return pl.pallas_call(
        kernel,
        out_shape=jax.ShapeDtypeStruct((above + TILE, TILE), bf16),
        in_specs=[HBM] * count,
        out_specs=VMEM,
        scratch_shapes=[pltpu.VMEM(a.shape, a.dtype) for a in operands]
        + [pltpu.SemaphoreType.DMA((count,))],
        compiler_params=room(8),
        cost_estimate=hint(1),
        name="packed",
    )(*(pltpu.with_memory_space_constraint(a, pltpu.HBM) for a in operands))


def unpacked(there, factor, local, fine, mid, listed):
    used = 2 * (fine + mid) + listed
    above = -(-used // SIDE) * SIDE
    size = 2 * TILE + local.shape[0]

    def kernel(there_ref, factor_ref, local_ref, fine_ref, mid_ref, list_ref, common_ref):
        lines = there_ref[pl.ds(0, above), :].astype(f32)
        at = 0
        for ref, tiles in ((fine_ref, fine), (mid_ref, mid)):
            for a in range(2):
                for t in range(tiles):
                    ref[a, t] = lines[at : at + 1]
                    at += 1
        list_ref[...] = lines[at : at + listed].astype(jnp.int32)
        for chip in range(HALF):
            common_ref[chip, pl.ds(0, TILE), :] = factor_ref[...]
            common_ref[chip, pl.ds(TILE, TILE), :] = there_ref[pl.ds(above, TILE), :]
            common_ref[chip, pl.ds(2 * TILE, local.shape[0]), :] = local_ref[...]

    shapes = [
        ((2, fine, 1, TILE), f32),
        ((2, mid, 1, TILE), f32),
        ((listed, TILE), jnp.int32),
        ((HALF, size, TILE), bf16),
    ]
    return call(kernel, shapes, (there, factor, local), "unpacked", 8, 1)


def in_row_order(place, common, partner, mid):
    at_centres, at_mid = 2 * TILE, 2 * TILE + SIDE

    def kernel(place_ref, own_ref, other_ref, down_ref, across_ref, centre_ref, line_ref):
        core, x = place_ref[0], place_ref[4]

        def rows(chip, of_core, at, size):
            own, other = own_ref[chip, pl.ds(at, size), :], other_ref[chip, pl.ds(at, size), :]
            return jnp.where(core == of_core, own.astype(f32), other.astype(f32))

        for block in range(SIDE):
            chip, of_core = block // 2, block % 2
            down_ref[pl.ds(block * TILE, TILE), :] = rows(chip, of_core, 0, TILE).astype(bf16)
            across_ref[block] = rows(chip, of_core, TILE, TILE).astype(bf16)
            lines = rows(chip, of_core, at_centres, SIDE)
            for a in range(2):
                centre_ref[a, block] = lines[a : a + 1]
        for q in range(LINE):
            lines = rows(x * (LINE // 2) + q // 2, q % 2, at_mid, 2 * mid)
            for a in range(2):
                for t in range(mid):
                    line_ref[a, q * mid + t] = lines[a * mid + t : a * mid + t + 1]

    shapes = [
        ((SIDE * TILE, TILE), bf16),
        ((SIDE, TILE, TILE), bf16),
        ((2, SIDE, 1, TILE), f32),
        ((2, LINE * mid, 1, TILE), f32),
    ]
    return call(kernel, shapes, (place, common, partner), "in_row_order", 8, 2, (), 1)


def set_points(left_ref, right_ref, left, right, support):
    stretch = stretch_of(support)
    for axis in range(2):
        for t in range(left.shape[1]):
            row = left_ref[axis, t] * stretch
            left[axis, t] = jnp.broadcast_to(row, (TILE, TILE)).T
        for t in range(right.shape[1]):
            right[axis, t] = right_ref[axis, t] * stretch


def point_scratch(left, right):
    return [pltpu.VMEM((2, left, TILE, TILE), f32), pltpu.VMEM((2, right, 1, TILE), f32)]


def add_tiles(list_ref, listed, first, contracted, left, right, vector, total, support):
    rows = rows_of(listed)
    group = 2 * GROUP
    steps = TILE // group
    line_j = first + contracted * rows
    line_i = first + (1 - contracted) * rows

    def step(g, carry):
        row, lane = g // steps, g % steps * group
        products = []
        for u in range(group):
            j = list_ref[line_j + row, lane + u]
            i = list_ref[line_i + row, lane + u]
            tile = wendland((left[0, j], left[1, j]), (right[0, i], right[1, i]), support)
            product = jnp.dot(vector[:, at_tile(j)], tile, preferred_element_type=f32)
            products.append((i, product))
        for i, product in products:
            total[i] += product
        return carry

    lax.fori_loop(0, listed // group, step, 0)


def product_a0(lists, place, left, right, vector, listed):
    tiles = right.shape[1]

    def kernel(
        list_ref, place_ref, left_ref, right_ref, vector_ref, own_ref, other_ref, left, right, total
    ):
        set_points(left_ref, right_ref, left, right, support_fine)
        me = place_ref[0]
        weight = jnp.where(place_ref[1] == place_ref[2], -2.0 / scale_of(tiles, listed), 0.0)
        for i in range(tiles):
            at = pl.ds(i * TILE, TILE)
            total[i] = vector_ref[:, at].astype(f32) * weight
        add_tiles(list_ref, listed, 0, 1, left, right, vector_ref, total, support_fine)
        for half in range(HALF):
            for i in range(tiles):
                at = pl.ds(i * TILE, TILE)
                own = pl.ds(pl.multiple_of((2 * half + me) * BLOCK, BLOCK), BLOCK)
                other = pl.ds(pl.multiple_of((2 * half + 1 - me) * BLOCK, BLOCK), BLOCK)
                own_ref[half, :, at] = total[i, own, :].astype(bf16)
                other_ref[half, :, at] = total[i, other, :].astype(bf16)

    half = ((HALF, BLOCK, tiles * TILE), bf16)
    scratch = [*point_scratch(left.shape[1], tiles), pltpu.VMEM((tiles, FIELDS, TILE), f32)]
    operands = (lists, place, left, right, vector)
    return call(kernel, [half, half], operands, "product_a0", 16, 20, scratch, 2)


def product(lists, listed, first, contracted, left, right, halves, support, tail=None):
    tiles = right.shape[1]
    length = left.shape[1] * TILE
    size = tiles * TILE

    def kernel(list_ref, left_ref, right_ref, own_ref, other_ref, *rest):
        *given, left, right, vector, total = rest
        set_points(left_ref, right_ref, left, right, support)
        total[...] = jnp.zeros_like(total)
        for ref, at in ((own_ref, 0), (other_ref, FIELDS // 2)):
            rows = ref[:, :, pl.ds(0, length)].reshape(FIELDS // 2, length)
            vector[pl.ds(at, FIELDS // 2), :] = rows
        add_tiles(list_ref, listed, first, contracted, left, right, vector, total, support)
        for i in range(tiles):
            low = total[i].astype(bf16)
            at = pl.ds(i * TILE, TILE)
            if tail is not None:
                given[1][:, :, at] = low.reshape(SIDE, BLOCK, TILE)
            else:
                pair = low.reshape(2, HALF, BLOCK, TILE)
                given[0][:, :, at] = pair[0]
                given[1][:, :, at] = pair[1]
        if tail is not None:
            for peer in range(SIDE):
                given[1][peer, :, pl.ds(size, TILE)] = given[0][...]

    scratch = [
        *point_scratch(left.shape[1], tiles),
        pltpu.VMEM((FIELDS, length), bf16),
        pltpu.VMEM((tiles, FIELDS, TILE), f32),
    ]
    operands = (lists, left, right, *halves)
    if tail is not None:
        shapes = [((SIDE, BLOCK, size + TILE), bf16)]
        operands = (*operands, tail)
    else:
        shapes = [((HALF, BLOCK, size), bf16)] * 2
    return call(kernel, shapes, operands, "product", 16, listed / 18, scratch, 1)


def quarter_of(lists, place, blocks, listed):
    held = rows_of(listed)

    def kernel(place_ref, list_ref, out_ref):
        zl = place_ref[3]
        row = lax.broadcasted_iota(jnp.int32, (TILE, TILE), 0)
        col = lax.broadcasted_iota(jnp.int32, (TILE, TILE), 1)
        before = (row < col).astype(bf16)
        slot = row.astype(f32)
        lane = lax.broadcasted_iota(jnp.int32, (1, TILE), 1)
        for block in range(blocks):
            count = jnp.zeros((1, 1), f32)
            total = jnp.zeros((BLOCK, TILE), f32)
            for part in range(held):
                at = block * 2 * held + part
                i = list_ref[at : at + 1, :]
                j = list_ref[at + held : at + held + 1, :]
                real = jnp.where(lane + part * TILE < listed, 1.0, 0.0)
                flag = jnp.where(((i >> 1) & (LINE - 1)) == zl, real, 0.0)
                rank = count + jnp.dot(
                    jnp.broadcast_to(flag, (BLOCK, TILE)).astype(bf16),
                    before,
                    preferred_element_type=f32,
                )[:1]
                here = jnp.where(slot == jnp.where(flag > 0.5, rank, -1.0), 1.0, 0.0).astype(bf16)
                lines = [((i >> 3) * 2 + (i & 1)).astype(f32), j.astype(f32)]
                lines.append(jnp.zeros((BLOCK - 2, TILE), f32))
                lines = jnp.concatenate(lines, axis=0).astype(bf16)
                total += lax.dot_general(
                    lines, here, (((1,), (1,)), ((), ())), preferred_element_type=f32
                )
                count += jnp.sum(flag, axis=1, keepdims=True)
            at = pl.ds(block * TILE, TILE)
            rows = jnp.where(lane.astype(f32) < count, total[0:1], float(QUARTER))
            groups = jnp.broadcast_to((count + (GROUP - 1)) * (1.0 / GROUP), (1, TILE))
            out_ref[0:1, at] = rows.astype(jnp.int32)
            out_ref[1:2, at] = total[1:2].astype(jnp.int32)
            out_ref[2:3, at] = groups.astype(jnp.int32)
            out_ref[3:, at] = jnp.zeros((BLOCK - 3, TILE), jnp.int32)

    shapes = [((BLOCK, blocks * TILE), jnp.int32)]
    return call(kernel, shapes, (place, lists), "quarter_of", 8, 3, (), 1)


def dense_block(lists, block, left, right, support):
    cols, rows = left.shape[1], right.shape[1]

    def kernel(list_ref, left_ref, right_ref, out_ref, left, right):
        set_points(left_ref, right_ref, left, right, support)
        out_ref[...] = jnp.zeros_like(out_ref)

        def step(g, carry):
            for u in range(GROUP):
                i = list_ref[0, block * TILE + g * GROUP + u]
                j = list_ref[1, block * TILE + g * GROUP + u]
                out_ref[at_tile(j), at_tile(i)] = wendland(
                    (left[0, j], left[1, j]), (right[0, i], right[1, i]), support
                )
            return carry

        lax.fori_loop(0, list_ref[2, block * TILE], step, 0)

    shapes = [((cols * TILE, rows * TILE), bf16)]
    scratch = point_scratch(cols, rows)
    return call(kernel, shapes, (lists, left, right), "dense_block", 12, 3, scratch, 1)


def product_dense(matrices, own, other):
    count = len(matrices)
    length, width = matrices[0].shape
    size = QUARTER * TILE

    def kernel(*refs):
        given, (own_ref, other_ref, out_ref, held, sems, vector, total) = refs[:count], refs[count:]
        copies = [pltpu.make_async_copy(given[q], held.at[q], sems.at[q]) for q in range(count)]
        for copy in copies:
            copy.start()
        for ref, first in ((own_ref, 0), (other_ref, FIELDS // 2)):
            for chip in range(HALF):
                for zl in range(LINE):
                    at = pl.ds(first + chip * BLOCK, BLOCK)
                    part = ref[chip * LINE + zl, :, pl.ds(0, length)]
                    vector[at, pl.ds(zl * length, length)] = part
        for q, copy in enumerate(copies):
            copy.wait()
            lines = vector[:, pl.ds(q * length, length)]
            for t in range(0, size, 2 * TILE):
                at = pl.ds(t, 2 * TILE)
                part = jnp.dot(lines, held[q, :, at], preferred_element_type=f32)
                if q == 0:
                    total[:, at] = part
                elif q < count - 1:
                    total[:, at] += part
                else:
                    out_ref[t // (2 * TILE)] = (total[:, at] + part).astype(bf16)

    return pl.pallas_call(
        kernel,
        out_shape=jax.ShapeDtypeStruct((QUARTER // 2, FIELDS, 2 * TILE), bf16),
        in_specs=[HBM] * count + [VMEM] * 2,
        out_specs=VMEM,
        scratch_shapes=[
            pltpu.VMEM((count, length, width), bf16),
            pltpu.SemaphoreType.DMA((count,)),
            pltpu.VMEM((FIELDS, count * length), bf16),
            pltpu.VMEM((FIELDS, size), f32),
        ],
        compiler_params=room(20),
        cost_estimate=hint(4),
        name="product_dense",
    )(*(pltpu.with_memory_space_constraint(m, pltpu.HBM) for m in matrices), own, other)


def all_pairs(left, right, support):
    rows, cols = left.shape[1], right.shape[1]

    def kernel(left_ref, right_ref, out_ref):
        stretch = stretch_of(support)
        ys = [jnp.broadcast_to(left_ref[a, 0] * stretch, (TILE, TILE)).T for a in range(2)]
        for j in range(cols):
            out_ref[:, pl.ds(j * TILE, TILE)] = wendland(
                ys, (right_ref[0, j] * stretch, right_ref[1, j] * stretch), support
            )

    return pl.pallas_call(
        kernel,
        out_shape=jax.ShapeDtypeStruct((rows * TILE, cols * TILE), bf16),
        grid=(rows,),
        in_specs=[pl.BlockSpec((2, 1, 1, TILE), lambda i: (0, i, 0, 0)), VMEM],
        out_specs=pl.BlockSpec((TILE, cols * TILE), lambda i: (i, 0)),
        compiler_params=room(8),
        cost_estimate=hint(6),
        name="all_pairs",
    )(left, right)


def sum_of(arrived):
    _, rows, n = arrived.shape

    def kernel(arrived_ref, out_ref):
        for t in range(0, n, 4 * TILE):
            at = pl.ds(t, 4 * TILE)
            out_ref[:, at] = arrived_ref[:, :, at].astype(f32).sum(axis=0).astype(bf16)

    return call(kernel, [((rows, n), bf16)], (arrived,), "sum_of", 8, 1)


def residual_of(here, there, scale):
    rows, n = here.shape

    def kernel(here_ref, there_ref, out_ref):
        squares = jnp.zeros((1, TILE), f32)
        for t in range(n // TILE):
            at = pl.ds(t * TILE, TILE)
            part = scale * (here_ref[:, at].astype(f32) + there_ref[:, at].astype(f32))
            squares += jnp.sum(part * part, axis=0, keepdims=True)
            low = part.astype(bf16)
            for chip in range(LINE):
                out_ref[chip, :, at] = low
        tail = three_rows(squares)
        for chip in range(LINE):
            out_ref[chip, pl.ds(0, BLOCK), pl.ds(n, TILE)] = tail
            out_ref[chip, pl.ds(BLOCK, BLOCK), pl.ds(n, TILE)] = jnp.zeros_like(tail)

    shapes = [((LINE, rows, n + TILE), bf16)]
    return call(kernel, shapes, (here, there), "residual_of", 8, 1)


def three_rows(x):
    high = x.astype(bf16).astype(f32)
    rest = x - high
    middle = rest.astype(bf16).astype(f32)
    rows = [high, middle, rest - middle, jnp.zeros((BLOCK - 3, TILE), f32)]
    return jnp.concatenate(rows, axis=0).astype(bf16)


def mid_of(arrived, scale):
    peers, _, n = arrived.shape
    n = n - TILE

    def kernel(arrived_ref, out_ref, low_ref):
        part = scale * arrived_ref[:, :, pl.ds(0, n)].astype(f32).sum(axis=0)
        out_ref[...] = part
        low = part.astype(bf16)
        for peer in range(peers):
            low_ref[peer] = low

    shapes = [((BLOCK, n), f32), ((peers, BLOCK, n), bf16)]
    return call(kernel, shapes, (arrived,), "mid_of", 8, 1)


def chunks_of(matrix_ref, held, sems):
    chunks = sems.shape[0]
    size = matrix_ref.shape[0] // chunks
    rows = [pl.ds(q * size, size) for q in range(chunks)]
    return [
        pltpu.make_async_copy(matrix_ref.at[r], held.at[r], sems.at[q]) for q, r in enumerate(rows)
    ]


def call_on_matrix(kernel, shape, kind, matrix, operands, name, scratch):
    chunks = 4
    return pl.pallas_call(
        kernel,
        out_shape=jax.ShapeDtypeStruct(shape, kind),
        in_specs=[HBM] + [VMEM] * len(operands),
        out_specs=VMEM,
        scratch_shapes=[
            pltpu.VMEM(matrix.shape, bf16),
            pltpu.SemaphoreType.DMA((chunks,)),
            *scratch,
        ],
        compiler_params=room(12),
        cost_estimate=hint(3),
        name=name,
    )(pltpu.with_memory_space_constraint(matrix, pltpu.HBM), *operands)


def coarse_product(matrix, arrived, mid_data, scale):
    rows, cols = matrix.shape

    def kernel(matrix_ref, arrived_ref, mid_ref, out_ref, held, sems, turned_ref):
        copies = chunks_of(matrix_ref, held, sems)
        for copy in copies:
            copy.start()
        whole = (scale * arrived_ref[...].astype(f32).sum(axis=0)).astype(bf16).astype(f32)
        whole = mid_ref[...] - 0.5 * whole
        for t in range(cols // TILE):
            lines = whole[:, t * TILE : (t + 1) * TILE]
            full = jnp.concatenate([lines, jnp.zeros((TILE - BLOCK, TILE), f32)], axis=0)
            turned_ref[pl.ds(t * TILE, TILE), :] = full.T.astype(bf16)
        each = rows // TILE // len(copies)
        for c, copy in enumerate(copies):
            copy.wait()
            for q in range(c * each, (c + 1) * each):
                part = jnp.dot(
                    held[pl.ds(q * TILE, TILE), :], turned_ref[...], preferred_element_type=f32
                )
                out_ref[q] = part.T[:BLOCK, :]

    shape = (rows // TILE, BLOCK, TILE)
    scratch = [pltpu.VMEM((cols, TILE), bf16)]
    operands = (arrived, mid_data)
    return call_on_matrix(kernel, shape, f32, matrix, operands, "coarse_product", scratch)


def coarse_data_of(arrived, own, other, scale):
    peers = arrived.shape[0]
    n = own.shape[2] - TILE

    def kernel(arrived_ref, own_ref, other_ref, out_ref):
        data = (scale * arrived_ref[...].sum(axis=0)).astype(bf16)
        squares = jnp.zeros((1, TILE), f32)
        for ref in (own_ref, other_ref):
            tails = ref[...].astype(f32).sum(axis=0)
            squares += jnp.sum(tails, axis=0, keepdims=True)
        tail = three_rows(squares)
        for peer in range(peers):
            out_ref[peer, 0] = data
            out_ref[peer, 1] = tail

    tails = (own[:, :, n:], other[:, :, n:])
    shapes = [((peers, 2, BLOCK, TILE), bf16)]
    return call(kernel, shapes, (arrived, *tails), "coarse_data_of", 8, 1)


def halfway_of(gathered_data, factor_down):
    peers = gathered_data.shape[0]

    def kernel(data_ref, factor_ref, out_ref):
        total = jnp.zeros((BLOCK, TILE), f32)
        for q in range(peers // 2):
            pair = jnp.concatenate([data_ref[2 * q, 0], data_ref[2 * q + 1, 0]], axis=1)
            rows = factor_ref[pl.ds(q * 2 * TILE, 2 * TILE), :]
            total += jnp.dot(pair, rows, preferred_element_type=f32)
        low = total.astype(bf16)
        for peer in range(peers):
            out_ref[peer] = low

    shapes = [((peers, BLOCK, TILE), bf16)]
    return call(kernel, shapes, (gathered_data, factor_down), "halfway_of", 8, 1)


def coarse_coef_of(halfway, factor_across):
    peers = halfway.shape[0]

    def kernel(half_ref, factor_ref, out_ref):
        total = jnp.zeros((BLOCK, TILE), f32)
        for q in range(peers):
            total += lax.dot_general(
                half_ref[q], factor_ref[q], (((1,), (1,)), ((), ())), preferred_element_type=f32
            )
        low = total.astype(bf16)
        for peer in range(peers):
            out_ref[peer] = low

    shapes = [((peers, BLOCK, TILE), bf16)]
    return call(kernel, shapes, (halfway, factor_across), "coarse_coef_of", 8, 1)


def prolong(matrix, coarse_coef, place, mid_data, scale):
    rows, cols = matrix.shape
    two = 2 * TILE

    def kernel(matrix_ref, coef_ref, low_ref, mid_ref, out_ref, held, sems):
        copies = chunks_of(matrix_ref, held, sems)
        for copy in copies:
            copy.start()
        for chip in range(HALF):
            for zl in range(LINE):
                out_ref[chip * LINE + zl, :, pl.ds(cols, TILE)] = low_ref[chip]
        total = jnp.zeros((BLOCK, cols), f32)
        each = rows // two // len(copies)
        for c, copy in enumerate(copies):
            copy.wait()
            for q in range(c * each, (c + 1) * each):
                pair = jnp.concatenate([coef_ref[2 * q], coef_ref[2 * q + 1]], axis=1)
                total += jnp.dot(pair, held[pl.ds(q * two, two), :], preferred_element_type=f32)
        low = (0.5 * mid_ref[...] + scale * total).astype(bf16)
        for chip in range(HALF * LINE):
            out_ref[chip, :, pl.ds(0, cols)] = low

    sent = coarse_coef.reshape(HALF, 2, BLOCK, TILE)
    sent = jnp.where(place[3] % 2 == 0, sent[:, 0], sent[:, 1])
    shape = (HALF * LINE, BLOCK, cols + TILE)
    operands = (coarse_coef, sent, mid_data)
    return call_on_matrix(kernel, shape, bf16, matrix, operands, "prolong", ())


def fine_of(arrived, data, core, scale):
    n = arrived.shape[2]

    def kernel(core_ref, arrived_ref, data_ref, out_ref, summed):
        me = core_ref[0]
        summed[...] = arrived_ref[...].astype(f32).sum(axis=0)
        rows = []
        for block in range(SIDE):
            at = ((block % 2) ^ me) * HALF + block // 2
            rows.append(summed[pl.ds(pl.multiple_of(at * BLOCK, BLOCK), BLOCK), :])
        whole = jnp.concatenate(rows, axis=0)
        for t in range(n // TILE):
            at = pl.ds(t * TILE, TILE)
            data = data_ref[at, :].astype(f32)
            out_ref[at, :] = 0.5 * data + scale * whole[:, t * TILE : (t + 1) * TILE].T

    scratch = [pltpu.VMEM((FIELDS, n), f32)]
    return call(kernel, [((n, FIELDS), f32)], (core, arrived, data), "fine_of", 8, 2, scratch, 1)


def in_field_order(x, core):
    n = x.shape[-1]
    x = jnp.where(core == 0, x, x[::-1])
    return x.transpose(3, 1, 0, 2).reshape(n, FIELDS)


def scale_of(tiles, listed):
    return (tiles * TILE / (SIDE * listed * TILE * TILE)) ** 0.5


def per_device(values, points0, points1, points2, tiles_a0, tiles_e1, tiles_a1, factor):
    core = lax.axis_index("k")
    col_id = lax.axis_index(COL)
    row_id = lax.axis_index(ROW)
    rows_fine, fields = values.shape
    rows_mid = points1.shape[1]
    rows_coarse = points2.shape[1]
    coarse = rows_coarse * SIDE
    share = rows_fine // SIDE
    tiles_fine, tiles_mid = rows_fine // TILE, rows_mid // TILE
    list_a0, list_e1, list_a1 = tiles_a0[0, 0], tiles_e1[0, 0], tiles_a1[0, 0]
    scale_a0 = scale_of(tiles_fine, list_a0.shape[1])
    scale_e1 = scale_of(tiles_fine, list_e1.shape[1])
    scale_a1 = scale_of(tiles_mid, list_a1.shape[1])
    scale_e2 = (1.0 / (rows_mid * SIDE)) ** 0.5

    listed_a0, listed_e1, listed_a1 = (a.shape[1] for a in (list_a0, list_e1, list_a1))

    first_e1 = 2 * rows_of(listed_a0)
    first_a1 = first_e1 + 2 * rows_of(listed_e1)

    own_e1 = in_rows(list_e1)
    there = turned(packed(points0, points1, (list_a0, list_e1, list_a1), factor))
    local = [points2, jnp.zeros((SIDE - 2, TILE), bf16), points1.reshape(2 * tiles_mid, TILE)]
    local = jnp.concatenate(local, axis=0)
    x_id, zl_id = lax.axis_index("x"), lax.axis_index("zl")
    place = jnp.stack([core, row_id, col_id, zl_id, x_id]).astype(jnp.int32)
    fine_here = points0.astype(f32).reshape(2, tiles_fine, 1, TILE)
    mid_here = points1.astype(f32).reshape(2, tiles_mid, 1, TILE)
    tail = jnp.pad(own_e1, ((0, BLOCK - own_e1.shape[0]), (0, 0))).astype(bf16)
    there, vector, local, fine_here, mid_here, tail, place = lax.optimization_barrier(
        (there, values.T, local, fine_here, mid_here, tail, place)
    )
    fine_there, mid_there, lists, common = unpacked(
        there, factor, local, tiles_fine, tiles_mid, first_a1 + 2 * rows_of(listed_a1)
    )

    common = exchanged(common, YZ)
    own, other = product_a0(lists, place, fine_here, fine_there, vector, listed_a0)
    own, other, common = lax.optimization_barrier((own, other, common))
    pair = pair_sum(own, other).reshape(LINE, 2 * BLOCK, rows_fine)
    arrived = exchanged(pair, "y")

    common, pair = lax.optimization_barrier((common, pair))
    ordered = in_row_order(place, common, from_partner(common), tiles_mid)
    arrived, ordered = lax.optimization_barrier((arrived, ordered))
    factor_down, factor_across, centres, mid_line = ordered
    summed = sum_of(arrived)
    centres, mid_later, fine_later, summed = lax.optimization_barrier(
        (centres, mid_there, fine_here, summed)
    )
    swapped = lax.ppermute(summed, "zh", [(0, 1), (1, 0)])
    coarse_kernel = all_pairs(centres, mid_later, support_coarse)
    swapped, coarse_kernel, fine_later = lax.optimization_barrier(
        (swapped, coarse_kernel, fine_later)
    )
    fine_own = exchanged(residual_of(summed, swapped, -0.5 * scale_a0), "y")
    fine_quarter = fine_later.reshape(2, QUARTER // 2, LINE, 2, 1, TILE)
    fine_quarter = lax.dynamic_index_in_dim(fine_quarter, zl_id, 2, keepdims=False)
    fine_quarter = fine_quarter.reshape(2, QUARTER, 1, TILE)
    fine_quarter = jnp.pad(fine_quarter, ((0, 0), (0, 1), (0, 0), (0, 0)), constant_values=8.0)
    fine_own, fine_quarter = lax.optimization_barrier((fine_own, fine_quarter))
    fine_own = fine_own.reshape(HALF, BLOCK, rows_fine + TILE)
    fine_other = from_partner(fine_own)

    restricted = product(
        lists, listed_e1, first_e1, 0, fine_there, mid_here, (fine_own, fine_other), support_mid, tail
    )
    restricted = exchanged(restricted, COL)
    mid_share, mid_all = mid_of(restricted, scale_e1)
    line_lists = lax.dynamic_slice_in_dim(restricted[:, :, rows_mid:], x_id * LINE, LINE, 0)
    line_lists = line_lists[:, : own_e1.shape[0]].reshape(-1, TILE).astype(jnp.int32)
    line_lists = quarter_of(line_lists, place, LINE, listed_e1)
    mid_all, mid_data, line_lists = lax.optimization_barrier(
        (exchanged(mid_all, COL), turned_blocks(mid_share), line_lists)
    )

    mid_halves = (mid_all[:HALF], mid_all[HALF:])
    mid_own, mid_other = product(
        lists, listed_a1, first_a1, 1, mid_here, mid_there, mid_halves, support_mid
    )
    def e1_block(lists, q):
        points = mid_line[:, q * tiles_mid : (q + 1) * tiles_mid]
        return dense_block(lists, q, points, fine_quarter, support_mid)

    pair, lists_then = lax.optimization_barrier((pair_sum(mid_own, mid_other), line_lists))
    arrived, *first_two = lax.optimization_barrier(
        (exchanged(pair, YZ), e1_block(lists_then, 0), e1_block(lists_then, 1))
    )
    coarse_part, lists_then = lax.optimization_barrier(
        (coarse_product(coarse_kernel, arrived, mid_data, scale_a1), line_lists)
    )
    arrived, third = lax.optimization_barrier(
        (exchanged(coarse_part, COL), e1_block(lists_then, 2))
    )
    coarse_data, lists_then = lax.optimization_barrier(
        (coarse_data_of(arrived, fine_own, fine_other, scale_e2), line_lists)
    )
    coarse_data, fourth = lax.optimization_barrier(
        (exchanged(coarse_data, COL), e1_block(lists_then, 3))
    )
    halfway = exchanged(halfway_of(coarse_data, factor_down), COL)
    coarse_all = exchanged(coarse_coef_of(halfway, factor_across), COL)

    new_own = exchanged(prolong(coarse_kernel, coarse_all, place, mid_data, scale_e2), YZL)
    new_other = from_partner(new_own)
    fine_part = product_dense((*first_two, third, fourth), new_own, new_other)
    fine_part, new_own, new_other = lax.optimization_barrier((fine_part, new_own, new_other))
    own_data = lax.dynamic_slice_in_dim(values, col_id * share, share, 0)
    fine_coef = fine_of(exchanged(fine_part, "x"), own_data, place, scale_e1)

    def from_line(zl, at, size):
        both = jnp.stack([new_own, new_other])[..., at : at + size]
        both = both.reshape(2, HALF, LINE, BLOCK, size)
        both = lax.dynamic_index_in_dim(both, zl, 2, keepdims=False)
        return in_field_order(both.astype(f32), core)

    mid_coef = from_line(zl_id, 0, rows_mid)
    coarse_coef = from_line(core, rows_mid, rows_coarse)
    norm = coarse_data[:, 1].astype(f32).sum() / (rows_fine * SIDE * fields)
    return (fine_coef, mid_coef, coarse_coef, jnp.stack([norm]))


def solution(mesh):
    fine_mesh = Mesh(mesh.devices.reshape(4, 2, 2, 4, 4), ALL)
    return jax.shard_map(
        per_device,
        mesh=fine_mesh,
        in_specs=(
            P(ROW, None),
            P(None, ROW),
            P(None, ROW),
            P(None, ROW),
            P(ROW, COL, None, None),
            P(ROW, COL, None, None),
            P(ROW, COL, None, None),
            P(ROW, COL),
        ),
        out_specs=(P(ALL, None), P(COL, None), P(ROW, None), P()),
        check_vma=False,
    )
```

```python
import jax
import jax.numpy as jnp
from jax import lax
from jax.experimental import pallas as pl
from jax.experimental.pallas import tpu as pltpu
from jax.sharding import Mesh
from jax.sharding import PartitionSpec as P

TILE = 128
SIDE = 16
HALF = 8
LINE = 4
QUARTER = 8
BLOCK = 8
FIELDS = SIDE * BLOCK
GROUP = 16

support_fine = 0.35
support_mid = 0.55
support_coarse = 0.8

ROW = ("y", "zh", "k")
YZ = ("y", "zh")
YZL = ("y", "zh", "zl")
COL = ("x", "zl")
ALL = ROW + COL

bf16 = jnp.bfloat16
f32 = jnp.float32

VMEM = pl.BlockSpec(memory_space=pltpu.VMEM)
SMEM = pl.BlockSpec(memory_space=pltpu.SMEM)
HBM = pl.BlockSpec(memory_space=pltpu.HBM)


def room(mebibytes):
    return pltpu.CompilerParams(vmem_limit_bytes=mebibytes * 1024 * 1024)


def hint(microseconds):
    return pl.CostEstimate(
        flops=0, transcendentals=0, bytes_accessed=int(microseconds * 3.0e6)
    )


def turned(x):
    pairs = [(c * SIDE + r, r * SIDE + c) for r in range(SIDE) for c in range(SIDE)]
    return lax.ppermute(x, ALL, pairs)


def place_of_block(block, core):
    return ((block % 2) ^ core) * HALF + block // 2


def turned_blocks(x):
    pairs = [
        (c * SIDE + place_of_block(r, c % 2), r * SIDE + c) for r in range(SIDE) for c in range(SIDE)
    ]
    return lax.ppermute(x, ALL, pairs)


def from_partner(x):
    return lax.ppermute(x, "k", [(0, 1), (1, 0)])


def exchanged(x, axes):
    return lax.all_to_all(x, axes, split_axis=0, concat_axis=0, tiled=True)


def pair_sum(own, other):
    return (own.astype(f32) + from_partner(other).astype(f32)).astype(bf16)


def stretch_of(support):
    return (4.0 / support**5) ** 0.2


def wendland(left, right, support):
    across, upward = left[0] - right[0], left[1] - right[1]
    square = jnp.maximum(across * across + upward * upward, 1e-30)
    edge = support * stretch_of(support)
    margin = jnp.maximum(edge - square * lax.rsqrt(square), 0.0)
    margin2 = margin * margin
    ratio = 5.0 / edge**4
    return (margin2 * margin2 * (ratio - margin)).astype(bf16)


def at_tile(i):
    return pl.ds(pl.multiple_of(i * TILE, TILE), TILE)


def call(kernel, shapes, operands, name, mebibytes, microseconds, scratch=(), scalars=0):
    out = pl.pallas_call(
        kernel,
        out_shape=[jax.ShapeDtypeStruct(shape, kind) for shape, kind in shapes],
        in_specs=[SMEM] * scalars + [VMEM] * (len(operands) - scalars),
        out_specs=[VMEM] * len(shapes),
        scratch_shapes=list(scratch),
        compiler_params=room(mebibytes),
        cost_estimate=hint(microseconds),
        name=name,
    )(*operands)
    return out if len(shapes) > 1 else out[0]


def rows_of(listed):
    return -(-listed // TILE)


def in_rows(listing):
    rows = rows_of(listing.shape[1])
    padded = jnp.pad(listing, ((0, 0), (0, rows * TILE - listing.shape[1])))
    return padded.reshape(2 * rows, TILE)


def packed(points0, points1, lists, factor):
    fine, mid = points0.shape[1] // TILE, points1.shape[1] // TILE
    used = 2 * (fine + mid) + sum(2 * rows_of(a.shape[1]) for a in lists)
    above = -(-used // SIDE) * SIDE

    operands = (points0, points1, *lists, factor)
    count = len(operands)

    def kernel(*refs):
        given, out_ref, held, sems = refs[:count], refs[count], refs[count + 1 : -1], refs[-1]
        copies = [
            pltpu.make_async_copy(ref, to, sems.at[n]) for n, (ref, to) in enumerate(zip(given, held))
        ]
        for copy in copies:
            copy.start()
        for copy in copies:
            copy.wait()
        lines = []
        for ref in held[:-1]:
            whole = ref[...].astype(f32)
            length = whole.shape[1]
            short = -length % TILE
            if short:
                whole = jnp.concatenate([whole, jnp.zeros((2, short), f32)], axis=1)
            for a in range(2):
                lines += [whole[a : a + 1, t : t + TILE] for t in range(0, length, TILE)]
        if above > used:
            lines.append(jnp.zeros((above - used, TILE), f32))
        out_ref[pl.ds(0, above), :] = jnp.concatenate(lines, axis=0).astype(bf16)
        out_ref[pl.ds(above, TILE), :] = held[-1][...]

    return pl.pallas_call(
        kernel,
        out_shape=jax.ShapeDtypeStruct((above + TILE, TILE), bf16),
        in_specs=[HBM] * count,
        out_specs=VMEM,
        scratch_shapes=[pltpu.VMEM(a.shape, a.dtype) for a in operands]
        + [pltpu.SemaphoreType.DMA((count,))],
        compiler_params=room(8),
        cost_estimate=hint(1),
        name="packed",
    )(*(pltpu.with_memory_space_constraint(a, pltpu.HBM) for a in operands))


def unpacked(there, factor, local, fine, mid, listed):
    used = 2 * (fine + mid) + listed
    above = -(-used // SIDE) * SIDE
    size = 2 * TILE + local.shape[0]

    def kernel(there_ref, factor_ref, local_ref, fine_ref, mid_ref, list_ref, common_ref):
        lines = there_ref[pl.ds(0, above), :].astype(f32)
        at = 0
        for ref, tiles in ((fine_ref, fine), (mid_ref, mid)):
            for a in range(2):
                for t in range(tiles):
                    ref[a, t] = lines[at : at + 1]
                    at += 1
        list_ref[...] = lines[at : at + listed].astype(jnp.int32)
        common_ref[pl.ds(0, TILE), :] = factor_ref[...]
        common_ref[pl.ds(TILE, TILE), :] = there_ref[pl.ds(above, TILE), :]
        common_ref[pl.ds(2 * TILE, local.shape[0]), :] = local_ref[...]

    shapes = [
        ((2, fine, 1, TILE), f32),
        ((2, mid, 1, TILE), f32),
        ((listed, TILE), jnp.int32),
        ((size, TILE), bf16),
    ]
    return call(kernel, shapes, (there, factor, local), "unpacked", 8, 1)


def split_common(place, common, mid):
    at_centres, at_mid = 2 * TILE, 2 * TILE + SIDE

    def kernel(place_ref, common_ref, down_ref, across_ref, centre_ref, line_ref):
        x = place_ref[4]
        for block in range(SIDE):
            down_ref[pl.ds(block * TILE, TILE), :] = common_ref[block, pl.ds(0, TILE), :]
            across_ref[block] = common_ref[block, pl.ds(TILE, TILE), :]
            lines = common_ref[block, pl.ds(at_centres, SIDE), :].astype(f32)
            for a in range(2):
                centre_ref[a, block] = lines[a : a + 1]
        for q in range(LINE):
            lines = common_ref[x * LINE + q, pl.ds(at_mid, 2 * mid), :].astype(f32)
            for a in range(2):
                for t in range(mid):
                    line_ref[a, q * mid + t] = lines[a * mid + t : a * mid + t + 1]

    shapes = [
        ((SIDE * TILE, TILE), bf16),
        ((SIDE, TILE, TILE), bf16),
        ((2, SIDE, 1, TILE), f32),
        ((2, LINE * mid, 1, TILE), f32),
    ]
    return call(kernel, shapes, (place, common), "split_common", 8, 2, (), 1)


def set_points(left_ref, right_ref, left, right, support):
    stretch = stretch_of(support)
    for axis in range(2):
        for t in range(left.shape[1]):
            row = left_ref[axis, t] * stretch
            left[axis, t] = jnp.broadcast_to(row, (TILE, TILE)).T
        for t in range(right.shape[1]):
            right[axis, t] = right_ref[axis, t] * stretch


def point_scratch(left, right):
    return [pltpu.VMEM((2, left, TILE, TILE), f32), pltpu.VMEM((2, right, 1, TILE), f32)]


def add_tiles(list_ref, listed, first, contracted, left, right, vector, total, support):
    rows = rows_of(listed)
    group = 2 * GROUP
    steps = TILE // group
    line_j = first + contracted * rows
    line_i = first + (1 - contracted) * rows

    def step(g, carry):
        row, lane = g // steps, g % steps * group
        products = []
        for u in range(group):
            j = list_ref[line_j + row, lane + u]
            i = list_ref[line_i + row, lane + u]
            tile = wendland((left[0, j], left[1, j]), (right[0, i], right[1, i]), support)
            product = jnp.dot(vector[:, at_tile(j)], tile, preferred_element_type=f32)
            products.append((i, product))
        for i, product in products:
            total[i] += product
        return carry

    lax.fori_loop(0, listed // group, step, 0)


def product_a0(lists, place, left, right, vector, listed):
    tiles = right.shape[1]

    def kernel(
        list_ref, place_ref, left_ref, right_ref, vector_ref, own_ref, other_ref, left, right, total
    ):
        set_points(left_ref, right_ref, left, right, support_fine)
        me = place_ref[0]
        weight = jnp.where(place_ref[1] == place_ref[2], -2.0 / scale_of(tiles, listed), 0.0)
        for i in range(tiles):
            at = pl.ds(i * TILE, TILE)
            total[i] = vector_ref[:, at].astype(f32) * weight
        add_tiles(list_ref, listed, 0, 1, left, right, vector_ref, total, support_fine)
        for half in range(HALF):
            for i in range(tiles):
                at = pl.ds(i * TILE, TILE)
                own = pl.ds(pl.multiple_of((2 * half + me) * BLOCK, BLOCK), BLOCK)
                other = pl.ds(pl.multiple_of((2 * half + 1 - me) * BLOCK, BLOCK), BLOCK)
                own_ref[half, :, at] = total[i, own, :].astype(bf16)
                other_ref[half, :, at] = total[i, other, :].astype(bf16)

    half = ((HALF, BLOCK, tiles * TILE), bf16)
    scratch = [*point_scratch(left.shape[1], tiles), pltpu.VMEM((tiles, FIELDS, TILE), f32)]
    operands = (lists, place, left, right, vector)
    return call(kernel, [half, half], operands, "product_a0", 16, 20, scratch, 2)


def product(lists, listed, first, contracted, left, right, halves, support, tail=None):
    tiles = right.shape[1]
    length = left.shape[1] * TILE
    size = tiles * TILE

    def kernel(list_ref, left_ref, right_ref, own_ref, other_ref, *rest):
        *given, left, right, vector, total = rest
        set_points(left_ref, right_ref, left, right, support)
        total[...] = jnp.zeros_like(total)
        for ref, at in ((own_ref, 0), (other_ref, FIELDS // 2)):
            rows = ref[:, :, pl.ds(0, length)].reshape(FIELDS // 2, length)
            vector[pl.ds(at, FIELDS // 2), :] = rows
        add_tiles(list_ref, listed, first, contracted, left, right, vector, total, support)
        for i in range(tiles):
            low = total[i].astype(bf16)
            at = pl.ds(i * TILE, TILE)
            if tail is not None:
                given[1][:, :, at] = low.reshape(SIDE, BLOCK, TILE)
            else:
                pair = low.reshape(2, HALF, BLOCK, TILE)
                given[0][:, :, at] = pair[0]
                given[1][:, :, at] = pair[1]
        if tail is not None:
            for peer in range(SIDE):
                given[1][peer, :, pl.ds(size, TILE)] = given[0][...]

    scratch = [
        *point_scratch(left.shape[1], tiles),
        pltpu.VMEM((FIELDS, length), bf16),
        pltpu.VMEM((tiles, FIELDS, TILE), f32),
    ]
    operands = (lists, left, right, *halves)
    if tail is not None:
        shapes = [((SIDE, BLOCK, size + TILE), bf16)]
        operands = (*operands, tail)
    else:
        shapes = [((HALF, BLOCK, size), bf16)] * 2
    return call(kernel, shapes, operands, "product", 16, listed / 18, scratch, 1)


def quarter_of(lists, place, blocks, listed):
    held = rows_of(listed)

    def kernel(place_ref, list_ref, out_ref):
        zl = place_ref[3]
        row = lax.broadcasted_iota(jnp.int32, (TILE, TILE), 0)
        col = lax.broadcasted_iota(jnp.int32, (TILE, TILE), 1)
        before = (row < col).astype(bf16)
        slot = row.astype(f32)
        lane = lax.broadcasted_iota(jnp.int32, (1, TILE), 1)
        for block in range(blocks):
            count = jnp.zeros((1, 1), f32)
            total = jnp.zeros((BLOCK, TILE), f32)
            for part in range(held):
                at = block * 2 * held + part
                i = list_ref[at : at + 1, :]
                j = list_ref[at + held : at + held + 1, :]
                real = jnp.where(lane + part * TILE < listed, 1.0, 0.0)
                flag = jnp.where(((i >> 1) & (LINE - 1)) == zl, real, 0.0)
                rank = count + jnp.dot(
                    jnp.broadcast_to(flag, (BLOCK, TILE)).astype(bf16),
                    before,
                    preferred_element_type=f32,
                )[:1]
                here = jnp.where(slot == jnp.where(flag > 0.5, rank, -1.0), 1.0, 0.0).astype(bf16)
                lines = [((i >> 3) * 2 + (i & 1)).astype(f32), j.astype(f32)]
                lines.append(jnp.zeros((BLOCK - 2, TILE), f32))
                lines = jnp.concatenate(lines, axis=0).astype(bf16)
                total += lax.dot_general(
                    lines, here, (((1,), (1,)), ((), ())), preferred_element_type=f32
                )
                count += jnp.sum(flag, axis=1, keepdims=True)
            at = pl.ds(block * TILE, TILE)
            rows = jnp.where(lane.astype(f32) < count, total[0:1], float(QUARTER))
            groups = jnp.broadcast_to((count + (GROUP - 1)) * (1.0 / GROUP), (1, TILE))
            out_ref[0:1, at] = rows.astype(jnp.int32)
            out_ref[1:2, at] = total[1:2].astype(jnp.int32)
            out_ref[2:3, at] = groups.astype(jnp.int32)
            out_ref[3:, at] = jnp.zeros((BLOCK - 3, TILE), jnp.int32)

    shapes = [((BLOCK, blocks * TILE), jnp.int32)]
    return call(kernel, shapes, (place, lists), "quarter_of", 8, 3, (), 1)


def dense_block(lists, block, left, right, support):
    cols, rows = left.shape[1], right.shape[1]

    def kernel(list_ref, left_ref, right_ref, out_ref, left, right):
        set_points(left_ref, right_ref, left, right, support)
        out_ref[...] = jnp.zeros_like(out_ref)

        def step(g, carry):
            for u in range(GROUP):
                i = list_ref[0, block * TILE + g * GROUP + u]
                j = list_ref[1, block * TILE + g * GROUP + u]
                out_ref[at_tile(j), at_tile(i)] = wendland(
                    (left[0, j], left[1, j]), (right[0, i], right[1, i]), support
                )
            return carry

        lax.fori_loop(0, list_ref[2, block * TILE], step, 0)

    shapes = [((cols * TILE, rows * TILE), bf16)]
    scratch = point_scratch(cols, rows)
    return call(kernel, shapes, (lists, left, right), "dense_block", 12, 3, scratch, 1)


def product_dense(matrices, own, other):
    count = len(matrices)
    length, width = matrices[0].shape
    size = QUARTER * TILE

    def kernel(*refs):
        given, (own_ref, other_ref, out_ref, held, sems, vector, total) = refs[:count], refs[count:]
        copies = [pltpu.make_async_copy(given[q], held.at[q], sems.at[q]) for q in range(count)]
        for copy in copies:
            copy.start()
        for ref, first in ((own_ref, 0), (other_ref, FIELDS // 2)):
            for chip in range(HALF):
                for zl in range(LINE):
                    at = pl.ds(first + chip * BLOCK, BLOCK)
                    part = ref[chip * LINE + zl, :, pl.ds(0, length)]
                    vector[at, pl.ds(zl * length, length)] = part
        for q, copy in enumerate(copies):
            copy.wait()
            lines = vector[:, pl.ds(q * length, length)]
            for t in range(0, size, 2 * TILE):
                at = pl.ds(t, 2 * TILE)
                part = jnp.dot(lines, held[q, :, at], preferred_element_type=f32)
                if q == 0:
                    total[:, at] = part
                elif q < count - 1:
                    total[:, at] += part
                else:
                    out_ref[t // (2 * TILE)] = (total[:, at] + part).astype(bf16)

    return pl.pallas_call(
        kernel,
        out_shape=jax.ShapeDtypeStruct((QUARTER // 2, FIELDS, 2 * TILE), bf16),
        in_specs=[HBM] * count + [VMEM] * 2,
        out_specs=VMEM,
        scratch_shapes=[
            pltpu.VMEM((count, length, width), bf16),
            pltpu.SemaphoreType.DMA((count,)),
            pltpu.VMEM((FIELDS, count * length), bf16),
            pltpu.VMEM((FIELDS, size), f32),
        ],
        compiler_params=room(20),
        cost_estimate=hint(4),
        name="product_dense",
    )(*(pltpu.with_memory_space_constraint(m, pltpu.HBM) for m in matrices), own, other)


def all_pairs(left, right, support):
    rows, cols = left.shape[1], right.shape[1]

    def kernel(left_ref, right_ref, out_ref):
        stretch = stretch_of(support)
        ys = [jnp.broadcast_to(left_ref[a, 0] * stretch, (TILE, TILE)).T for a in range(2)]
        for j in range(cols):
            out_ref[:, pl.ds(j * TILE, TILE)] = wendland(
                ys, (right_ref[0, j] * stretch, right_ref[1, j] * stretch), support
            )

    return pl.pallas_call(
        kernel,
        out_shape=jax.ShapeDtypeStruct((rows * TILE, cols * TILE), bf16),
        grid=(rows,),
        in_specs=[pl.BlockSpec((2, 1, 1, TILE), lambda i: (0, i, 0, 0)), VMEM],
        out_specs=pl.BlockSpec((TILE, cols * TILE), lambda i: (i, 0)),
        compiler_params=room(8),
        cost_estimate=hint(6),
        name="all_pairs",
    )(left, right)


def sum_of(arrived):
    _, rows, n = arrived.shape

    def kernel(arrived_ref, out_ref):
        for t in range(0, n, 4 * TILE):
            at = pl.ds(t, 4 * TILE)
            out_ref[:, at] = arrived_ref[:, :, at].astype(f32).sum(axis=0).astype(bf16)

    return call(kernel, [((rows, n), bf16)], (arrived,), "sum_of", 8, 1)


def residual_of(here, there, scale):
    rows, n = here.shape

    def kernel(here_ref, there_ref, out_ref):
        squares = jnp.zeros((1, TILE), f32)
        for t in range(n // TILE):
            at = pl.ds(t * TILE, TILE)
            part = scale * (here_ref[:, at].astype(f32) + there_ref[:, at].astype(f32))
            squares += jnp.sum(part * part, axis=0, keepdims=True)
            low = part.astype(bf16)
            for chip in range(LINE):
                out_ref[chip, :, at] = low
        tail = three_rows(squares)
        for chip in range(LINE):
            out_ref[chip, pl.ds(0, BLOCK), pl.ds(n, TILE)] = tail
            out_ref[chip, pl.ds(BLOCK, BLOCK), pl.ds(n, TILE)] = jnp.zeros_like(tail)

    shapes = [((LINE, rows, n + TILE), bf16)]
    return call(kernel, shapes, (here, there), "residual_of", 8, 1)


def three_rows(x):
    high = x.astype(bf16).astype(f32)
    rest = x - high
    middle = rest.astype(bf16).astype(f32)
    rows = [high, middle, rest - middle, jnp.zeros((BLOCK - 3, TILE), f32)]
    return jnp.concatenate(rows, axis=0).astype(bf16)


def mid_of(arrived, scale):
    peers, _, n = arrived.shape
    n = n - TILE

    def kernel(arrived_ref, out_ref, low_ref):
        part = scale * arrived_ref[:, :, pl.ds(0, n)].astype(f32).sum(axis=0)
        out_ref[...] = part
        low = part.astype(bf16)
        for peer in range(peers):
            low_ref[peer] = low

    shapes = [((BLOCK, n), f32), ((peers, BLOCK, n), bf16)]
    return call(kernel, shapes, (arrived,), "mid_of", 8, 1)


def chunks_of(matrix_ref, held, sems):
    chunks = sems.shape[0]
    size = matrix_ref.shape[0] // chunks
    rows = [pl.ds(q * size, size) for q in range(chunks)]
    return [
        pltpu.make_async_copy(matrix_ref.at[r], held.at[r], sems.at[q]) for q, r in enumerate(rows)
    ]


def call_on_matrix(kernel, shape, kind, matrix, operands, name, scratch):
    chunks = 4
    return pl.pallas_call(
        kernel,
        out_shape=jax.ShapeDtypeStruct(shape, kind),
        in_specs=[HBM] + [VMEM] * len(operands),
        out_specs=VMEM,
        scratch_shapes=[
            pltpu.VMEM(matrix.shape, bf16),
            pltpu.SemaphoreType.DMA((chunks,)),
            *scratch,
        ],
        compiler_params=room(12),
        cost_estimate=hint(3),
        name=name,
    )(pltpu.with_memory_space_constraint(matrix, pltpu.HBM), *operands)


def coarse_product(matrix, arrived, mid_data, scale):
    rows, cols = matrix.shape

    def kernel(matrix_ref, arrived_ref, mid_ref, out_ref, held, sems, turned_ref):
        copies = chunks_of(matrix_ref, held, sems)
        for copy in copies:
            copy.start()
        whole = (scale * arrived_ref[...].astype(f32).sum(axis=0)).astype(bf16).astype(f32)
        whole = mid_ref[...] - 0.5 * whole
        for t in range(cols // TILE):
            lines = whole[:, t * TILE : (t + 1) * TILE]
            full = jnp.concatenate([lines, jnp.zeros((TILE - BLOCK, TILE), f32)], axis=0)
            turned_ref[pl.ds(t * TILE, TILE), :] = full.T.astype(bf16)
        each = rows // TILE // len(copies)
        for c, copy in enumerate(copies):
            copy.wait()
            for q in range(c * each, (c + 1) * each):
                part = jnp.dot(
                    held[pl.ds(q * TILE, TILE), :], turned_ref[...], preferred_element_type=f32
                )
                out_ref[q] = part.T[:BLOCK, :]

    shape = (rows // TILE, BLOCK, TILE)
    scratch = [pltpu.VMEM((cols, TILE), bf16)]
    operands = (arrived, mid_data)
    return call_on_matrix(kernel, shape, f32, matrix, operands, "coarse_product", scratch)


def coarse_data_of(arrived, own, other, scale):
    peers = arrived.shape[0]
    n = own.shape[2] - TILE

    def kernel(arrived_ref, own_ref, other_ref, out_ref):
        data = (scale * arrived_ref[...].sum(axis=0)).astype(bf16)
        squares = jnp.zeros((1, TILE), f32)
        for ref in (own_ref, other_ref):
            tails = ref[...].astype(f32).sum(axis=0)
            squares += jnp.sum(tails, axis=0, keepdims=True)
        tail = three_rows(squares)
        for peer in range(peers):
            out_ref[peer, 0] = data
            out_ref[peer, 1] = tail

    tails = (own[:, :, n:], other[:, :, n:])
    shapes = [((peers, 2, BLOCK, TILE), bf16)]
    return call(kernel, shapes, (arrived, *tails), "coarse_data_of", 8, 1)


def halfway_of(gathered_data, factor_down):
    peers = gathered_data.shape[0]

    def kernel(data_ref, factor_ref, out_ref):
        total = jnp.zeros((BLOCK, TILE), f32)
        for q in range(peers // 2):
            pair = jnp.concatenate([data_ref[2 * q, 0], data_ref[2 * q + 1, 0]], axis=1)
            rows = factor_ref[pl.ds(q * 2 * TILE, 2 * TILE), :]
            total += jnp.dot(pair, rows, preferred_element_type=f32)
        low = total.astype(bf16)
        for peer in range(peers):
            out_ref[peer] = low

    shapes = [((peers, BLOCK, TILE), bf16)]
    return call(kernel, shapes, (gathered_data, factor_down), "halfway_of", 8, 1)


def coarse_coef_of(halfway, factor_across):
    peers = halfway.shape[0]

    def kernel(half_ref, factor_ref, out_ref):
        total = jnp.zeros((BLOCK, TILE), f32)
        for q in range(peers):
            total += lax.dot_general(
                half_ref[q], factor_ref[q], (((1,), (1,)), ((), ())), preferred_element_type=f32
            )
        low = total.astype(bf16)
        for peer in range(peers):
            out_ref[peer] = low

    shapes = [((peers, BLOCK, TILE), bf16)]
    return call(kernel, shapes, (halfway, factor_across), "coarse_coef_of", 8, 1)


def prolong(matrix, coarse_coef, place, mid_data, scale):
    rows, cols = matrix.shape
    two = 2 * TILE

    def kernel(matrix_ref, coef_ref, low_ref, mid_ref, out_ref, held, sems):
        copies = chunks_of(matrix_ref, held, sems)
        for copy in copies:
            copy.start()
        for chip in range(HALF):
            for zl in range(LINE):
                out_ref[chip * LINE + zl, :, pl.ds(cols, TILE)] = low_ref[chip]
        total = jnp.zeros((BLOCK, cols), f32)
        each = rows // two // len(copies)
        for c, copy in enumerate(copies):
            copy.wait()
            for q in range(c * each, (c + 1) * each):
                pair = jnp.concatenate([coef_ref[2 * q], coef_ref[2 * q + 1]], axis=1)
                total += jnp.dot(pair, held[pl.ds(q * two, two), :], preferred_element_type=f32)
        low = (0.5 * mid_ref[...] + scale * total).astype(bf16)
        for chip in range(HALF * LINE):
            out_ref[chip, :, pl.ds(0, cols)] = low

    sent = coarse_coef.reshape(HALF, 2, BLOCK, TILE)
    sent = jnp.where(place[3] % 2 == 0, sent[:, 0], sent[:, 1])
    shape = (HALF * LINE, BLOCK, cols + TILE)
    operands = (coarse_coef, sent, mid_data)
    return call_on_matrix(kernel, shape, bf16, matrix, operands, "prolong", ())


def fine_of(arrived, data, core, scale):
    n = arrived.shape[2]

    def kernel(core_ref, arrived_ref, data_ref, out_ref, summed):
        me = core_ref[0]
        summed[...] = arrived_ref[...].astype(f32).sum(axis=0)
        rows = []
        for block in range(SIDE):
            at = ((block % 2) ^ me) * HALF + block // 2
            rows.append(summed[pl.ds(pl.multiple_of(at * BLOCK, BLOCK), BLOCK), :])
        whole = jnp.concatenate(rows, axis=0)
        for t in range(n // TILE):
            at = pl.ds(t * TILE, TILE)
            data = data_ref[at, :].astype(f32)
            out_ref[at, :] = 0.5 * data + scale * whole[:, t * TILE : (t + 1) * TILE].T

    scratch = [pltpu.VMEM((FIELDS, n), f32)]
    return call(kernel, [((n, FIELDS), f32)], (core, arrived, data), "fine_of", 8, 2, scratch, 1)


def in_field_order(x, core):
    n = x.shape[-1]
    x = jnp.where(core == 0, x, x[::-1])
    return x.transpose(3, 1, 0, 2).reshape(n, FIELDS)


def scale_of(tiles, listed):
    return (tiles * TILE / (SIDE * listed * TILE * TILE)) ** 0.5


def per_device(values, points0, points1, points2, tiles_a0, tiles_e1, tiles_a1, factor):
    core = lax.axis_index("k")
    col_id = lax.axis_index(COL)
    row_id = lax.axis_index(ROW)
    rows_fine, fields = values.shape
    rows_mid = points1.shape[1]
    rows_coarse = points2.shape[1]
    coarse = rows_coarse * SIDE
    share = rows_fine // SIDE
    tiles_fine, tiles_mid = rows_fine // TILE, rows_mid // TILE
    list_a0, list_e1, list_a1 = tiles_a0[0, 0], tiles_e1[0, 0], tiles_a1[0, 0]
    scale_a0 = scale_of(tiles_fine, list_a0.shape[1])
    scale_e1 = scale_of(tiles_fine, list_e1.shape[1])
    scale_a1 = scale_of(tiles_mid, list_a1.shape[1])
    scale_e2 = (1.0 / (rows_mid * SIDE)) ** 0.5

    listed_a0, listed_e1, listed_a1 = (a.shape[1] for a in (list_a0, list_e1, list_a1))

    first_e1 = 2 * rows_of(listed_a0)
    first_a1 = first_e1 + 2 * rows_of(listed_e1)

    own_e1 = in_rows(list_e1)
    there = turned(packed(points0, points1, (list_a0, list_e1, list_a1), factor))
    local = [points2, jnp.zeros((SIDE - 2, TILE), bf16), points1.reshape(2 * tiles_mid, TILE)]
    local = jnp.concatenate(local, axis=0)
    x_id, zl_id = lax.axis_index("x"), lax.axis_index("zl")
    place = jnp.stack([core, row_id, col_id, zl_id, x_id]).astype(jnp.int32)
    fine_here = points0.astype(f32).reshape(2, tiles_fine, 1, TILE)
    mid_here = points1.astype(f32).reshape(2, tiles_mid, 1, TILE)
    tail = jnp.pad(own_e1, ((0, BLOCK - own_e1.shape[0]), (0, 0))).astype(bf16)
    there, vector, local, fine_here, mid_here, tail, place = lax.optimization_barrier(
        (there, values.T, local, fine_here, mid_here, tail, place)
    )
    fine_there, mid_there, lists, common = unpacked(
        there, factor, local, tiles_fine, tiles_mid, first_a1 + 2 * rows_of(listed_a1)
    )

    common = lax.all_gather(common, ROW, axis=0)
    own, other = product_a0(lists, place, fine_here, fine_there, vector, listed_a0)
    pair = pair_sum(own, other).reshape(LINE, 2 * BLOCK, rows_fine)
    summed = sum_of(exchanged(pair, "y"))
    swapped = lax.ppermute(summed, "zh", [(0, 1), (1, 0)])
    fine_own = exchanged(residual_of(summed, swapped, -0.5 * scale_a0), "y")
    fine_own = fine_own.reshape(HALF, BLOCK, rows_fine + TILE)
    fine_other = from_partner(fine_own)

    restricted = product(
        lists, listed_e1, first_e1, 0, fine_there, mid_here, (fine_own, fine_other), support_mid, tail
    )
    common, fine_later, mid_later = lax.optimization_barrier(
        (common, fine_here, mid_there, restricted)
    )[:3]
    factor_down, factor_across, centres, mid_line = split_common(place, common, tiles_mid)
    coarse_kernel = all_pairs(centres, mid_later, support_coarse)
    fine_quarter = fine_later.reshape(2, QUARTER // 2, LINE, 2, 1, TILE)
    fine_quarter = lax.dynamic_index_in_dim(fine_quarter, zl_id, 2, keepdims=False)
    fine_quarter = fine_quarter.reshape(2, QUARTER, 1, TILE)
    fine_quarter = jnp.pad(fine_quarter, ((0, 0), (0, 1), (0, 0), (0, 0)), constant_values=8.0)
    restricted, coarse_kernel, factor_down, factor_across, mid_line, fine_quarter = (
        lax.optimization_barrier(
            (
                exchanged(restricted, COL),
                coarse_kernel,
                factor_down,
                factor_across,
                mid_line,
                fine_quarter,
            )
        )
    )
    mid_share, mid_all = mid_of(restricted, scale_e1)
    line_lists = lax.dynamic_slice_in_dim(restricted[:, :, rows_mid:], x_id * LINE, LINE, 0)
    line_lists = line_lists[:, : own_e1.shape[0]].reshape(-1, TILE).astype(jnp.int32)
    line_lists = quarter_of(line_lists, place, LINE, listed_e1)
    mid_all, mid_data, line_lists = lax.optimization_barrier(
        (exchanged(mid_all, COL), turned_blocks(mid_share), line_lists)
    )

    mid_halves = (mid_all[:HALF], mid_all[HALF:])
    mid_own, mid_other = product(
        lists, listed_a1, first_a1, 1, mid_here, mid_there, mid_halves, support_mid
    )
    def e1_block(lists, q):
        points = mid_line[:, q * tiles_mid : (q + 1) * tiles_mid]
        return dense_block(lists, q, points, fine_quarter, support_mid)

    pair, lists_then = lax.optimization_barrier((pair_sum(mid_own, mid_other), line_lists))
    arrived, first = lax.optimization_barrier((exchanged(pair, YZ), e1_block(lists_then, 0)))
    coarse_part, lists_then = lax.optimization_barrier(
        (coarse_product(coarse_kernel, arrived, mid_data, scale_a1), line_lists)
    )
    arrived, second = lax.optimization_barrier(
        (exchanged(coarse_part, COL), e1_block(lists_then, 1))
    )
    coarse_data, lists_then = lax.optimization_barrier(
        (coarse_data_of(arrived, fine_own, fine_other, scale_e2), line_lists)
    )
    coarse_data, third = lax.optimization_barrier(
        (exchanged(coarse_data, COL), e1_block(lists_then, 2))
    )
    halfway, lists_then = lax.optimization_barrier(
        (halfway_of(coarse_data, factor_down), line_lists)
    )
    halfway, fourth = lax.optimization_barrier((exchanged(halfway, COL), e1_block(lists_then, 3)))
    coarse_all = exchanged(coarse_coef_of(halfway, factor_across), COL)

    new_own = exchanged(prolong(coarse_kernel, coarse_all, place, mid_data, scale_e2), YZL)
    new_other = from_partner(new_own)
    fine_part = product_dense((first, second, third, fourth), new_own, new_other)
    fine_part, new_own, new_other = lax.optimization_barrier((fine_part, new_own, new_other))
    own_data = lax.dynamic_slice_in_dim(values, col_id * share, share, 0)
    fine_coef = fine_of(exchanged(fine_part, "x"), own_data, place, scale_e1)

    def from_line(zl, at, size):
        both = jnp.stack([new_own, new_other])[..., at : at + size]
        both = both.reshape(2, HALF, LINE, BLOCK, size)
        both = lax.dynamic_index_in_dim(both, zl, 2, keepdims=False)
        return in_field_order(both.astype(f32), core)

    mid_coef = from_line(zl_id, 0, rows_mid)
    coarse_coef = from_line(core, rows_mid, rows_coarse)
    norm = coarse_data[:, 1].astype(f32).sum() / (rows_fine * SIDE * fields)
    return (fine_coef, mid_coef, coarse_coef, jnp.stack([norm]))


def solution(mesh):
    fine_mesh = Mesh(mesh.devices.reshape(4, 2, 2, 4, 4), ALL)
    return jax.shard_map(
        per_device,
        mesh=fine_mesh,
        in_specs=(
            P(ROW, None),
            P(None, ROW),
            P(None, ROW),
            P(None, ROW),
            P(ROW, COL, None, None),
            P(ROW, COL, None, None),
            P(ROW, COL, None, None),
            P(ROW, COL),
        ),
        out_specs=(P(ALL, None), P(COL, None), P(ROW, None), P()),
        check_vma=False,
    )
```

```python
import jax
import jax.numpy as jnp
from jax import lax
from jax.experimental import pallas as pl
from jax.experimental.pallas import tpu as pltpu
from jax.sharding import Mesh
from jax.sharding import PartitionSpec as P

TILE = 128
SIDE = 16
HALF = 8
LINE = 4
QUARTER = 8
BLOCK = 8
FIELDS = SIDE * BLOCK
GROUP = 16

support_fine = 0.35
support_mid = 0.55
support_coarse = 0.8

ROW = ("y", "zh", "k")
YZ = ("y", "zh")
YZL = ("y", "zh", "zl")
COL = ("x", "zl")
ALL = ROW + COL

bf16 = jnp.bfloat16
f32 = jnp.float32

VMEM = pl.BlockSpec(memory_space=pltpu.VMEM)
SMEM = pl.BlockSpec(memory_space=pltpu.SMEM)
HBM = pl.BlockSpec(memory_space=pltpu.HBM)


def room(mebibytes):
    return pltpu.CompilerParams(vmem_limit_bytes=mebibytes * 1024 * 1024)


def hint(microseconds):
    return pl.CostEstimate(
        flops=0, transcendentals=0, bytes_accessed=int(microseconds * 3.0e6)
    )


def turned(x):
    pairs = [(c * SIDE + r, r * SIDE + c) for r in range(SIDE) for c in range(SIDE)]
    return lax.ppermute(x, ALL, pairs)


def place_of_block(block, core):
    return ((block % 2) ^ core) * HALF + block // 2


def turned_blocks(x):
    pairs = [
        (c * SIDE + place_of_block(r, c % 2), r * SIDE + c) for r in range(SIDE) for c in range(SIDE)
    ]
    return lax.ppermute(x, ALL, pairs)


def from_partner(x):
    return lax.ppermute(x, "k", [(0, 1), (1, 0)])


def exchanged(x, axes):
    return lax.all_to_all(x, axes, split_axis=0, concat_axis=0, tiled=True)


def pair_sum(own, other):
    return (own.astype(f32) + from_partner(other).astype(f32)).astype(bf16)


def stretch_of(support):
    return (4.0 / support**5) ** 0.2


def wendland(left, right, support):
    across, upward = left[0] - right[0], left[1] - right[1]
    square = jnp.maximum(across * across + upward * upward, 1e-30)
    edge = support * stretch_of(support)
    margin = jnp.maximum(edge - square * lax.rsqrt(square), 0.0)
    margin2 = margin * margin
    ratio = 5.0 / edge**4
    return (margin2 * margin2 * (ratio - margin)).astype(bf16)


def at_tile(i):
    return pl.ds(pl.multiple_of(i * TILE, TILE), TILE)


def call(kernel, shapes, operands, name, mebibytes, microseconds, scratch=(), scalars=0):
    out = pl.pallas_call(
        kernel,
        out_shape=[jax.ShapeDtypeStruct(shape, kind) for shape, kind in shapes],
        in_specs=[SMEM] * scalars + [VMEM] * (len(operands) - scalars),
        out_specs=[VMEM] * len(shapes),
        scratch_shapes=list(scratch),
        compiler_params=room(mebibytes),
        cost_estimate=hint(microseconds),
        name=name,
    )(*operands)
    return out if len(shapes) > 1 else out[0]


def rows_of(listed):
    return -(-listed // TILE)


def in_rows(listing):
    rows = rows_of(listing.shape[1])
    padded = jnp.pad(listing, ((0, 0), (0, rows * TILE - listing.shape[1])))
    return padded.reshape(2 * rows, TILE)


def packed(points0, points1, lists, factor):
    fine, mid = points0.shape[1] // TILE, points1.shape[1] // TILE
    used = 2 * (fine + mid) + sum(2 * rows_of(a.shape[1]) for a in lists)
    above = -(-used // SIDE) * SIDE

    operands = (points0, points1, *lists, factor)
    count = len(operands)

    def kernel(*refs):
        given, out_ref, held, sems = refs[:count], refs[count], refs[count + 1 : -1], refs[-1]
        copies = [
            pltpu.make_async_copy(ref, to, sems.at[n]) for n, (ref, to) in enumerate(zip(given, held))
        ]
        for copy in copies:
            copy.start()
        for copy in copies:
            copy.wait()
        lines = []
        for ref in held[:-1]:
            whole = ref[...].astype(f32)
            length = whole.shape[1]
            short = -length % TILE
            if short:
                whole = jnp.concatenate([whole, jnp.zeros((2, short), f32)], axis=1)
            for a in range(2):
                lines += [whole[a : a + 1, t : t + TILE] for t in range(0, length, TILE)]
        if above > used:
            lines.append(jnp.zeros((above - used, TILE), f32))
        out_ref[pl.ds(0, above), :] = jnp.concatenate(lines, axis=0).astype(bf16)
        out_ref[pl.ds(above, TILE), :] = held[-1][...]

    return pl.pallas_call(
        kernel,
        out_shape=jax.ShapeDtypeStruct((above + TILE, TILE), bf16),
        in_specs=[HBM] * count,
        out_specs=VMEM,
        scratch_shapes=[pltpu.VMEM(a.shape, a.dtype) for a in operands]
        + [pltpu.SemaphoreType.DMA((count,))],
        compiler_params=room(8),
        cost_estimate=hint(1),
        name="packed",
    )(*(pltpu.with_memory_space_constraint(a, pltpu.HBM) for a in operands))


def unpacked(there, factor, local, fine, mid, listed):
    used = 2 * (fine + mid) + listed
    above = -(-used // SIDE) * SIDE
    size = 2 * TILE + local.shape[0]

    def kernel(there_ref, factor_ref, local_ref, fine_ref, mid_ref, list_ref, common_ref):
        lines = there_ref[pl.ds(0, above), :].astype(f32)
        at = 0
        for ref, tiles in ((fine_ref, fine), (mid_ref, mid)):
            for a in range(2):
                for t in range(tiles):
                    ref[a, t] = lines[at : at + 1]
                    at += 1
        list_ref[...] = lines[at : at + listed].astype(jnp.int32)
        for chip in range(HALF):
            common_ref[chip, pl.ds(0, TILE), :] = factor_ref[...]
            common_ref[chip, pl.ds(TILE, TILE), :] = there_ref[pl.ds(above, TILE), :]
            common_ref[chip, pl.ds(2 * TILE, local.shape[0]), :] = local_ref[...]

    shapes = [
        ((2, fine, 1, TILE), f32),
        ((2, mid, 1, TILE), f32),
        ((listed, TILE), jnp.int32),
        ((HALF, size, TILE), bf16),
    ]
    return call(kernel, shapes, (there, factor, local), "unpacked", 8, 1)


def in_row_order(place, common, partner, mid):
    at_centres, at_mid = 2 * TILE, 2 * TILE + SIDE

    def kernel(place_ref, own_ref, other_ref, down_ref, across_ref, centre_ref, line_ref):
        core, x = place_ref[0], place_ref[4]

        def rows(chip, of_core, at, size):
            own, other = own_ref[chip, pl.ds(at, size), :], other_ref[chip, pl.ds(at, size), :]
            return jnp.where(core == of_core, own.astype(f32), other.astype(f32))

        for block in range(SIDE):
            chip, of_core = block // 2, block % 2
            down_ref[pl.ds(block * TILE, TILE), :] = rows(chip, of_core, 0, TILE).astype(bf16)
            across_ref[block] = rows(chip, of_core, TILE, TILE).astype(bf16)
            lines = rows(chip, of_core, at_centres, SIDE)
            for a in range(2):
                centre_ref[a, block] = lines[a : a + 1]
        for q in range(LINE):
            lines = rows(x * (LINE // 2) + q // 2, q % 2, at_mid, 2 * mid)
            for a in range(2):
                for t in range(mid):
                    line_ref[a, q * mid + t] = lines[a * mid + t : a * mid + t + 1]

    shapes = [
        ((SIDE * TILE, TILE), bf16),
        ((SIDE, TILE, TILE), bf16),
        ((2, SIDE, 1, TILE), f32),
        ((2, LINE * mid, 1, TILE), f32),
    ]
    return call(kernel, shapes, (place, common, partner), "in_row_order", 8, 2, (), 1)


def set_points(left_ref, right_ref, left, right, support):
    stretch = stretch_of(support)
    for axis in range(2):
        for t in range(left.shape[1]):
            row = left_ref[axis, t] * stretch
            left[axis, t] = jnp.broadcast_to(row, (TILE, TILE)).T
        for t in range(right.shape[1]):
            right[axis, t] = right_ref[axis, t] * stretch


def point_scratch(left, right):
    return [pltpu.VMEM((2, left, TILE, TILE), f32), pltpu.VMEM((2, right, 1, TILE), f32)]


def add_tiles(list_ref, listed, first, contracted, left, right, vector, total, support):
    rows = rows_of(listed)
    group = 2 * GROUP
    steps = TILE // group
    line_j = first + contracted * rows
    line_i = first + (1 - contracted) * rows

    def step(g, carry):
        row, lane = g // steps, g % steps * group
        products = []
        for u in range(group):
            j = list_ref[line_j + row, lane + u]
            i = list_ref[line_i + row, lane + u]
            tile = wendland((left[0, j], left[1, j]), (right[0, i], right[1, i]), support)
            product = jnp.dot(vector[:, at_tile(j)], tile, preferred_element_type=f32)
            products.append((i, product))
        for i, product in products:
            total[i] += product
        return carry

    lax.fori_loop(0, listed // group, step, 0)


def product_a0(lists, place, left, right, vector, listed):
    tiles = right.shape[1]

    def kernel(
        list_ref, place_ref, left_ref, right_ref, vector_ref, own_ref, other_ref, left, right, total
    ):
        set_points(left_ref, right_ref, left, right, support_fine)
        me = place_ref[0]
        weight = jnp.where(place_ref[1] == place_ref[2], -2.0 / scale_of(tiles, listed), 0.0)
        for i in range(tiles):
            at = pl.ds(i * TILE, TILE)
            total[i] = vector_ref[:, at].astype(f32) * weight
        add_tiles(list_ref, listed, 0, 1, left, right, vector_ref, total, support_fine)
        for half in range(HALF):
            for i in range(tiles):
                at = pl.ds(i * TILE, TILE)
                own = pl.ds(pl.multiple_of((2 * half + me) * BLOCK, BLOCK), BLOCK)
                other = pl.ds(pl.multiple_of((2 * half + 1 - me) * BLOCK, BLOCK), BLOCK)
                own_ref[half, :, at] = total[i, own, :].astype(bf16)
                other_ref[half, :, at] = total[i, other, :].astype(bf16)

    half = ((HALF, BLOCK, tiles * TILE), bf16)
    scratch = [*point_scratch(left.shape[1], tiles), pltpu.VMEM((tiles, FIELDS, TILE), f32)]
    operands = (lists, place, left, right, vector)
    return call(kernel, [half, half], operands, "product_a0", 16, 20, scratch, 2)


def product(lists, listed, first, contracted, left, right, halves, support, tail=None):
    tiles = right.shape[1]
    length = left.shape[1] * TILE
    size = tiles * TILE

    def kernel(list_ref, left_ref, right_ref, own_ref, other_ref, *rest):
        *given, left, right, vector, total = rest
        set_points(left_ref, right_ref, left, right, support)
        total[...] = jnp.zeros_like(total)
        for ref, at in ((own_ref, 0), (other_ref, FIELDS // 2)):
            rows = ref[:, :, pl.ds(0, length)].reshape(FIELDS // 2, length)
            vector[pl.ds(at, FIELDS // 2), :] = rows
        add_tiles(list_ref, listed, first, contracted, left, right, vector, total, support)
        for i in range(tiles):
            low = total[i].astype(bf16)
            at = pl.ds(i * TILE, TILE)
            if tail is not None:
                given[1][:, :, at] = low.reshape(SIDE, BLOCK, TILE)
            else:
                pair = low.reshape(2, HALF, BLOCK, TILE)
                given[0][:, :, at] = pair[0]
                given[1][:, :, at] = pair[1]
        if tail is not None:
            for peer in range(SIDE):
                given[1][peer, :, pl.ds(size, TILE)] = given[0][...]

    scratch = [
        *point_scratch(left.shape[1], tiles),
        pltpu.VMEM((FIELDS, length), bf16),
        pltpu.VMEM((tiles, FIELDS, TILE), f32),
    ]
    operands = (lists, left, right, *halves)
    if tail is not None:
        shapes = [((SIDE, BLOCK, size + TILE), bf16)]
        operands = (*operands, tail)
    else:
        shapes = [((HALF, BLOCK, size), bf16)] * 2
    return call(kernel, shapes, operands, "product", 16, listed / 18, scratch, 1)


def quarter_of(lists, place, blocks, listed):
    held = rows_of(listed)

    def kernel(place_ref, list_ref, out_ref):
        zl = place_ref[3]
        row = lax.broadcasted_iota(jnp.int32, (TILE, TILE), 0)
        col = lax.broadcasted_iota(jnp.int32, (TILE, TILE), 1)
        before = (row < col).astype(bf16)
        slot = row.astype(f32)
        lane = lax.broadcasted_iota(jnp.int32, (1, TILE), 1)
        for block in range(blocks):
            count = jnp.zeros((1, 1), f32)
            total = jnp.zeros((BLOCK, TILE), f32)
            for part in range(held):
                at = block * 2 * held + part
                i = list_ref[at : at + 1, :]
                j = list_ref[at + held : at + held + 1, :]
                real = jnp.where(lane + part * TILE < listed, 1.0, 0.0)
                flag = jnp.where(((i >> 1) & (LINE - 1)) == zl, real, 0.0)
                rank = count + jnp.dot(
                    jnp.broadcast_to(flag, (BLOCK, TILE)).astype(bf16),
                    before,
                    preferred_element_type=f32,
                )[:1]
                here = jnp.where(slot == jnp.where(flag > 0.5, rank, -1.0), 1.0, 0.0).astype(bf16)
                lines = [((i >> 3) * 2 + (i & 1)).astype(f32), j.astype(f32)]
                lines.append(jnp.zeros((BLOCK - 2, TILE), f32))
                lines = jnp.concatenate(lines, axis=0).astype(bf16)
                total += lax.dot_general(
                    lines, here, (((1,), (1,)), ((), ())), preferred_element_type=f32
                )
                count += jnp.sum(flag, axis=1, keepdims=True)
            at = pl.ds(block * TILE, TILE)
            rows = jnp.where(lane.astype(f32) < count, total[0:1], float(QUARTER))
            groups = jnp.broadcast_to((count + (GROUP - 1)) * (1.0 / GROUP), (1, TILE))
            out_ref[0:1, at] = rows.astype(jnp.int32)
            out_ref[1:2, at] = total[1:2].astype(jnp.int32)
            out_ref[2:3, at] = groups.astype(jnp.int32)
            out_ref[3:, at] = jnp.zeros((BLOCK - 3, TILE), jnp.int32)

    shapes = [((BLOCK, blocks * TILE), jnp.int32)]
    return call(kernel, shapes, (place, lists), "quarter_of", 8, 3, (), 1)


def dense_block(lists, block, left, right, support):
    cols, rows = left.shape[1], right.shape[1]

    def kernel(list_ref, left_ref, right_ref, out_ref, left, right):
        set_points(left_ref, right_ref, left, right, support)
        out_ref[...] = jnp.zeros_like(out_ref)

        def step(g, carry):
            for u in range(GROUP):
                i = list_ref[0, block * TILE + g * GROUP + u]
                j = list_ref[1, block * TILE + g * GROUP + u]
                out_ref[at_tile(j), at_tile(i)] = wendland(
                    (left[0, j], left[1, j]), (right[0, i], right[1, i]), support
                )
            return carry

        lax.fori_loop(0, list_ref[2, block * TILE], step, 0)

    shapes = [((cols * TILE, rows * TILE), bf16)]
    scratch = point_scratch(cols, rows)
    return call(kernel, shapes, (lists, left, right), "dense_block", 12, 3, scratch, 1)


def product_dense(matrices, own, other):
    count = len(matrices)
    length, width = matrices[0].shape
    size = QUARTER * TILE

    def kernel(*refs):
        given, (own_ref, other_ref, out_ref, held, sems, vector, total) = refs[:count], refs[count:]
        copies = [pltpu.make_async_copy(given[q], held.at[q], sems.at[q]) for q in range(count)]
        for copy in copies:
            copy.start()
        for ref, first in ((own_ref, 0), (other_ref, FIELDS // 2)):
            for chip in range(HALF):
                for zl in range(LINE):
                    at = pl.ds(first + chip * BLOCK, BLOCK)
                    part = ref[chip * LINE + zl, :, pl.ds(0, length)]
                    vector[at, pl.ds(zl * length, length)] = part
        for q, copy in enumerate(copies):
            copy.wait()
            lines = vector[:, pl.ds(q * length, length)]
            for t in range(0, size, 2 * TILE):
                at = pl.ds(t, 2 * TILE)
                part = jnp.dot(lines, held[q, :, at], preferred_element_type=f32)
                if q == 0:
                    total[:, at] = part
                elif q < count - 1:
                    total[:, at] += part
                else:
                    out_ref[t // (2 * TILE)] = (total[:, at] + part).astype(bf16)

    return pl.pallas_call(
        kernel,
        out_shape=jax.ShapeDtypeStruct((QUARTER // 2, FIELDS, 2 * TILE), bf16),
        in_specs=[HBM] * count + [VMEM] * 2,
        out_specs=VMEM,
        scratch_shapes=[
            pltpu.VMEM((count, length, width), bf16),
            pltpu.SemaphoreType.DMA((count,)),
            pltpu.VMEM((FIELDS, count * length), bf16),
            pltpu.VMEM((FIELDS, size), f32),
        ],
        compiler_params=room(20),
        cost_estimate=hint(4),
        name="product_dense",
    )(*(pltpu.with_memory_space_constraint(m, pltpu.HBM) for m in matrices), own, other)


def all_pairs(left, right, support):
    rows, cols = left.shape[1], right.shape[1]

    def kernel(left_ref, right_ref, out_ref):
        stretch = stretch_of(support)
        ys = [jnp.broadcast_to(left_ref[a, 0] * stretch, (TILE, TILE)).T for a in range(2)]
        for j in range(cols):
            out_ref[:, pl.ds(j * TILE, TILE)] = wendland(
                ys, (right_ref[0, j] * stretch, right_ref[1, j] * stretch), support
            )

    return pl.pallas_call(
        kernel,
        out_shape=jax.ShapeDtypeStruct((rows * TILE, cols * TILE), bf16),
        grid=(rows,),
        in_specs=[pl.BlockSpec((2, 1, 1, TILE), lambda i: (0, i, 0, 0)), VMEM],
        out_specs=pl.BlockSpec((TILE, cols * TILE), lambda i: (i, 0)),
        compiler_params=room(8),
        cost_estimate=hint(6),
        name="all_pairs",
    )(left, right)


def sum_of(arrived):
    _, rows, n = arrived.shape

    def kernel(arrived_ref, out_ref):
        for t in range(0, n, 4 * TILE):
            at = pl.ds(t, 4 * TILE)
            out_ref[:, at] = arrived_ref[:, :, at].astype(f32).sum(axis=0).astype(bf16)

    return call(kernel, [((rows, n), bf16)], (arrived,), "sum_of", 8, 1)


def residual_of(here, there, scale):
    rows, n = here.shape

    def kernel(here_ref, there_ref, out_ref):
        squares = jnp.zeros((1, TILE), f32)
        for t in range(n // TILE):
            at = pl.ds(t * TILE, TILE)
            part = scale * (here_ref[:, at].astype(f32) + there_ref[:, at].astype(f32))
            squares += jnp.sum(part * part, axis=0, keepdims=True)
            low = part.astype(bf16)
            for chip in range(LINE):
                out_ref[chip, :, at] = low
        tail = three_rows(squares)
        for chip in range(LINE):
            out_ref[chip, pl.ds(0, BLOCK), pl.ds(n, TILE)] = tail
            out_ref[chip, pl.ds(BLOCK, BLOCK), pl.ds(n, TILE)] = jnp.zeros_like(tail)

    shapes = [((LINE, rows, n + TILE), bf16)]
    return call(kernel, shapes, (here, there), "residual_of", 8, 1)


def three_rows(x):
    high = x.astype(bf16).astype(f32)
    rest = x - high
    middle = rest.astype(bf16).astype(f32)
    rows = [high, middle, rest - middle, jnp.zeros((BLOCK - 3, TILE), f32)]
    return jnp.concatenate(rows, axis=0).astype(bf16)


def mid_of(arrived, scale):
    peers, _, n = arrived.shape
    n = n - TILE

    def kernel(arrived_ref, out_ref, low_ref):
        part = scale * arrived_ref[:, :, pl.ds(0, n)].astype(f32).sum(axis=0)
        out_ref[...] = part
        low = part.astype(bf16)
        for peer in range(peers):
            low_ref[peer] = low

    shapes = [((BLOCK, n), f32), ((peers, BLOCK, n), bf16)]
    return call(kernel, shapes, (arrived,), "mid_of", 8, 1)


def chunks_of(matrix_ref, held, sems):
    chunks = sems.shape[0]
    size = matrix_ref.shape[0] // chunks
    rows = [pl.ds(q * size, size) for q in range(chunks)]
    return [
        pltpu.make_async_copy(matrix_ref.at[r], held.at[r], sems.at[q]) for q, r in enumerate(rows)
    ]


def call_on_matrix(kernel, shape, kind, matrix, operands, name, scratch):
    chunks = 4
    return pl.pallas_call(
        kernel,
        out_shape=jax.ShapeDtypeStruct(shape, kind),
        in_specs=[HBM] + [VMEM] * len(operands),
        out_specs=VMEM,
        scratch_shapes=[
            pltpu.VMEM(matrix.shape, bf16),
            pltpu.SemaphoreType.DMA((chunks,)),
            *scratch,
        ],
        compiler_params=room(12),
        cost_estimate=hint(3),
        name=name,
    )(pltpu.with_memory_space_constraint(matrix, pltpu.HBM), *operands)


def coarse_product(matrix, arrived, mid_data, scale):
    rows, cols = matrix.shape

    def kernel(matrix_ref, arrived_ref, mid_ref, out_ref, held, sems, turned_ref):
        copies = chunks_of(matrix_ref, held, sems)
        for copy in copies:
            copy.start()
        whole = (scale * arrived_ref[...].astype(f32).sum(axis=0)).astype(bf16).astype(f32)
        whole = mid_ref[...] - 0.5 * whole
        for t in range(cols // TILE):
            lines = whole[:, t * TILE : (t + 1) * TILE]
            full = jnp.concatenate([lines, jnp.zeros((TILE - BLOCK, TILE), f32)], axis=0)
            turned_ref[pl.ds(t * TILE, TILE), :] = full.T.astype(bf16)
        each = rows // TILE // len(copies)
        for c, copy in enumerate(copies):
            copy.wait()
            for q in range(c * each, (c + 1) * each):
                part = jnp.dot(
                    held[pl.ds(q * TILE, TILE), :], turned_ref[...], preferred_element_type=f32
                )
                out_ref[q] = part.T[:BLOCK, :]

    shape = (rows // TILE, BLOCK, TILE)
    scratch = [pltpu.VMEM((cols, TILE), bf16)]
    operands = (arrived, mid_data)
    return call_on_matrix(kernel, shape, f32, matrix, operands, "coarse_product", scratch)


def coarse_data_of(arrived, own, other, scale):
    peers = arrived.shape[0]
    n = own.shape[2] - TILE

    def kernel(arrived_ref, own_ref, other_ref, out_ref):
        data = (scale * arrived_ref[...].sum(axis=0)).astype(bf16)
        squares = jnp.zeros((1, TILE), f32)
        for ref in (own_ref, other_ref):
            tails = ref[...].astype(f32).sum(axis=0)
            squares += jnp.sum(tails, axis=0, keepdims=True)
        tail = three_rows(squares)
        for peer in range(peers):
            out_ref[peer, 0] = data
            out_ref[peer, 1] = tail

    tails = (own[:, :, n:], other[:, :, n:])
    shapes = [((peers, 2, BLOCK, TILE), bf16)]
    return call(kernel, shapes, (arrived, *tails), "coarse_data_of", 8, 1)


def halfway_of(gathered_data, factor_down):
    peers = gathered_data.shape[0]

    def kernel(data_ref, factor_ref, out_ref):
        total = jnp.zeros((BLOCK, TILE), f32)
        for q in range(peers // 2):
            pair = jnp.concatenate([data_ref[2 * q, 0], data_ref[2 * q + 1, 0]], axis=1)
            rows = factor_ref[pl.ds(q * 2 * TILE, 2 * TILE), :]
            total += jnp.dot(pair, rows, preferred_element_type=f32)
        low = total.astype(bf16)
        for peer in range(peers):
            out_ref[peer] = low

    shapes = [((peers, BLOCK, TILE), bf16)]
    return call(kernel, shapes, (gathered_data, factor_down), "halfway_of", 8, 1)


def coarse_coef_of(halfway, factor_across):
    peers = halfway.shape[0]

    def kernel(half_ref, factor_ref, out_ref):
        total = jnp.zeros((BLOCK, TILE), f32)
        for q in range(peers):
            total += lax.dot_general(
                half_ref[q], factor_ref[q], (((1,), (1,)), ((), ())), preferred_element_type=f32
            )
        low = total.astype(bf16)
        for peer in range(peers):
            out_ref[peer] = low

    shapes = [((peers, BLOCK, TILE), bf16)]
    return call(kernel, shapes, (halfway, factor_across), "coarse_coef_of", 8, 1)


def prolong(matrix, coarse_coef, place, mid_data, scale):
    rows, cols = matrix.shape
    two = 2 * TILE

    def kernel(matrix_ref, coef_ref, low_ref, mid_ref, out_ref, held, sems):
        copies = chunks_of(matrix_ref, held, sems)
        for copy in copies:
            copy.start()
        for chip in range(HALF):
            for zl in range(LINE):
                out_ref[chip * LINE + zl, :, pl.ds(cols, TILE)] = low_ref[chip]
        total = jnp.zeros((BLOCK, cols), f32)
        each = rows // two // len(copies)
        for c, copy in enumerate(copies):
            copy.wait()
            for q in range(c * each, (c + 1) * each):
                pair = jnp.concatenate([coef_ref[2 * q], coef_ref[2 * q + 1]], axis=1)
                total += jnp.dot(pair, held[pl.ds(q * two, two), :], preferred_element_type=f32)
        low = (0.5 * mid_ref[...] + scale * total).astype(bf16)
        for chip in range(HALF * LINE):
            out_ref[chip, :, pl.ds(0, cols)] = low

    sent = coarse_coef.reshape(HALF, 2, BLOCK, TILE)
    sent = jnp.where(place[3] % 2 == 0, sent[:, 0], sent[:, 1])
    shape = (HALF * LINE, BLOCK, cols + TILE)
    operands = (coarse_coef, sent, mid_data)
    return call_on_matrix(kernel, shape, bf16, matrix, operands, "prolong", ())


def fine_of(arrived, data, core, scale):
    n = arrived.shape[2]

    def kernel(core_ref, arrived_ref, data_ref, out_ref, summed):
        me = core_ref[0]
        summed[...] = arrived_ref[...].astype(f32).sum(axis=0)
        rows = []
        for block in range(SIDE):
            at = ((block % 2) ^ me) * HALF + block // 2
            rows.append(summed[pl.ds(pl.multiple_of(at * BLOCK, BLOCK), BLOCK), :])
        whole = jnp.concatenate(rows, axis=0)
        for t in range(n // TILE):
            at = pl.ds(t * TILE, TILE)
            data = data_ref[at, :].astype(f32)
            out_ref[at, :] = 0.5 * data + scale * whole[:, t * TILE : (t + 1) * TILE].T

    scratch = [pltpu.VMEM((FIELDS, n), f32)]
    return call(kernel, [((n, FIELDS), f32)], (core, arrived, data), "fine_of", 8, 2, scratch, 1)


def in_field_order(x, core):
    n = x.shape[-1]
    x = jnp.where(core == 0, x, x[::-1])
    return x.transpose(3, 1, 0, 2).reshape(n, FIELDS)


def scale_of(tiles, listed):
    return (tiles * TILE / (SIDE * listed * TILE * TILE)) ** 0.5


def per_device(values, points0, points1, points2, tiles_a0, tiles_e1, tiles_a1, factor):
    core = lax.axis_index("k")
    col_id = lax.axis_index(COL)
    row_id = lax.axis_index(ROW)
    rows_fine, fields = values.shape
    rows_mid = points1.shape[1]
    rows_coarse = points2.shape[1]
    coarse = rows_coarse * SIDE
    share = rows_fine // SIDE
    tiles_fine, tiles_mid = rows_fine // TILE, rows_mid // TILE
    list_a0, list_e1, list_a1 = tiles_a0[0, 0], tiles_e1[0, 0], tiles_a1[0, 0]
    scale_a0 = scale_of(tiles_fine, list_a0.shape[1])
    scale_e1 = scale_of(tiles_fine, list_e1.shape[1])
    scale_a1 = scale_of(tiles_mid, list_a1.shape[1])
    scale_e2 = (1.0 / (rows_mid * SIDE)) ** 0.5

    listed_a0, listed_e1, listed_a1 = (a.shape[1] for a in (list_a0, list_e1, list_a1))

    first_e1 = 2 * rows_of(listed_a0)
    first_a1 = first_e1 + 2 * rows_of(listed_e1)

    own_e1 = in_rows(list_e1)
    there = turned(packed(points0, points1, (list_a0, list_e1, list_a1), factor))
    local = [points2, jnp.zeros((SIDE - 2, TILE), bf16), points1.reshape(2 * tiles_mid, TILE)]
    local = jnp.concatenate(local, axis=0)
    x_id, zl_id = lax.axis_index("x"), lax.axis_index("zl")
    place = jnp.stack([core, row_id, col_id, zl_id, x_id]).astype(jnp.int32)
    fine_here = points0.astype(f32).reshape(2, tiles_fine, 1, TILE)
    mid_here = points1.astype(f32).reshape(2, tiles_mid, 1, TILE)
    tail = jnp.pad(own_e1, ((0, BLOCK - own_e1.shape[0]), (0, 0))).astype(bf16)
    there, vector, local, fine_here, mid_here, tail, place = lax.optimization_barrier(
        (there, values.T, local, fine_here, mid_here, tail, place)
    )
    fine_there, mid_there, lists, common = unpacked(
        there, factor, local, tiles_fine, tiles_mid, first_a1 + 2 * rows_of(listed_a1)
    )

    own, other = product_a0(lists, place, fine_here, fine_there, vector, listed_a0)
    pair = pair_sum(own, other).reshape(LINE, 2 * BLOCK, rows_fine)
    summed = sum_of(exchanged(pair, "y"))
    swapped = lax.ppermute(summed, "zh", [(0, 1), (1, 0)])
    fine_own = exchanged(residual_of(summed, swapped, -0.5 * scale_a0), "y")
    fine_own = fine_own.reshape(HALF, BLOCK, rows_fine + TILE)
    fine_other = from_partner(fine_own)

    common, fine_own, fine_other = lax.optimization_barrier((common, fine_own, fine_other))
    common = exchanged(common, YZ)
    restricted = product(
        lists, listed_e1, first_e1, 0, fine_there, mid_here, (fine_own, fine_other), support_mid, tail
    )
    restricted, common = lax.optimization_barrier((restricted, common))
    ordered = in_row_order(place, common, from_partner(common), tiles_mid)
    fine_quarter = fine_here.reshape(2, QUARTER // 2, LINE, 2, 1, TILE)
    fine_quarter = lax.dynamic_index_in_dim(fine_quarter, zl_id, 2, keepdims=False)
    fine_quarter = fine_quarter.reshape(2, QUARTER, 1, TILE)
    fine_quarter = jnp.pad(fine_quarter, ((0, 0), (0, 1), (0, 0), (0, 0)), constant_values=8.0)
    restricted, ordered, fine_quarter = lax.optimization_barrier(
        (exchanged(restricted, COL), ordered, fine_quarter)
    )
    factor_down, factor_across, centres, mid_line = ordered
    mid_share, mid_all = mid_of(restricted, scale_e1)
    line_lists = lax.dynamic_slice_in_dim(restricted[:, :, rows_mid:], x_id * LINE, LINE, 0)
    line_lists = line_lists[:, : own_e1.shape[0]].reshape(-1, TILE).astype(jnp.int32)
    line_lists = quarter_of(line_lists, place, LINE, listed_e1)

    def e1_block(lists, q):
        points = mid_line[:, q * tiles_mid : (q + 1) * tiles_mid]
        return dense_block(lists, q, points, fine_quarter, support_mid)

    mid_all, mid_data, line_lists, first = lax.optimization_barrier(
        (exchanged(mid_all, COL), turned_blocks(mid_share), line_lists, e1_block(line_lists, 0))
    )

    mid_halves = (mid_all[:HALF], mid_all[HALF:])
    mid_own, mid_other = product(
        lists, listed_a1, first_a1, 1, mid_here, mid_there, mid_halves, support_mid
    )
    pair, centres, mid_later = lax.optimization_barrier(
        (pair_sum(mid_own, mid_other), centres, mid_there)
    )
    arrived, coarse_kernel = lax.optimization_barrier(
        (exchanged(pair, YZ), all_pairs(centres, mid_later, support_coarse))
    )
    coarse_part, lists_then = lax.optimization_barrier(
        (coarse_product(coarse_kernel, arrived, mid_data, scale_a1), line_lists)
    )
    arrived, second = lax.optimization_barrier(
        (exchanged(coarse_part, COL), e1_block(lists_then, 1))
    )
    coarse_data, lists_then = lax.optimization_barrier(
        (coarse_data_of(arrived, fine_own, fine_other, scale_e2), line_lists)
    )
    coarse_data, third = lax.optimization_barrier(
        (exchanged(coarse_data, COL), e1_block(lists_then, 2))
    )
    halfway, lists_then = lax.optimization_barrier(
        (halfway_of(coarse_data, factor_down), line_lists)
    )
    halfway, fourth = lax.optimization_barrier((exchanged(halfway, COL), e1_block(lists_then, 3)))
    coarse_all = exchanged(coarse_coef_of(halfway, factor_across), COL)

    new_own = exchanged(prolong(coarse_kernel, coarse_all, place, mid_data, scale_e2), YZL)
    new_other = from_partner(new_own)
    fine_part = product_dense((first, second, third, fourth), new_own, new_other)
    fine_part, new_own, new_other = lax.optimization_barrier((fine_part, new_own, new_other))
    own_data = lax.dynamic_slice_in_dim(values, col_id * share, share, 0)
    fine_coef = fine_of(exchanged(fine_part, "x"), own_data, place, scale_e1)

    def from_line(zl, at, size):
        both = jnp.stack([new_own, new_other])[..., at : at + size]
        both = both.reshape(2, HALF, LINE, BLOCK, size)
        both = lax.dynamic_index_in_dim(both, zl, 2, keepdims=False)
        return in_field_order(both.astype(f32), core)

    mid_coef = from_line(zl_id, 0, rows_mid)
    coarse_coef = from_line(core, rows_mid, rows_coarse)
    norm = coarse_data[:, 1].astype(f32).sum() / (rows_fine * SIDE * fields)
    return (fine_coef, mid_coef, coarse_coef, jnp.stack([norm]))


def solution(mesh):
    fine_mesh = Mesh(mesh.devices.reshape(4, 2, 2, 4, 4), ALL)
    return jax.shard_map(
        per_device,
        mesh=fine_mesh,
        in_specs=(
            P(ROW, None),
            P(None, ROW),
            P(None, ROW),
            P(None, ROW),
            P(ROW, COL, None, None),
            P(ROW, COL, None, None),
            P(ROW, COL, None, None),
            P(ROW, COL),
        ),
        out_specs=(P(ALL, None), P(COL, None), P(ROW, None), P()),
        check_vma=False,
    )
```

```python
import jax
import jax.numpy as jnp
from jax import lax
from jax.experimental import pallas as pl
from jax.experimental.pallas import tpu as pltpu
from jax.sharding import Mesh
from jax.sharding import PartitionSpec as P

TILE = 128
SIDE = 16
HALF = 8
LINE = 4
QUARTER = 8
BLOCK = 8
FIELDS = SIDE * BLOCK
GROUP = 16

support_fine = 0.35
support_mid = 0.55
support_coarse = 0.8

ROW = ("y", "zh", "k")
YZ = ("y", "zh")
YZL = ("y", "zh", "zl")
COL = ("x", "zl")
ALL = ROW + COL

bf16 = jnp.bfloat16
f32 = jnp.float32

VMEM = pl.BlockSpec(memory_space=pltpu.VMEM)
SMEM = pl.BlockSpec(memory_space=pltpu.SMEM)
HBM = pl.BlockSpec(memory_space=pltpu.HBM)


def room(mebibytes):
    return pltpu.CompilerParams(vmem_limit_bytes=mebibytes * 1024 * 1024)


def hint(microseconds):
    return pl.CostEstimate(
        flops=0, transcendentals=0, bytes_accessed=int(microseconds * 3.0e6)
    )


def turned(x):
    pairs = [(c * SIDE + r, r * SIDE + c) for r in range(SIDE) for c in range(SIDE)]
    return lax.ppermute(x, ALL, pairs)


def place_of_block(block, core):
    return ((block % 2) ^ core) * HALF + block // 2


def turned_blocks(x):
    pairs = [
        (c * SIDE + place_of_block(r, c % 2), r * SIDE + c) for r in range(SIDE) for c in range(SIDE)
    ]
    return lax.ppermute(x, ALL, pairs)


def from_partner(x):
    return lax.ppermute(x, "k", [(0, 1), (1, 0)])


def exchanged(x, axes):
    return lax.all_to_all(x, axes, split_axis=0, concat_axis=0, tiled=True)


def pair_sum(own, other):
    return (own.astype(f32) + from_partner(other).astype(f32)).astype(bf16)


def stretch_of(support):
    return (4.0 / support**5) ** 0.2


def wendland(left, right, support):
    across, upward = left[0] - right[0], left[1] - right[1]
    square = jnp.maximum(across * across + upward * upward, 1e-30)
    edge = support * stretch_of(support)
    margin = jnp.maximum(edge - square * lax.rsqrt(square), 0.0)
    margin2 = margin * margin
    ratio = 5.0 / edge**4
    return (margin2 * margin2 * (ratio - margin)).astype(bf16)


def at_tile(i):
    return pl.ds(pl.multiple_of(i * TILE, TILE), TILE)


def call(kernel, shapes, operands, name, mebibytes, microseconds, scratch=(), scalars=0):
    out = pl.pallas_call(
        kernel,
        out_shape=[jax.ShapeDtypeStruct(shape, kind) for shape, kind in shapes],
        in_specs=[SMEM] * scalars + [VMEM] * (len(operands) - scalars),
        out_specs=[VMEM] * len(shapes),
        scratch_shapes=list(scratch),
        compiler_params=room(mebibytes),
        cost_estimate=hint(microseconds),
        name=name,
    )(*operands)
    return out if len(shapes) > 1 else out[0]


def rows_of(listed):
    return -(-listed // TILE)


def in_rows(listing):
    rows = rows_of(listing.shape[1])
    padded = jnp.pad(listing, ((0, 0), (0, rows * TILE - listing.shape[1])))
    return padded.reshape(2 * rows, TILE)


def packed(points0, points1, lists, factor):
    fine, mid = points0.shape[1] // TILE, points1.shape[1] // TILE
    used = 2 * (fine + mid) + sum(2 * rows_of(a.shape[1]) for a in lists)
    above = -(-used // SIDE) * SIDE

    operands = (points0, points1, *lists, factor)
    count = len(operands)

    def kernel(*refs):
        given, out_ref, held, sems = refs[:count], refs[count], refs[count + 1 : -1], refs[-1]
        copies = [
            pltpu.make_async_copy(ref, to, sems.at[n]) for n, (ref, to) in enumerate(zip(given, held))
        ]
        for copy in copies:
            copy.start()
        for copy in copies:
            copy.wait()
        lines = []
        for ref in held[:-1]:
            whole = ref[...].astype(f32)
            length = whole.shape[1]
            short = -length % TILE
            if short:
                whole = jnp.concatenate([whole, jnp.zeros((2, short), f32)], axis=1)
            for a in range(2):
                lines += [whole[a : a + 1, t : t + TILE] for t in range(0, length, TILE)]
        if above > used:
            lines.append(jnp.zeros((above - used, TILE), f32))
        out_ref[pl.ds(0, above), :] = jnp.concatenate(lines, axis=0).astype(bf16)
        out_ref[pl.ds(above, TILE), :] = held[-1][...]

    return pl.pallas_call(
        kernel,
        out_shape=jax.ShapeDtypeStruct((above + TILE, TILE), bf16),
        in_specs=[HBM] * count,
        out_specs=VMEM,
        scratch_shapes=[pltpu.VMEM(a.shape, a.dtype) for a in operands]
        + [pltpu.SemaphoreType.DMA((count,))],
        compiler_params=room(8),
        cost_estimate=hint(1),
        name="packed",
    )(*(pltpu.with_memory_space_constraint(a, pltpu.HBM) for a in operands))


def unpacked(there, factor, local, fine, mid, listed):
    used = 2 * (fine + mid) + listed
    above = -(-used // SIDE) * SIDE
    size = 2 * TILE + local.shape[0]

    def kernel(there_ref, factor_ref, local_ref, fine_ref, mid_ref, list_ref, common_ref):
        lines = there_ref[pl.ds(0, above), :].astype(f32)
        at = 0
        for ref, tiles in ((fine_ref, fine), (mid_ref, mid)):
            for a in range(2):
                for t in range(tiles):
                    ref[a, t] = lines[at : at + 1]
                    at += 1
        list_ref[...] = lines[at : at + listed].astype(jnp.int32)
        common_ref[pl.ds(0, TILE), :] = factor_ref[...]
        common_ref[pl.ds(TILE, TILE), :] = there_ref[pl.ds(above, TILE), :]
        common_ref[pl.ds(2 * TILE, local.shape[0]), :] = local_ref[...]

    shapes = [
        ((2, fine, 1, TILE), f32),
        ((2, mid, 1, TILE), f32),
        ((listed, TILE), jnp.int32),
        ((size, TILE), bf16),
    ]
    return call(kernel, shapes, (there, factor, local), "unpacked", 8, 1)


def in_row_order(place, common, partner, mid):
    at_centres, at_mid = 2 * TILE, 2 * TILE + SIDE
    length = common.shape[1] // 2

    def kernel(place_ref, own_ref, other_ref, down_ref, across_ref, centre_ref, line_ref):
        core, x, zh = place_ref[0], place_ref[4], place_ref[5]

        def rows(y, of_zh, of_core, at, size):
            first = jnp.where(zh == of_zh, 0, length)
            lines = pl.ds(pl.multiple_of(first + at, SIDE), size)
            own, other = own_ref[y, lines, :], other_ref[y, lines, :]
            return jnp.where(core == of_core, own.astype(f32), other.astype(f32))

        for block in range(SIDE):
            chip = (block // LINE, block // 2 % 2, block % 2)
            down_ref[pl.ds(block * TILE, TILE), :] = rows(*chip, 0, TILE).astype(bf16)
            across_ref[block] = rows(*chip, TILE, TILE).astype(bf16)
            lines = rows(*chip, at_centres, SIDE)
            for a in range(2):
                centre_ref[a, block] = lines[a : a + 1]
        for q in range(LINE):
            lines = rows(x, q // 2, q % 2, at_mid, 2 * mid)
            for a in range(2):
                for t in range(mid):
                    line_ref[a, q * mid + t] = lines[a * mid + t : a * mid + t + 1]

    shapes = [
        ((SIDE * TILE, TILE), bf16),
        ((SIDE, TILE, TILE), bf16),
        ((2, SIDE, 1, TILE), f32),
        ((2, LINE * mid, 1, TILE), f32),
    ]
    return call(kernel, shapes, (place, common, partner), "in_row_order", 8, 2, (), 1)


def set_points(left_ref, right_ref, left, right, support):
    stretch = stretch_of(support)
    for axis in range(2):
        for t in range(left.shape[1]):
            row = left_ref[axis, t] * stretch
            left[axis, t] = jnp.broadcast_to(row, (TILE, TILE)).T
        for t in range(right.shape[1]):
            right[axis, t] = right_ref[axis, t] * stretch


def point_scratch(left, right):
    return [pltpu.VMEM((2, left, TILE, TILE), f32), pltpu.VMEM((2, right, 1, TILE), f32)]


def add_tiles(list_ref, listed, first, contracted, left, right, vector, total, support):
    rows = rows_of(listed)
    group = 2 * GROUP
    steps = TILE // group
    line_j = first + contracted * rows
    line_i = first + (1 - contracted) * rows

    def step(g, carry):
        row, lane = g // steps, g % steps * group
        products = []
        for u in range(group):
            j = list_ref[line_j + row, lane + u]
            i = list_ref[line_i + row, lane + u]
            tile = wendland((left[0, j], left[1, j]), (right[0, i], right[1, i]), support)
            product = jnp.dot(vector[:, at_tile(j)], tile, preferred_element_type=f32)
            products.append((i, product))
        for i, product in products:
            total[i] += product
        return carry

    lax.fori_loop(0, listed // group, step, 0)


def product_a0(lists, place, left, right, vector, listed):
    tiles = right.shape[1]

    def kernel(
        list_ref, place_ref, left_ref, right_ref, vector_ref, own_ref, other_ref, left, right, total
    ):
        set_points(left_ref, right_ref, left, right, support_fine)
        me = place_ref[0]
        weight = jnp.where(place_ref[1] == place_ref[2], -2.0 / scale_of(tiles, listed), 0.0)
        for i in range(tiles):
            at = pl.ds(i * TILE, TILE)
            total[i] = vector_ref[:, at].astype(f32) * weight
        add_tiles(list_ref, listed, 0, 1, left, right, vector_ref, total, support_fine)
        for half in range(HALF):
            for i in range(tiles):
                at = pl.ds(i * TILE, TILE)
                own = pl.ds(pl.multiple_of((2 * half + me) * BLOCK, BLOCK), BLOCK)
                other = pl.ds(pl.multiple_of((2 * half + 1 - me) * BLOCK, BLOCK), BLOCK)
                own_ref[half, :, at] = total[i, own, :].astype(bf16)
                other_ref[half, :, at] = total[i, other, :].astype(bf16)

    half = ((HALF, BLOCK, tiles * TILE), bf16)
    scratch = [*point_scratch(left.shape[1], tiles), pltpu.VMEM((tiles, FIELDS, TILE), f32)]
    operands = (lists, place, left, right, vector)
    return call(kernel, [half, half], operands, "product_a0", 16, 20, scratch, 2)


def product(lists, listed, first, contracted, left, right, halves, support, tail=None):
    tiles = right.shape[1]
    length = left.shape[1] * TILE
    size = tiles * TILE

    def kernel(list_ref, left_ref, right_ref, own_ref, other_ref, *rest):
        *given, left, right, vector, total = rest
        set_points(left_ref, right_ref, left, right, support)
        total[...] = jnp.zeros_like(total)
        for ref, at in ((own_ref, 0), (other_ref, FIELDS // 2)):
            rows = ref[:, :, pl.ds(0, length)].reshape(FIELDS // 2, length)
            vector[pl.ds(at, FIELDS // 2), :] = rows
        add_tiles(list_ref, listed, first, contracted, left, right, vector, total, support)
        for i in range(tiles):
            low = total[i].astype(bf16)
            at = pl.ds(i * TILE, TILE)
            if tail is not None:
                given[1][:, :, at] = low.reshape(SIDE, BLOCK, TILE)
            else:
                pair = low.reshape(2, HALF, BLOCK, TILE)
                given[0][:, :, at] = pair[0]
                given[1][:, :, at] = pair[1]
        if tail is not None:
            for peer in range(SIDE):
                given[1][peer, :, pl.ds(size, TILE)] = given[0][...]

    scratch = [
        *point_scratch(left.shape[1], tiles),
        pltpu.VMEM((FIELDS, length), bf16),
        pltpu.VMEM((tiles, FIELDS, TILE), f32),
    ]
    operands = (lists, left, right, *halves)
    if tail is not None:
        shapes = [((SIDE, BLOCK, size + TILE), bf16)]
        operands = (*operands, tail)
    else:
        shapes = [((HALF, BLOCK, size), bf16)] * 2
    return call(kernel, shapes, operands, "product", 16, listed / 18, scratch, 1)


def quarter_of(lists, place, blocks, listed, tiles):
    held = rows_of(listed)
    size = rows_of(LINE * QUARTER * tiles) * TILE

    def kernel(place_ref, list_ref, out_ref):
        zl = place_ref[3]
        row = lax.broadcasted_iota(jnp.int32, (TILE, TILE), 0)
        col = lax.broadcasted_iota(jnp.int32, (TILE, TILE), 1)
        before = (row < col).astype(bf16)
        slot = lax.broadcasted_iota(jnp.int32, (size, TILE), 0).astype(f32)
        lane = lax.broadcasted_iota(jnp.int32, (1, TILE), 1)
        count = jnp.zeros((1, 1), f32)
        total = jnp.zeros((BLOCK, size), f32)
        for block in range(blocks):
            for part in range(held):
                at = block * 2 * held + part
                i = list_ref[at : at + 1, :]
                j = list_ref[at + held : at + held + 1, :] + block * tiles
                real = jnp.where(lane + part * TILE < listed, 1.0, 0.0)
                flag = jnp.where(((i >> 1) & (LINE - 1)) == zl, real, 0.0)
                rank = count + jnp.dot(
                    jnp.broadcast_to(flag, (BLOCK, TILE)).astype(bf16),
                    before,
                    preferred_element_type=f32,
                )[:1]
                here = jnp.where(slot == jnp.where(flag > 0.5, rank, -1.0), 1.0, 0.0).astype(bf16)
                lines = [((i >> 3) * 2 + (i & 1)).astype(f32), j.astype(f32)]
                lines.append(jnp.zeros((BLOCK - 2, TILE), f32))
                lines = jnp.concatenate(lines, axis=0).astype(bf16)
                total += lax.dot_general(
                    lines, here, (((1,), (1,)), ((), ())), preferred_element_type=f32
                )
                count += jnp.sum(flag, axis=1, keepdims=True)
        slots = lax.broadcasted_iota(jnp.int32, (1, size), 1).astype(f32)
        out_ref[0:1, :] = jnp.where(slots < count, total[0:1], float(QUARTER)).astype(jnp.int32)
        out_ref[1:2, :] = total[1:2].astype(jnp.int32)
        groups = ((count + (GROUP - 1)) * (1.0 / GROUP)).astype(jnp.int32)
        out_ref[2:3, :] = jnp.broadcast_to(groups, (1, size))
        out_ref[3:, :] = jnp.zeros((BLOCK - 3, size), jnp.int32)

    shapes = [((BLOCK, size), jnp.int32)]
    return call(kernel, shapes, (place, lists), "quarter_of", 8, 3, (), 1)


def product_quarter(lists, left, right, own, other, support):
    tiles = right.shape[1]
    length = left.shape[1] * TILE // LINE

    def kernel(list_ref, left_ref, right_ref, own_ref, other_ref, out_ref, left, right, vector, total):
        set_points(left_ref, right_ref, left, right, support)
        total[...] = jnp.zeros_like(total)
        for ref, first in ((own_ref, 0), (other_ref, FIELDS // 2)):
            for chip in range(HALF):
                for zl in range(LINE):
                    at = pl.ds(first + chip * BLOCK, BLOCK)
                    part = ref[chip * LINE + zl, :, pl.ds(0, length)]
                    vector[at, pl.ds(zl * length, length)] = part

        def step(g, carry):
            products = []
            for u in range(GROUP):
                i = list_ref[0, g * GROUP + u]
                j = list_ref[1, g * GROUP + u]
                tile = wendland((left[0, j], left[1, j]), (right[0, i], right[1, i]), support)
                product = jnp.dot(vector[:, at_tile(j)], tile, preferred_element_type=f32)
                products.append((i, product))
            for i, product in products:
                total[i] += product
            return carry

        lax.fori_loop(0, list_ref[2, 0], step, 0)
        for i in range(QUARTER):
            out_ref[i // 2, :, pl.ds(i % 2 * TILE, TILE)] = total[i].astype(bf16)

    scratch = [
        *point_scratch(left.shape[1], tiles),
        pltpu.VMEM((FIELDS, length * LINE), bf16),
        pltpu.VMEM((tiles, FIELDS, TILE), f32),
    ]
    operands = (lists, left, right, own, other)
    shapes = [((QUARTER // 2, FIELDS, 2 * TILE), bf16)]
    return call(kernel, shapes, operands, "product_quarter", 20, 10, scratch, 1)


def all_pairs(left, right, support):
    rows, cols = left.shape[1], right.shape[1]

    def kernel(left_ref, right_ref, out_ref):
        stretch = stretch_of(support)
        ys = [jnp.broadcast_to(left_ref[a, 0] * stretch, (TILE, TILE)).T for a in range(2)]
        for j in range(cols):
            out_ref[:, pl.ds(j * TILE, TILE)] = wendland(
                ys, (right_ref[0, j] * stretch, right_ref[1, j] * stretch), support
            )

    return pl.pallas_call(
        kernel,
        out_shape=jax.ShapeDtypeStruct((rows * TILE, cols * TILE), bf16),
        grid=(rows,),
        in_specs=[pl.BlockSpec((2, 1, 1, TILE), lambda i: (0, i, 0, 0)), VMEM],
        out_specs=pl.BlockSpec((TILE, cols * TILE), lambda i: (i, 0)),
        compiler_params=room(8),
        cost_estimate=hint(6),
        name="all_pairs",
    )(left, right)


def sum_of(arrived):
    _, rows, n = arrived.shape

    def kernel(arrived_ref, out_ref):
        for t in range(0, n, 4 * TILE):
            at = pl.ds(t, 4 * TILE)
            out_ref[:, at] = arrived_ref[:, :, at].astype(f32).sum(axis=0).astype(bf16)

    return call(kernel, [((rows, n), bf16)], (arrived,), "sum_of", 8, 1)


def residual_of(here, there, scale):
    rows, n = here.shape

    def kernel(here_ref, there_ref, out_ref):
        squares = jnp.zeros((1, TILE), f32)
        for t in range(n // TILE):
            at = pl.ds(t * TILE, TILE)
            part = scale * (here_ref[:, at].astype(f32) + there_ref[:, at].astype(f32))
            squares += jnp.sum(part * part, axis=0, keepdims=True)
            low = part.astype(bf16)
            for chip in range(LINE):
                out_ref[chip, :, at] = low
        tail = three_rows(squares)
        for chip in range(LINE):
            out_ref[chip, pl.ds(0, BLOCK), pl.ds(n, TILE)] = tail
            out_ref[chip, pl.ds(BLOCK, BLOCK), pl.ds(n, TILE)] = jnp.zeros_like(tail)

    shapes = [((LINE, rows, n + TILE), bf16)]
    return call(kernel, shapes, (here, there), "residual_of", 8, 1)


def three_rows(x):
    high = x.astype(bf16).astype(f32)
    rest = x - high
    middle = rest.astype(bf16).astype(f32)
    rows = [high, middle, rest - middle, jnp.zeros((BLOCK - 3, TILE), f32)]
    return jnp.concatenate(rows, axis=0).astype(bf16)


def mid_of(arrived, scale):
    peers, _, n = arrived.shape
    n = n - TILE

    def kernel(arrived_ref, out_ref, low_ref):
        part = scale * arrived_ref[:, :, pl.ds(0, n)].astype(f32).sum(axis=0)
        out_ref[...] = part
        low = part.astype(bf16)
        for peer in range(peers):
            low_ref[peer] = low

    shapes = [((BLOCK, n), f32), ((peers, BLOCK, n), bf16)]
    return call(kernel, shapes, (arrived,), "mid_of", 8, 1)


def chunks_of(matrix_ref, held, sems):
    chunks = sems.shape[0]
    size = matrix_ref.shape[0] // chunks
    rows = [pl.ds(q * size, size) for q in range(chunks)]
    return [
        pltpu.make_async_copy(matrix_ref.at[r], held.at[r], sems.at[q]) for q, r in enumerate(rows)
    ]


def call_on_matrix(kernel, shape, kind, matrix, operands, name, scratch):
    chunks = 4
    return pl.pallas_call(
        kernel,
        out_shape=jax.ShapeDtypeStruct(shape, kind),
        in_specs=[HBM] + [VMEM] * len(operands),
        out_specs=VMEM,
        scratch_shapes=[
            pltpu.VMEM(matrix.shape, bf16),
            pltpu.SemaphoreType.DMA((chunks,)),
            *scratch,
        ],
        compiler_params=room(12),
        cost_estimate=hint(3),
        name=name,
    )(pltpu.with_memory_space_constraint(matrix, pltpu.HBM), *operands)


def coarse_product(matrix, arrived, mid_data, scale):
    rows, cols = matrix.shape

    def kernel(matrix_ref, arrived_ref, mid_ref, out_ref, held, sems, turned_ref):
        copies = chunks_of(matrix_ref, held, sems)
        for copy in copies:
            copy.start()
        whole = (scale * arrived_ref[...].astype(f32).sum(axis=0)).astype(bf16).astype(f32)
        whole = mid_ref[...] - 0.5 * whole
        for t in range(cols // TILE):
            lines = whole[:, t * TILE : (t + 1) * TILE]
            full = jnp.concatenate([lines, jnp.zeros((TILE - BLOCK, TILE), f32)], axis=0)
            turned_ref[pl.ds(t * TILE, TILE), :] = full.T.astype(bf16)
        each = rows // TILE // len(copies)
        for c, copy in enumerate(copies):
            copy.wait()
            for q in range(c * each, (c + 1) * each):
                part = jnp.dot(
                    held[pl.ds(q * TILE, TILE), :], turned_ref[...], preferred_element_type=f32
                )
                out_ref[q] = part.T[:BLOCK, :]

    shape = (rows // TILE, BLOCK, TILE)
    scratch = [pltpu.VMEM((cols, TILE), bf16)]
    operands = (arrived, mid_data)
    return call_on_matrix(kernel, shape, f32, matrix, operands, "coarse_product", scratch)


def coarse_data_of(arrived, own, other, scale):
    peers = arrived.shape[0]
    n = own.shape[2] - TILE

    def kernel(arrived_ref, own_ref, other_ref, out_ref):
        data = (scale * arrived_ref[...].sum(axis=0)).astype(bf16)
        squares = jnp.zeros((1, TILE), f32)
        for ref in (own_ref, other_ref):
            tails = ref[...].astype(f32).sum(axis=0)
            squares += jnp.sum(tails, axis=0, keepdims=True)
        tail = three_rows(squares)
        for peer in range(peers):
            out_ref[peer, 0] = data
            out_ref[peer, 1] = tail

    tails = (own[:, :, n:], other[:, :, n:])
    shapes = [((peers, 2, BLOCK, TILE), bf16)]
    return call(kernel, shapes, (arrived, *tails), "coarse_data_of", 8, 1)


def halfway_of(gathered_data, factor_down):
    peers = gathered_data.shape[0]

    def kernel(data_ref, factor_ref, out_ref):
        total = jnp.zeros((BLOCK, TILE), f32)
        for q in range(peers // 2):
            pair = jnp.concatenate([data_ref[2 * q, 0], data_ref[2 * q + 1, 0]], axis=1)
            rows = factor_ref[pl.ds(q * 2 * TILE, 2 * TILE), :]
            total += jnp.dot(pair, rows, preferred_element_type=f32)
        low = total.astype(bf16)
        for peer in range(peers):
            out_ref[peer] = low

    shapes = [((peers, BLOCK, TILE), bf16)]
    return call(kernel, shapes, (gathered_data, factor_down), "halfway_of", 8, 1)


def coarse_coef_of(halfway, factor_across):
    peers = halfway.shape[0]

    def kernel(half_ref, factor_ref, out_ref):
        total = jnp.zeros((BLOCK, TILE), f32)
        for q in range(peers):
            total += lax.dot_general(
                half_ref[q], factor_ref[q], (((1,), (1,)), ((), ())), preferred_element_type=f32
            )
        low = total.astype(bf16)
        for peer in range(peers):
            out_ref[peer] = low

    shapes = [((peers, BLOCK, TILE), bf16)]
    return call(kernel, shapes, (halfway, factor_across), "coarse_coef_of", 8, 1)


def prolong(matrix, coarse_coef, place, mid_data, scale):
    rows, cols = matrix.shape
    two = 2 * TILE

    def kernel(matrix_ref, coef_ref, low_ref, mid_ref, out_ref, held, sems):
        copies = chunks_of(matrix_ref, held, sems)
        for copy in copies:
            copy.start()
        for chip in range(HALF):
            for zl in range(LINE):
                out_ref[chip * LINE + zl, :, pl.ds(cols, TILE)] = low_ref[chip]
        total = jnp.zeros((BLOCK, cols), f32)
        each = rows // two // len(copies)
        for c, copy in enumerate(copies):
            copy.wait()
            for q in range(c * each, (c + 1) * each):
                pair = jnp.concatenate([coef_ref[2 * q], coef_ref[2 * q + 1]], axis=1)
                total += jnp.dot(pair, held[pl.ds(q * two, two), :], preferred_element_type=f32)
        low = (0.5 * mid_ref[...] + scale * total).astype(bf16)
        for chip in range(HALF * LINE):
            out_ref[chip, :, pl.ds(0, cols)] = low

    sent = coarse_coef.reshape(HALF, 2, BLOCK, TILE)
    sent = jnp.where(place[3] % 2 == 0, sent[:, 0], sent[:, 1])
    shape = (HALF * LINE, BLOCK, cols + TILE)
    operands = (coarse_coef, sent, mid_data)
    return call_on_matrix(kernel, shape, bf16, matrix, operands, "prolong", ())


def fine_of(arrived, data, core, scale):
    n = arrived.shape[2]

    def kernel(core_ref, arrived_ref, data_ref, out_ref, summed):
        me = core_ref[0]
        summed[...] = arrived_ref[...].astype(f32).sum(axis=0)
        rows = []
        for block in range(SIDE):
            at = ((block % 2) ^ me) * HALF + block // 2
            rows.append(summed[pl.ds(pl.multiple_of(at * BLOCK, BLOCK), BLOCK), :])
        whole = jnp.concatenate(rows, axis=0)
        for t in range(n // TILE):
            at = pl.ds(t * TILE, TILE)
            data = data_ref[at, :].astype(f32)
            out_ref[at, :] = 0.5 * data + scale * whole[:, t * TILE : (t + 1) * TILE].T

    scratch = [pltpu.VMEM((FIELDS, n), f32)]
    return call(kernel, [((n, FIELDS), f32)], (core, arrived, data), "fine_of", 8, 2, scratch, 1)


def in_field_order(x, core):
    n = x.shape[-1]
    x = jnp.where(core == 0, x, x[::-1])
    return x.transpose(3, 1, 0, 2).reshape(n, FIELDS)


def scale_of(tiles, listed):
    return (tiles * TILE / (SIDE * listed * TILE * TILE)) ** 0.5


def per_device(values, points0, points1, points2, tiles_a0, tiles_e1, tiles_a1, factor):
    core = lax.axis_index("k")
    col_id = lax.axis_index(COL)
    row_id = lax.axis_index(ROW)
    rows_fine, fields = values.shape
    rows_mid = points1.shape[1]
    rows_coarse = points2.shape[1]
    coarse = rows_coarse * SIDE
    share = rows_fine // SIDE
    tiles_fine, tiles_mid = rows_fine // TILE, rows_mid // TILE
    list_a0, list_e1, list_a1 = tiles_a0[0, 0], tiles_e1[0, 0], tiles_a1[0, 0]
    scale_a0 = scale_of(tiles_fine, list_a0.shape[1])
    scale_e1 = scale_of(tiles_fine, list_e1.shape[1])
    scale_a1 = scale_of(tiles_mid, list_a1.shape[1])
    scale_e2 = (1.0 / (rows_mid * SIDE)) ** 0.5

    listed_a0, listed_e1, listed_a1 = (a.shape[1] for a in (list_a0, list_e1, list_a1))

    first_e1 = 2 * rows_of(listed_a0)
    first_a1 = first_e1 + 2 * rows_of(listed_e1)

    own_e1 = in_rows(list_e1)
    there = turned(packed(points0, points1, (list_a0, list_e1, list_a1), factor))
    local = [points2, jnp.zeros((SIDE - 2, TILE), bf16), points1.reshape(2 * tiles_mid, TILE)]
    local = jnp.concatenate(local, axis=0)
    x_id, zl_id = lax.axis_index("x"), lax.axis_index("zl")
    place = jnp.stack([core, row_id, col_id, zl_id, x_id, lax.axis_index("zh")]).astype(jnp.int32)
    fine_here = points0.astype(f32).reshape(2, tiles_fine, 1, TILE)
    mid_here = points1.astype(f32).reshape(2, tiles_mid, 1, TILE)
    tail = jnp.pad(own_e1, ((0, BLOCK - own_e1.shape[0]), (0, 0))).astype(bf16)
    there, vector, local, fine_here, mid_here, tail, place = lax.optimization_barrier(
        (there, values.T, local, fine_here, mid_here, tail, place)
    )
    fine_there, mid_there, lists, common = unpacked(
        there, factor, local, tiles_fine, tiles_mid, first_a1 + 2 * rows_of(listed_a1)
    )

    own, other = product_a0(lists, place, fine_here, fine_there, vector, listed_a0)
    pair = pair_sum(own, other).reshape(LINE, 2 * BLOCK, rows_fine)
    summed = sum_of(exchanged(pair, "y"))
    common, summed = lax.optimization_barrier((common, summed))
    swapped = lax.ppermute(summed, "zh", [(0, 1), (1, 0)])
    swapped, common, crossed = lax.optimization_barrier(
        (swapped, common, lax.ppermute(common, "zh", [(0, 1), (1, 0)]))
    )
    common = jnp.concatenate([common, crossed], axis=0)
    common = jnp.broadcast_to(common, (LINE, *common.shape))
    fine_own = exchanged(residual_of(summed, swapped, -0.5 * scale_a0), "y")
    fine_own, common = lax.optimization_barrier((fine_own, common))
    fine_own = fine_own.reshape(HALF, BLOCK, rows_fine + TILE)
    fine_other = from_partner(fine_own)

    common, fine_own, fine_other = lax.optimization_barrier((common, fine_own, fine_other))
    common = exchanged(common, "y")
    restricted = product(
        lists, listed_e1, first_e1, 0, fine_there, mid_here, (fine_own, fine_other), support_mid, tail
    )
    restricted, common = lax.optimization_barrier((restricted, common))
    ordered = in_row_order(place, common, from_partner(common), tiles_mid)
    fine_quarter = fine_here.reshape(2, QUARTER // 2, LINE, 2, 1, TILE)
    fine_quarter = lax.dynamic_index_in_dim(fine_quarter, zl_id, 2, keepdims=False)
    fine_quarter = fine_quarter.reshape(2, QUARTER, 1, TILE)
    fine_quarter = jnp.pad(fine_quarter, ((0, 0), (0, 1), (0, 0), (0, 0)), constant_values=8.0)
    factor_down, factor_across, centres, mid_line = ordered
    coarse_kernel = all_pairs(centres, mid_there, support_coarse)
    restricted, coarse_kernel, factor_down, factor_across, mid_line, fine_quarter = (
        lax.optimization_barrier(
            (
                exchanged(restricted, COL),
                coarse_kernel,
                factor_down,
                factor_across,
                mid_line,
                fine_quarter,
            )
        )
    )
    mid_share, mid_all = mid_of(restricted, scale_e1)
    line_lists = lax.dynamic_slice_in_dim(restricted[:, :, rows_mid:], x_id * LINE, LINE, 0)
    line_lists = line_lists[:, : own_e1.shape[0]].reshape(-1, TILE).astype(jnp.int32)
    line_lists = quarter_of(line_lists, place, LINE, listed_e1, tiles_mid)
    mid_all, mid_data, line_lists = lax.optimization_barrier(
        (exchanged(mid_all, COL), turned_blocks(mid_share), line_lists)
    )

    mid_halves = (mid_all[:HALF], mid_all[HALF:])
    mid_own, mid_other = product(
        lists, listed_a1, first_a1, 1, mid_here, mid_there, mid_halves, support_mid
    )
    arrived = exchanged(pair_sum(mid_own, mid_other), YZ)

    coarse_part = coarse_product(coarse_kernel, arrived, mid_data, scale_a1)
    coarse_data = coarse_data_of(exchanged(coarse_part, COL), fine_own, fine_other, scale_e2)
    coarse_data = exchanged(coarse_data, COL)
    halfway = exchanged(halfway_of(coarse_data, factor_down), COL)
    coarse_all = exchanged(coarse_coef_of(halfway, factor_across), COL)

    new_own = exchanged(prolong(coarse_kernel, coarse_all, place, mid_data, scale_e2), YZL)
    new_other = from_partner(new_own)
    fine_part = product_quarter(
        line_lists, mid_line, fine_quarter, new_own, new_other, support_mid
    )
    fine_part, new_own, new_other = lax.optimization_barrier((fine_part, new_own, new_other))
    own_data = lax.dynamic_slice_in_dim(values, col_id * share, share, 0)
    fine_coef = fine_of(exchanged(fine_part, "x"), own_data, place, scale_e1)

    def from_line(zl, at, size):
        both = jnp.stack([new_own, new_other])[..., at : at + size]
        both = both.reshape(2, HALF, LINE, BLOCK, size)
        both = lax.dynamic_index_in_dim(both, zl, 2, keepdims=False)
        return in_field_order(both.astype(f32), core)

    mid_coef = from_line(zl_id, 0, rows_mid)
    coarse_coef = from_line(core, rows_mid, rows_coarse)
    norm = coarse_data[:, 1].astype(f32).sum() / (rows_fine * SIDE * fields)
    return (fine_coef, mid_coef, coarse_coef, jnp.stack([norm]))


def solution(mesh):
    fine_mesh = Mesh(mesh.devices.reshape(4, 2, 2, 4, 4), ALL)
    return jax.shard_map(
        per_device,
        mesh=fine_mesh,
        in_specs=(
            P(ROW, None),
            P(None, ROW),
            P(None, ROW),
            P(None, ROW),
            P(ROW, COL, None, None),
            P(ROW, COL, None, None),
            P(ROW, COL, None, None),
            P(ROW, COL),
        ),
        out_specs=(P(ALL, None), P(COL, None), P(ROW, None), P()),
        check_vma=False,
    )
```

```python
import jax
import jax.numpy as jnp
from jax import lax
from jax.experimental import pallas as pl
from jax.experimental.pallas import tpu as pltpu
from jax.sharding import Mesh
from jax.sharding import PartitionSpec as P

TILE = 128
SIDE = 16
HALF = 8
LINE = 4
QUARTER = 8
BLOCK = 8
FIELDS = SIDE * BLOCK
GROUP = 16

support_fine = 0.35
support_mid = 0.55
support_coarse = 0.8

ROW = ("y", "zh", "k")
YZ = ("y", "zh")
YZL = ("y", "zh", "zl")
COL = ("x", "zl")
ALL = ROW + COL

bf16 = jnp.bfloat16
f32 = jnp.float32

VMEM = pl.BlockSpec(memory_space=pltpu.VMEM)
SMEM = pl.BlockSpec(memory_space=pltpu.SMEM)
HBM = pl.BlockSpec(memory_space=pltpu.HBM)


def room(mebibytes):
    return pltpu.CompilerParams(vmem_limit_bytes=mebibytes * 1024 * 1024)


def hint(microseconds):
    return pl.CostEstimate(
        flops=0, transcendentals=0, bytes_accessed=int(microseconds * 3.0e6)
    )


def turned(x):
    pairs = [(c * SIDE + r, r * SIDE + c) for r in range(SIDE) for c in range(SIDE)]
    return lax.ppermute(x, ALL, pairs)


def place_of_block(block, core):
    return ((block % 2) ^ core) * HALF + block // 2


def turned_blocks(x):
    pairs = [
        (c * SIDE + place_of_block(r, c % 2), r * SIDE + c) for r in range(SIDE) for c in range(SIDE)
    ]
    return lax.ppermute(x, ALL, pairs)


def from_partner(x):
    return lax.ppermute(x, "k", [(0, 1), (1, 0)])


def exchanged(x, axes):
    return lax.all_to_all(x, axes, split_axis=0, concat_axis=0, tiled=True)


def pair_sum(own, other):
    return (own.astype(f32) + from_partner(other).astype(f32)).astype(bf16)


def stretch_of(support):
    return (4.0 / support**5) ** 0.2


def wendland(left, right, support):
    across, upward = left[0] - right[0], left[1] - right[1]
    square = jnp.maximum(across * across + upward * upward, 1e-30)
    edge = support * stretch_of(support)
    margin = jnp.maximum(edge - square * lax.rsqrt(square), 0.0)
    margin2 = margin * margin
    ratio = 5.0 / edge**4
    return (margin2 * margin2 * (ratio - margin)).astype(bf16)


def at_tile(i):
    return pl.ds(pl.multiple_of(i * TILE, TILE), TILE)


def call(kernel, shapes, operands, name, mebibytes, microseconds, scratch=(), scalars=0):
    out = pl.pallas_call(
        kernel,
        out_shape=[jax.ShapeDtypeStruct(shape, kind) for shape, kind in shapes],
        in_specs=[SMEM] * scalars + [VMEM] * (len(operands) - scalars),
        out_specs=[VMEM] * len(shapes),
        scratch_shapes=list(scratch),
        compiler_params=room(mebibytes),
        cost_estimate=hint(microseconds),
        name=name,
    )(*operands)
    return out if len(shapes) > 1 else out[0]


def rows_of(listed):
    return -(-listed // TILE)


def in_rows(listing):
    rows = rows_of(listing.shape[1])
    padded = jnp.pad(listing, ((0, 0), (0, rows * TILE - listing.shape[1])))
    return padded.reshape(2 * rows, TILE)


def packed(points0, points1, lists, factor):
    fine, mid = points0.shape[1] // TILE, points1.shape[1] // TILE
    used = 2 * (fine + mid) + sum(2 * rows_of(a.shape[1]) for a in lists)
    above = -(-used // SIDE) * SIDE

    operands = (points0, points1, *lists, factor)
    count = len(operands)

    def kernel(*refs):
        given, out_ref, held, sems = refs[:count], refs[count], refs[count + 1 : -1], refs[-1]
        copies = [
            pltpu.make_async_copy(ref, to, sems.at[n]) for n, (ref, to) in enumerate(zip(given, held))
        ]
        for copy in copies:
            copy.start()
        for copy in copies:
            copy.wait()
        lines = []
        for ref in held[:-1]:
            whole = ref[...].astype(f32)
            length = whole.shape[1]
            short = -length % TILE
            if short:
                whole = jnp.concatenate([whole, jnp.zeros((2, short), f32)], axis=1)
            for a in range(2):
                lines += [whole[a : a + 1, t : t + TILE] for t in range(0, length, TILE)]
        if above > used:
            lines.append(jnp.zeros((above - used, TILE), f32))
        out_ref[pl.ds(0, above), :] = jnp.concatenate(lines, axis=0).astype(bf16)
        out_ref[pl.ds(above, TILE), :] = held[-1][...]

    return pl.pallas_call(
        kernel,
        out_shape=jax.ShapeDtypeStruct((above + TILE, TILE), bf16),
        in_specs=[HBM] * count,
        out_specs=VMEM,
        scratch_shapes=[pltpu.VMEM(a.shape, a.dtype) for a in operands]
        + [pltpu.SemaphoreType.DMA((count,))],
        compiler_params=room(8),
        cost_estimate=hint(1),
        name="packed",
    )(*(pltpu.with_memory_space_constraint(a, pltpu.HBM) for a in operands))


def unpacked(there, factor, local, fine, mid, listed):
    used = 2 * (fine + mid) + listed
    above = -(-used // SIDE) * SIDE
    size = 2 * TILE + local.shape[0]

    def kernel(there_ref, factor_ref, local_ref, fine_ref, mid_ref, list_ref, common_ref):
        lines = there_ref[pl.ds(0, above), :].astype(f32)
        at = 0
        for ref, tiles in ((fine_ref, fine), (mid_ref, mid)):
            for a in range(2):
                for t in range(tiles):
                    ref[a, t] = lines[at : at + 1]
                    at += 1
        list_ref[...] = lines[at : at + listed].astype(jnp.int32)
        common_ref[pl.ds(0, TILE), :] = factor_ref[...]
        common_ref[pl.ds(TILE, TILE), :] = there_ref[pl.ds(above, TILE), :]
        common_ref[pl.ds(2 * TILE, local.shape[0]), :] = local_ref[...]

    shapes = [
        ((2, fine, 1, TILE), f32),
        ((2, mid, 1, TILE), f32),
        ((listed, TILE), jnp.int32),
        ((size, TILE), bf16),
    ]
    return call(kernel, shapes, (there, factor, local), "unpacked", 8, 1)


def in_row_order(place, common, partner, mid):
    at_centres, at_mid = 2 * TILE, 2 * TILE + SIDE
    length = common.shape[1] // 2

    def kernel(place_ref, own_ref, other_ref, down_ref, across_ref, centre_ref, line_ref):
        core, x, zh = place_ref[0], place_ref[4], place_ref[5]

        def rows(y, of_zh, of_core, at, size):
            first = jnp.where(zh == of_zh, 0, length)
            lines = pl.ds(pl.multiple_of(first + at, SIDE), size)
            own, other = own_ref[y, lines, :], other_ref[y, lines, :]
            return jnp.where(core == of_core, own.astype(f32), other.astype(f32))

        for block in range(SIDE):
            chip = (block // LINE, block // 2 % 2, block % 2)
            down_ref[pl.ds(block * TILE, TILE), :] = rows(*chip, 0, TILE).astype(bf16)
            across_ref[block] = rows(*chip, TILE, TILE).astype(bf16)
            lines = rows(*chip, at_centres, SIDE)
            for a in range(2):
                centre_ref[a, block] = lines[a : a + 1]
        for q in range(LINE):
            lines = rows(x, q // 2, q % 2, at_mid, 2 * mid)
            for a in range(2):
                for t in range(mid):
                    line_ref[a, q * mid + t] = lines[a * mid + t : a * mid + t + 1]

    shapes = [
        ((SIDE * TILE, TILE), bf16),
        ((SIDE, TILE, TILE), bf16),
        ((2, SIDE, 1, TILE), f32),
        ((2, LINE * mid, 1, TILE), f32),
    ]
    return call(kernel, shapes, (place, common, partner), "in_row_order", 8, 2, (), 1)


def set_points(left_ref, right_ref, left, right, support):
    stretch = stretch_of(support)
    for axis in range(2):
        for t in range(left.shape[1]):
            row = left_ref[axis, t] * stretch
            left[axis, t] = jnp.broadcast_to(row, (TILE, TILE)).T
        for t in range(right.shape[1]):
            right[axis, t] = right_ref[axis, t] * stretch


def point_scratch(left, right):
    return [pltpu.VMEM((2, left, TILE, TILE), f32), pltpu.VMEM((2, right, 1, TILE), f32)]


def add_tiles(list_ref, listed, first, contracted, left, right, vector, total, support):
    rows = rows_of(listed)
    group = 2 * GROUP
    steps = TILE // group
    line_j = first + contracted * rows
    line_i = first + (1 - contracted) * rows

    def step(g, carry):
        row, lane = g // steps, g % steps * group
        products = []
        for u in range(group):
            j = list_ref[line_j + row, lane + u]
            i = list_ref[line_i + row, lane + u]
            tile = wendland((left[0, j], left[1, j]), (right[0, i], right[1, i]), support)
            product = jnp.dot(vector[:, at_tile(j)], tile, preferred_element_type=f32)
            products.append((i, product))
        for i, product in products:
            total[i] += product
        return carry

    lax.fori_loop(0, listed // group, step, 0)


def product_a0(lists, place, left, right, vector, listed):
    tiles = right.shape[1]

    def kernel(
        list_ref, place_ref, left_ref, right_ref, vector_ref, own_ref, other_ref, left, right, total
    ):
        set_points(left_ref, right_ref, left, right, support_fine)
        me = place_ref[0]
        weight = jnp.where(place_ref[1] == place_ref[2], -2.0 / scale_of(tiles, listed), 0.0)
        for i in range(tiles):
            at = pl.ds(i * TILE, TILE)
            total[i] = vector_ref[:, at].astype(f32) * weight
        add_tiles(list_ref, listed, 0, 1, left, right, vector_ref, total, support_fine)
        for half in range(HALF):
            for i in range(tiles):
                at = pl.ds(i * TILE, TILE)
                own = pl.ds(pl.multiple_of((2 * half + me) * BLOCK, BLOCK), BLOCK)
                other = pl.ds(pl.multiple_of((2 * half + 1 - me) * BLOCK, BLOCK), BLOCK)
                own_ref[half, :, at] = total[i, own, :].astype(bf16)
                other_ref[half, :, at] = total[i, other, :].astype(bf16)

    half = ((HALF, BLOCK, tiles * TILE), bf16)
    scratch = [*point_scratch(left.shape[1], tiles), pltpu.VMEM((tiles, FIELDS, TILE), f32)]
    operands = (lists, place, left, right, vector)
    return call(kernel, [half, half], operands, "product_a0", 16, 20, scratch, 2)


def product(lists, listed, first, contracted, left, right, halves, support, tail=None):
    tiles = right.shape[1]
    length = left.shape[1] * TILE
    size = tiles * TILE

    def kernel(list_ref, left_ref, right_ref, own_ref, other_ref, *rest):
        *given, left, right, vector, total = rest
        set_points(left_ref, right_ref, left, right, support)
        total[...] = jnp.zeros_like(total)
        for ref, at in ((own_ref, 0), (other_ref, FIELDS // 2)):
            rows = ref[:, :, pl.ds(0, length)].reshape(FIELDS // 2, length)
            vector[pl.ds(at, FIELDS // 2), :] = rows
        add_tiles(list_ref, listed, first, contracted, left, right, vector, total, support)
        for i in range(tiles):
            low = total[i].astype(bf16)
            at = pl.ds(i * TILE, TILE)
            if tail is not None:
                given[1][:, :, at] = low.reshape(SIDE, BLOCK, TILE)
            else:
                pair = low.reshape(2, HALF, BLOCK, TILE)
                given[0][:, :, at] = pair[0]
                given[1][:, :, at] = pair[1]
        if tail is not None:
            for peer in range(SIDE):
                given[1][peer, :, pl.ds(size, TILE)] = given[0][...]

    scratch = [
        *point_scratch(left.shape[1], tiles),
        pltpu.VMEM((FIELDS, length), bf16),
        pltpu.VMEM((tiles, FIELDS, TILE), f32),
    ]
    operands = (lists, left, right, *halves)
    if tail is not None:
        shapes = [((SIDE, BLOCK, size + TILE), bf16)]
        operands = (*operands, tail)
    else:
        shapes = [((HALF, BLOCK, size), bf16)] * 2
    return call(kernel, shapes, operands, "product", 16, listed / 18, scratch, 1)


def quarter_of(lists, place, blocks, listed, tiles):
    held = rows_of(listed)
    size = rows_of(LINE * QUARTER * tiles) * TILE

    def kernel(place_ref, list_ref, out_ref):
        zl = place_ref[3]
        row = lax.broadcasted_iota(jnp.int32, (TILE, TILE), 0)
        col = lax.broadcasted_iota(jnp.int32, (TILE, TILE), 1)
        before = (row < col).astype(bf16)
        slot = lax.broadcasted_iota(jnp.int32, (size, TILE), 0).astype(f32)
        lane = lax.broadcasted_iota(jnp.int32, (1, TILE), 1)
        count = jnp.zeros((1, 1), f32)
        total = jnp.zeros((BLOCK, size), f32)
        for block in range(blocks):
            for part in range(held):
                at = block * 2 * held + part
                i = list_ref[at : at + 1, :]
                j = list_ref[at + held : at + held + 1, :] + block * tiles
                real = jnp.where(lane + part * TILE < listed, 1.0, 0.0)
                flag = jnp.where(((i >> 1) & (LINE - 1)) == zl, real, 0.0)
                rank = count + jnp.dot(
                    jnp.broadcast_to(flag, (BLOCK, TILE)).astype(bf16),
                    before,
                    preferred_element_type=f32,
                )[:1]
                here = jnp.where(slot == jnp.where(flag > 0.5, rank, -1.0), 1.0, 0.0).astype(bf16)
                lines = [((i >> 3) * 2 + (i & 1)).astype(f32), j.astype(f32)]
                lines.append(jnp.zeros((BLOCK - 2, TILE), f32))
                lines = jnp.concatenate(lines, axis=0).astype(bf16)
                total += lax.dot_general(
                    lines, here, (((1,), (1,)), ((), ())), preferred_element_type=f32
                )
                count += jnp.sum(flag, axis=1, keepdims=True)
        slots = lax.broadcasted_iota(jnp.int32, (1, size), 1).astype(f32)
        out_ref[0:1, :] = jnp.where(slots < count, total[0:1], float(QUARTER)).astype(jnp.int32)
        out_ref[1:2, :] = total[1:2].astype(jnp.int32)
        groups = ((count + (GROUP - 1)) * (1.0 / GROUP)).astype(jnp.int32)
        out_ref[2:3, :] = jnp.broadcast_to(groups, (1, size))
        out_ref[3:, :] = jnp.zeros((BLOCK - 3, size), jnp.int32)

    shapes = [((BLOCK, size), jnp.int32)]
    return call(kernel, shapes, (place, lists), "quarter_of", 8, 3, (), 1)


def product_quarter(lists, left, right, own, other, support):
    tiles = right.shape[1]
    length = left.shape[1] * TILE // LINE

    def kernel(list_ref, left_ref, right_ref, own_ref, other_ref, out_ref, left, right, vector, total):
        set_points(left_ref, right_ref, left, right, support)
        total[...] = jnp.zeros_like(total)
        for ref, first in ((own_ref, 0), (other_ref, FIELDS // 2)):
            for chip in range(HALF):
                for zl in range(LINE):
                    at = pl.ds(first + chip * BLOCK, BLOCK)
                    part = ref[chip * LINE + zl, :, pl.ds(0, length)]
                    vector[at, pl.ds(zl * length, length)] = part

        def step(g, carry):
            products = []
            for u in range(GROUP):
                i = list_ref[0, g * GROUP + u]
                j = list_ref[1, g * GROUP + u]
                tile = wendland((left[0, j], left[1, j]), (right[0, i], right[1, i]), support)
                product = jnp.dot(vector[:, at_tile(j)], tile, preferred_element_type=f32)
                products.append((i, product))
            for i, product in products:
                total[i] += product
            return carry

        lax.fori_loop(0, list_ref[2, 0], step, 0)
        for i in range(QUARTER):
            out_ref[i // 2, :, pl.ds(i % 2 * TILE, TILE)] = total[i].astype(bf16)

    scratch = [
        *point_scratch(left.shape[1], tiles),
        pltpu.VMEM((FIELDS, length * LINE), bf16),
        pltpu.VMEM((tiles, FIELDS, TILE), f32),
    ]
    operands = (lists, left, right, own, other)
    shapes = [((QUARTER // 2, FIELDS, 2 * TILE), bf16)]
    return call(kernel, shapes, operands, "product_quarter", 20, 10, scratch, 1)


def all_pairs(left, right, support):
    rows, cols = left.shape[1], right.shape[1]

    def kernel(left_ref, right_ref, out_ref):
        stretch = stretch_of(support)
        ys = [jnp.broadcast_to(left_ref[a, 0] * stretch, (TILE, TILE)).T for a in range(2)]
        for j in range(cols):
            out_ref[:, pl.ds(j * TILE, TILE)] = wendland(
                ys, (right_ref[0, j] * stretch, right_ref[1, j] * stretch), support
            )

    return pl.pallas_call(
        kernel,
        out_shape=jax.ShapeDtypeStruct((rows * TILE, cols * TILE), bf16),
        grid=(rows,),
        in_specs=[pl.BlockSpec((2, 1, 1, TILE), lambda i: (0, i, 0, 0)), VMEM],
        out_specs=pl.BlockSpec((TILE, cols * TILE), lambda i: (i, 0)),
        compiler_params=room(8),
        cost_estimate=hint(6),
        name="all_pairs",
    )(left, right)


def sum_of(arrived):
    _, rows, n = arrived.shape

    def kernel(arrived_ref, out_ref):
        for t in range(0, n, 4 * TILE):
            at = pl.ds(t, 4 * TILE)
            out_ref[:, at] = arrived_ref[:, :, at].astype(f32).sum(axis=0).astype(bf16)

    return call(kernel, [((rows, n), bf16)], (arrived,), "sum_of", 8, 1)


def residual_of(here, there, scale):
    rows, n = here.shape

    def kernel(here_ref, there_ref, out_ref):
        squares = jnp.zeros((1, TILE), f32)
        for t in range(n // TILE):
            at = pl.ds(t * TILE, TILE)
            part = scale * (here_ref[:, at].astype(f32) + there_ref[:, at].astype(f32))
            squares += jnp.sum(part * part, axis=0, keepdims=True)
            low = part.astype(bf16)
            for chip in range(LINE):
                out_ref[chip, :, at] = low
        tail = three_rows(squares)
        for chip in range(LINE):
            out_ref[chip, pl.ds(0, BLOCK), pl.ds(n, TILE)] = tail
            out_ref[chip, pl.ds(BLOCK, BLOCK), pl.ds(n, TILE)] = jnp.zeros_like(tail)

    shapes = [((LINE, rows, n + TILE), bf16)]
    return call(kernel, shapes, (here, there), "residual_of", 8, 1)


def three_rows(x):
    high = x.astype(bf16).astype(f32)
    rest = x - high
    middle = rest.astype(bf16).astype(f32)
    rows = [high, middle, rest - middle, jnp.zeros((BLOCK - 3, TILE), f32)]
    return jnp.concatenate(rows, axis=0).astype(bf16)


def mid_of(arrived, scale):
    peers, _, n = arrived.shape
    n = n - TILE

    def kernel(arrived_ref, out_ref, low_ref):
        part = scale * arrived_ref[:, :, pl.ds(0, n)].astype(f32).sum(axis=0)
        out_ref[...] = part
        low = part.astype(bf16)
        for peer in range(peers):
            low_ref[peer] = low

    shapes = [((BLOCK, n), f32), ((peers, BLOCK, n), bf16)]
    return call(kernel, shapes, (arrived,), "mid_of", 8, 1)


def chunks_of(matrix_ref, held, sems):
    chunks = sems.shape[0]
    size = matrix_ref.shape[0] // chunks
    rows = [pl.ds(q * size, size) for q in range(chunks)]
    return [
        pltpu.make_async_copy(matrix_ref.at[r], held.at[r], sems.at[q]) for q, r in enumerate(rows)
    ]


def call_on_matrix(kernel, shape, kind, matrix, operands, name, scratch):
    chunks = 4
    return pl.pallas_call(
        kernel,
        out_shape=jax.ShapeDtypeStruct(shape, kind),
        in_specs=[HBM] + [VMEM] * len(operands),
        out_specs=VMEM,
        scratch_shapes=[
            pltpu.VMEM(matrix.shape, bf16),
            pltpu.SemaphoreType.DMA((chunks,)),
            *scratch,
        ],
        compiler_params=room(12),
        cost_estimate=hint(3),
        name=name,
    )(pltpu.with_memory_space_constraint(matrix, pltpu.HBM), *operands)


def coarse_product(matrix, arrived, mid_data, scale):
    rows, cols = matrix.shape

    def kernel(matrix_ref, arrived_ref, mid_ref, out_ref, held, sems, turned_ref):
        copies = chunks_of(matrix_ref, held, sems)
        for copy in copies:
            copy.start()
        whole = (scale * arrived_ref[...].astype(f32).sum(axis=0)).astype(bf16).astype(f32)
        whole = mid_ref[...] - 0.5 * whole
        for t in range(cols // TILE):
            lines = whole[:, t * TILE : (t + 1) * TILE]
            full = jnp.concatenate([lines, jnp.zeros((TILE - BLOCK, TILE), f32)], axis=0)
            turned_ref[pl.ds(t * TILE, TILE), :] = full.T.astype(bf16)
        each = rows // TILE // len(copies)
        for c, copy in enumerate(copies):
            copy.wait()
            for q in range(c * each, (c + 1) * each):
                part = jnp.dot(
                    held[pl.ds(q * TILE, TILE), :], turned_ref[...], preferred_element_type=f32
                )
                out_ref[q] = part.T[:BLOCK, :].astype(bf16)

    shape = (rows // TILE, BLOCK, TILE)
    scratch = [pltpu.VMEM((cols, TILE), bf16)]
    operands = (arrived, mid_data)
    return call_on_matrix(kernel, shape, bf16, matrix, operands, "coarse_product", scratch)


def coarse_data_of(arrived, own, other, scale):
    peers = arrived.shape[0]
    n = own.shape[2] - TILE

    def kernel(arrived_ref, own_ref, other_ref, out_ref):
        data = (scale * arrived_ref[...].astype(f32).sum(axis=0)).astype(bf16)
        squares = jnp.zeros((1, TILE), f32)
        for ref in (own_ref, other_ref):
            tails = ref[...].astype(f32).sum(axis=0)
            squares += jnp.sum(tails, axis=0, keepdims=True)
        tail = three_rows(squares)
        for peer in range(peers):
            out_ref[peer, 0] = data
            out_ref[peer, 1] = tail

    tails = (own[:, :, n:], other[:, :, n:])
    shapes = [((peers, 2, BLOCK, TILE), bf16)]
    return call(kernel, shapes, (arrived, *tails), "coarse_data_of", 8, 1)


def halfway_of(gathered_data, factor_down):
    peers = gathered_data.shape[0]

    def kernel(data_ref, factor_ref, out_ref):
        total = jnp.zeros((BLOCK, TILE), f32)
        for q in range(peers // 2):
            pair = jnp.concatenate([data_ref[2 * q, 0], data_ref[2 * q + 1, 0]], axis=1)
            rows = factor_ref[pl.ds(q * 2 * TILE, 2 * TILE), :]
            total += jnp.dot(pair, rows, preferred_element_type=f32)
        low = total.astype(bf16)
        for peer in range(peers):
            out_ref[peer] = low

    shapes = [((peers, BLOCK, TILE), bf16)]
    return call(kernel, shapes, (gathered_data, factor_down), "halfway_of", 8, 1)


def coarse_coef_of(halfway, factor_across):
    peers = halfway.shape[0]

    def kernel(half_ref, factor_ref, out_ref):
        total = jnp.zeros((BLOCK, TILE), f32)
        for q in range(peers):
            total += lax.dot_general(
                half_ref[q], factor_ref[q], (((1,), (1,)), ((), ())), preferred_element_type=f32
            )
        low = total.astype(bf16)
        for peer in range(peers):
            out_ref[peer] = low

    shapes = [((peers, BLOCK, TILE), bf16)]
    return call(kernel, shapes, (halfway, factor_across), "coarse_coef_of", 8, 1)


def prolong(matrix, coarse_coef, place, mid_data, scale):
    rows, cols = matrix.shape
    two = 2 * TILE

    def kernel(matrix_ref, coef_ref, low_ref, mid_ref, out_ref, held, sems):
        copies = chunks_of(matrix_ref, held, sems)
        for copy in copies:
            copy.start()
        for chip in range(HALF):
            for zl in range(LINE):
                out_ref[chip * LINE + zl, :, pl.ds(cols, TILE)] = low_ref[chip]
        total = jnp.zeros((BLOCK, cols), f32)
        each = rows // two // len(copies)
        for c, copy in enumerate(copies):
            copy.wait()
            for q in range(c * each, (c + 1) * each):
                pair = jnp.concatenate([coef_ref[2 * q], coef_ref[2 * q + 1]], axis=1)
                total += jnp.dot(pair, held[pl.ds(q * two, two), :], preferred_element_type=f32)
        low = (0.5 * mid_ref[...] + scale * total).astype(bf16)
        for chip in range(HALF * LINE):
            out_ref[chip, :, pl.ds(0, cols)] = low

    sent = coarse_coef.reshape(HALF, 2, BLOCK, TILE)
    sent = jnp.where(place[3] % 2 == 0, sent[:, 0], sent[:, 1])
    shape = (HALF * LINE, BLOCK, cols + TILE)
    operands = (coarse_coef, sent, mid_data)
    return call_on_matrix(kernel, shape, bf16, matrix, operands, "prolong", ())


def fine_of(arrived, data, core, scale):
    n = arrived.shape[2]

    def kernel(core_ref, arrived_ref, data_ref, out_ref, summed):
        me = core_ref[0]
        summed[...] = arrived_ref[...].astype(f32).sum(axis=0)
        rows = []
        for block in range(SIDE):
            at = ((block % 2) ^ me) * HALF + block // 2
            rows.append(summed[pl.ds(pl.multiple_of(at * BLOCK, BLOCK), BLOCK), :])
        whole = jnp.concatenate(rows, axis=0)
        for t in range(n // TILE):
            at = pl.ds(t * TILE, TILE)
            data = data_ref[at, :].astype(f32)
            out_ref[at, :] = 0.5 * data + scale * whole[:, t * TILE : (t + 1) * TILE].T

    scratch = [pltpu.VMEM((FIELDS, n), f32)]
    return call(kernel, [((n, FIELDS), f32)], (core, arrived, data), "fine_of", 8, 2, scratch, 1)


def in_field_order(x, core):
    n = x.shape[-1]
    x = jnp.where(core == 0, x, x[::-1])
    return x.transpose(3, 1, 0, 2).reshape(n, FIELDS)


def scale_of(tiles, listed):
    return (tiles * TILE / (SIDE * listed * TILE * TILE)) ** 0.5


def per_device(values, points0, points1, points2, tiles_a0, tiles_e1, tiles_a1, factor):
    core = lax.axis_index("k")
    col_id = lax.axis_index(COL)
    row_id = lax.axis_index(ROW)
    rows_fine, fields = values.shape
    rows_mid = points1.shape[1]
    rows_coarse = points2.shape[1]
    coarse = rows_coarse * SIDE
    share = rows_fine // SIDE
    tiles_fine, tiles_mid = rows_fine // TILE, rows_mid // TILE
    list_a0, list_e1, list_a1 = tiles_a0[0, 0], tiles_e1[0, 0], tiles_a1[0, 0]
    scale_a0 = scale_of(tiles_fine, list_a0.shape[1])
    scale_e1 = scale_of(tiles_fine, list_e1.shape[1])
    scale_a1 = scale_of(tiles_mid, list_a1.shape[1])
    scale_e2 = (1.0 / (rows_mid * SIDE)) ** 0.5

    listed_a0, listed_e1, listed_a1 = (a.shape[1] for a in (list_a0, list_e1, list_a1))

    first_e1 = 2 * rows_of(listed_a0)
    first_a1 = first_e1 + 2 * rows_of(listed_e1)

    own_e1 = in_rows(list_e1)
    there = turned(packed(points0, points1, (list_a0, list_e1, list_a1), factor))
    local = [points2, jnp.zeros((SIDE - 2, TILE), bf16), points1.reshape(2 * tiles_mid, TILE)]
    local = jnp.concatenate(local, axis=0)
    x_id, zl_id = lax.axis_index("x"), lax.axis_index("zl")
    place = jnp.stack([core, row_id, col_id, zl_id, x_id, lax.axis_index("zh")]).astype(jnp.int32)
    fine_here = points0.astype(f32).reshape(2, tiles_fine, 1, TILE)
    mid_here = points1.astype(f32).reshape(2, tiles_mid, 1, TILE)
    tail = jnp.pad(own_e1, ((0, BLOCK - own_e1.shape[0]), (0, 0))).astype(bf16)
    there, vector, local, fine_here, mid_here, tail, place = lax.optimization_barrier(
        (there, values.T, local, fine_here, mid_here, tail, place)
    )
    fine_there, mid_there, lists, common = unpacked(
        there, factor, local, tiles_fine, tiles_mid, first_a1 + 2 * rows_of(listed_a1)
    )

    own, other = product_a0(lists, place, fine_here, fine_there, vector, listed_a0)
    pair = pair_sum(own, other).reshape(LINE, 2 * BLOCK, rows_fine)
    summed = sum_of(exchanged(pair, "y"))
    common, summed = lax.optimization_barrier((common, summed))
    swapped = lax.ppermute(summed, "zh", [(0, 1), (1, 0)])
    swapped, common, crossed = lax.optimization_barrier(
        (swapped, common, lax.ppermute(common, "zh", [(0, 1), (1, 0)]))
    )
    common = jnp.concatenate([common, crossed], axis=0)
    common = jnp.broadcast_to(common, (LINE, *common.shape))
    fine_own = exchanged(residual_of(summed, swapped, -0.5 * scale_a0), "y")
    fine_own, common = lax.optimization_barrier((fine_own, common))
    fine_own = fine_own.reshape(HALF, BLOCK, rows_fine + TILE)
    fine_other = from_partner(fine_own)

    common, fine_own, fine_other = lax.optimization_barrier((common, fine_own, fine_other))
    common = exchanged(common, "y")
    restricted = product(
        lists, listed_e1, first_e1, 0, fine_there, mid_here, (fine_own, fine_other), support_mid, tail
    )
    restricted, common = lax.optimization_barrier((restricted, common))
    ordered = in_row_order(place, common, from_partner(common), tiles_mid)
    fine_quarter = fine_here.reshape(2, QUARTER // 2, LINE, 2, 1, TILE)
    fine_quarter = lax.dynamic_index_in_dim(fine_quarter, zl_id, 2, keepdims=False)
    fine_quarter = fine_quarter.reshape(2, QUARTER, 1, TILE)
    fine_quarter = jnp.pad(fine_quarter, ((0, 0), (0, 1), (0, 0), (0, 0)), constant_values=8.0)
    factor_down, factor_across, centres, mid_line = ordered
    coarse_kernel = all_pairs(centres, mid_there, support_coarse)
    restricted, coarse_kernel, factor_down, factor_across, mid_line, fine_quarter = (
        lax.optimization_barrier(
            (
                exchanged(restricted, COL),
                coarse_kernel,
                factor_down,
                factor_across,
                mid_line,
                fine_quarter,
            )
        )
    )
    mid_share, mid_all = mid_of(restricted, scale_e1)
    line_lists = lax.dynamic_slice_in_dim(restricted[:, :, rows_mid:], x_id * LINE, LINE, 0)
    line_lists = line_lists[:, : own_e1.shape[0]].reshape(-1, TILE).astype(jnp.int32)
    line_lists = quarter_of(line_lists, place, LINE, listed_e1, tiles_mid)
    mid_all, mid_data, line_lists = lax.optimization_barrier(
        (exchanged(mid_all, COL), turned_blocks(mid_share), line_lists)
    )

    mid_halves = (mid_all[:HALF], mid_all[HALF:])
    mid_own, mid_other = product(
        lists, listed_a1, first_a1, 1, mid_here, mid_there, mid_halves, support_mid
    )
    arrived = exchanged(pair_sum(mid_own, mid_other), YZ)

    coarse_part = coarse_product(coarse_kernel, arrived, mid_data, scale_a1)
    coarse_data = coarse_data_of(exchanged(coarse_part, COL), fine_own, fine_other, scale_e2)
    coarse_data = exchanged(coarse_data, COL)
    halfway = exchanged(halfway_of(coarse_data, factor_down), COL)
    coarse_all = exchanged(coarse_coef_of(halfway, factor_across), COL)

    new_own = exchanged(prolong(coarse_kernel, coarse_all, place, mid_data, scale_e2), YZL)
    new_other = from_partner(new_own)
    fine_part = product_quarter(
        line_lists, mid_line, fine_quarter, new_own, new_other, support_mid
    )
    fine_part, new_own, new_other = lax.optimization_barrier((fine_part, new_own, new_other))
    own_data = lax.dynamic_slice_in_dim(values, col_id * share, share, 0)
    fine_coef = fine_of(exchanged(fine_part, "x"), own_data, place, scale_e1)

    def from_line(zl, at, size):
        both = jnp.stack([new_own, new_other])[..., at : at + size]
        both = both.reshape(2, HALF, LINE, BLOCK, size)
        both = lax.dynamic_index_in_dim(both, zl, 2, keepdims=False)
        return in_field_order(both.astype(f32), core)

    mid_coef = from_line(zl_id, 0, rows_mid)
    coarse_coef = from_line(core, rows_mid, rows_coarse)
    norm = coarse_data[:, 1].astype(f32).sum() / (rows_fine * SIDE * fields)
    return (fine_coef, mid_coef, coarse_coef, jnp.stack([norm]))


def solution(mesh):
    fine_mesh = Mesh(mesh.devices.reshape(4, 2, 2, 4, 4), ALL)
    return jax.shard_map(
        per_device,
        mesh=fine_mesh,
        in_specs=(
            P(ROW, None),
            P(None, ROW),
            P(None, ROW),
            P(None, ROW),
            P(ROW, COL, None, None),
            P(ROW, COL, None, None),
            P(ROW, COL, None, None),
            P(ROW, COL),
        ),
        out_specs=(P(ALL, None), P(COL, None), P(ROW, None), P()),
        check_vma=False,
    )
```
